128 devices in a mesh: dp: 4 (over x_hi, core), patch: 32 (over y, x_lo, z).
Axes of the slice: x: 4 (x_hi: 2, x_lo: 2; x = x_hi * 2 + x_lo), y: 4, z: 4, core: 2. Of those that a mesh axis runs over, the one named last changes fastest.
Arguments:
- query_tokens: bfloat16 [4, 64, 128, 768], P('dp', 'patch')
- past_tokens: bfloat16 [4, 256, 128, 768], P('dp', 'patch'), may hold values from -6 to 6
- source_dev: int32 [64, 4, 3], replicated, may hold values from 0 to 31, all different within a row; in each aligned block of 8 rows (0 to 7, 8 to 15, ..., all dimensions but the last counted through in order) at most 2 rows name the same one
- source_slot: int32 [64, 4, 3], replicated, may hold values from 0 to 7
- kept: int32 [64, 4, 3], replicated, may hold values 0 or 1
- w_query: bfloat16 [768, 768], replicated
- w_key: bfloat16 [768, 768], replicated
- w_value: bfloat16 [768, 768], replicated, may hold values from -0.21875 to 0.21875
- w_out: bfloat16 [768, 768], replicated, may hold values from -0.875 to 0.875
- grad_out: bfloat16 [4, 64, 128, 768], P('dp', 'patch'), may hold values from -6 to 6
Outputs:
- attn_out: bfloat16 [4, 64, 128, 768], P('dp', 'patch')
- grad_query_tokens: bfloat16 [4, 64, 128, 768], P('dp', 'patch')
- grad_past_tokens: bfloat16 [4, 256, 128, 768], P('dp', 'patch')
- grad_w_query: float32 [768, 768], replicated
- grad_w_key: float32 [768, 768], replicated
- grad_w_value: float32 [768, 768], replicated
- grad_w_out: float32 [768, 768], replicated
The draws below stay inside these ranges and needn't reach their ends.
Inputs may be any that keep to these rules, and one draw needn't show every extreme that they name: `source_dev`: row (p, f) lists the devices holding the frame-f blocks that patch p reads: 3 different devices a row. Over the rows of one device's 2 patches, no device is listed more than 2 times, and some device is listed exactly 2 times.
All inputs are finite; a program needn't handle non-finite values.
Results may differ from the reference program's by a relative error of at most 0.013.
The reference program's roundings to bfloat16 on the way (of `soft_weights`, `mixed`, `upstream`, `grad_score` and `far_grad`) count: a program that leaves them out, or rounds other values in their place, can miss the bound.
Values may be sent and summed in bfloat16 or wider, within the bound.
A program may use at most 256 MiB of HBM per device.

```python
import math
import jax
import jax.numpy as jnp
import numpy as np
from jax import lax

D = 768
H = 12
HD = 64
BLK = 128
FRAMES = 4
NB = 3
P_DEV = 2
BATCH = 4
PATCHES = 64
SLOTS_DEV = 8
SLOTS = 256
CAP = 2
N_PATCH = 32


def weight_pair(key):
    folded = jax.random.fold_in(key, 11)
    first_draw = jax.random.normal(jax.random.fold_in(folded, 1), (D, D), jnp.float32)
    second = jax.random.normal(jax.random.fold_in(folded, 2), (D, D), jnp.float32)
    spread = (2.0 / D) ** 0.5
    return (first_draw * spread, second * spread)


def draw_w_query(key, part):
    return weight_pair(key)[0].astype(jnp.bfloat16)


def draw_w_key(key, part):
    return weight_pair(key)[1].astype(jnp.bfloat16)


def draw_query_tokens(key, part):
    tensor_shape = (BATCH, PATCHES, BLK, D)
    return jax.random.normal(key, tensor_shape, jnp.float32).astype(jnp.bfloat16)


def set_ends(drawn, stream_key, smallest, high):
    place = [jax.random.randint(jax.random.fold_in(stream_key, axis), (), 0, length) for axis, length in enumerate(drawn.shape)]
    main_axis = drawn.shape.index(max(drawn.shape))
    beside = place[:main_axis] + [(place[main_axis] + 1) % drawn.shape[main_axis]] + place[main_axis + 1:]
    return drawn.at[tuple(place)].set(smallest).at[tuple(beside)].set(high)


def shard_levels(rng, extent, split, least, high):
    def one(position, blocks):
        heights = jax.random.uniform(jax.random.fold_in(jax.random.fold_in(rng, 6), position), (blocks,), jnp.float32, least / len(split), high / len(split))
        return jnp.repeat(jnp.exp(heights), extent[position] // blocks).reshape((-1,) + (1,) * (len(extent) - position - 1))

    gain = one(*split[0])
    for cut in split[1:]:
        gain = gain * one(*cut)
    return gain


def routed_block(stream_key, own, number, rows, number_of, top, bound, lean):
    ranking = jax.random.permutation(stream_key, number_of)
    heavy_load, usual = shares(number_of, rows * top, bound, lean, True), shares(number_of, rows * top, bound, lean, False)
    places = jnp.arange(number_of)

    def named(sizes, turn):
        used = int((sizes > 0).sum())
        fixed = max(1, used // 4)
        moved = fixed + (places - fixed + turn * (used - fixed)) % max(1, number_of - fixed)
        return jnp.zeros((number_of,), jnp.int32).at[ranking[jnp.where(places < fixed, places, moved)]].set(jnp.asarray(sizes, jnp.int32))

    sizes = jnp.where(number % 4 == 0, named(heavy_load, number // 4), named(usual, number - number // 4 - 1))
    mixed = jax.random.permutation(jax.random.fold_in(own, 3), number_of)
    donor, receiver = mixed[0:number_of // 2 * 2:2], mixed[1:number_of // 2 * 2:2]
    room = jnp.minimum(sizes[donor] - 1, bound - sizes[receiver]) // 2
    room = jnp.where((donor == ranking[0]) | (receiver == ranking[0]) | (sizes[receiver] == 0), 0, jnp.maximum(room, 0))
    moved = jax.random.randint(jax.random.fold_in(own, 4), (number_of // 2,), 0, 1 << 20) % (room + 1)
    sizes = sizes.at[donor].add(-moved).at[receiver].add(moved)
    labels = jnp.searchsorted(jnp.cumsum(sizes), jnp.arange(rows * top), side="right").astype(jnp.int32)
    listing = labels.reshape(top, rows).T
    listing = listing[jax.random.permutation(jax.random.fold_in(own, 1), rows)]
    turn = jax.random.randint(jax.random.fold_in(own, 2), (rows, 1), 0, top)
    return jnp.take_along_axis(listing, (jnp.arange(top)[None, :] + turn) % top, axis=1)


def shares(count, total, bound, lean, full):
    portions = [(1 << 20) // math.isqrt(standing ** lean) + 1 for standing in range(1, count + 1)]
    largest = bound if full else min(bound, max(-(-total // count), total * portions[0] // sum(portions)))
    least = 1 if total - largest >= count - 1 else 0
    holding, rest = [largest] + [least] * (count - 1), total - largest - least * (count - 1)
    while rest > 0:
        free = [i for i in range(1, count) if holding[i] < largest] or [i for i in range(1, count) if holding[i] < bound]
        pool, left = sum([portions[i] for i in free]), rest
        for i in free:
            addition = min(bound - holding[i], max(1, left * portions[i] // pool), rest)
            holding[i] = holding[i] + addition
            rest = rest - addition
    return np.array(holding)


def noise(rng, dims, scale, most, cuts=(), held_as=jnp.bfloat16):
    drawn = jax.random.normal(rng, dims, jnp.float32) * scale
    if len(cuts) > 0:
        drawn = shard_levels(rng, dims, cuts, -0.22, 0.18) * drawn
    return jnp.clip(drawn, min=-most, max=most).astype(held_as)


def setup_inputs(seed: int = 0) -> dict:
    streams_of = jax.random.split(jax.random.key(seed), 11)
    query_tokens = draw_query_tokens(jax.random.fold_in(streams_of[10], 71), 0)
    past_tokens = noise(streams_of[1], (BATCH, SLOTS, BLK, D), 1.0, 6.0, ((0, 4), (1, 32)))
    source_dev_keys = jax.random.split(jax.random.fold_in(streams_of[2], 1), PATCHES * FRAMES // (P_DEV * FRAMES))
    source_dev_turns = jax.random.permutation(jax.random.fold_in(streams_of[2], 3), PATCHES * FRAMES // (P_DEV * FRAMES))
    source_dev = jax.vmap(lambda own, number: routed_block(jax.random.fold_in(streams_of[2], 2), own, number, P_DEV * FRAMES, N_PATCH, NB, CAP, 2))(source_dev_keys, source_dev_turns).reshape((PATCHES, FRAMES, NB))
    source_slot = set_ends(jax.random.randint(streams_of[3], (PATCHES, FRAMES, NB), 0, SLOTS_DEV), jax.random.fold_in(streams_of[3], 1), 0, SLOTS_DEV - 1).astype(jnp.int32)
    kept = set_ends((jax.random.randint(streams_of[4], (PATCHES, FRAMES, NB), 0, 16) < 15).astype(jnp.int32), jax.random.fold_in(streams_of[4], 1), 0, 1)
    w_query = draw_w_query(jax.random.fold_in(streams_of[10], 71), 0)
    w_key = draw_w_key(jax.random.fold_in(streams_of[10], 71), 0)
    w_value = noise(streams_of[7], (D, D), D ** -0.5, 0.21875)
    w_out = noise(streams_of[8], (D, D), (D // 16) ** -0.5, 0.875)
    grad_out = noise(streams_of[9], (BATCH, PATCHES, BLK, D), 1.0, 6.0, ((0, 4), (1, 32)))
    return dict(query_tokens=query_tokens, past_tokens=past_tokens, source_dev=source_dev, source_slot=source_slot, kept=kept, w_query=w_query, w_key=w_key, w_value=w_value, w_out=w_out, grad_out=grad_out)


def attend(queries, keys, values, live):
    groups, query_rows, model_width = queries.shape
    key_rows = keys.shape[1]
    inv_scale = 1.0 / math.sqrt(HD)
    head_query = queries.astype(jnp.float32).reshape(groups, query_rows, H, HD)
    head_key = keys.astype(jnp.float32).reshape(groups, key_rows, H, HD)
    head_value = values.astype(jnp.float32).reshape(groups, key_rows, H, HD)
    scores = jnp.einsum('gqhe,gkhe->ghqk', head_query, head_key) * inv_scale
    scores = jnp.where(live[:, None, None, :] > 0, scores, -jnp.inf)
    row_max = lax.optimization_barrier(jnp.max(scores, axis=-1, keepdims=True))
    shifted = jnp.exp(scores - row_max)
    soft_probs = shifted / lax.optimization_barrier(jnp.sum(shifted, axis=-1, keepdims=True))
    soft_weights = soft_probs.astype(jnp.bfloat16)
    mixed = jnp.einsum('ghqk,gkhe->gqhe', soft_weights.astype(jnp.float32), head_value)
    mixed = mixed.reshape(groups, query_rows, model_width).astype(jnp.bfloat16)
    return (mixed, soft_probs, soft_weights)

def attend_back(queries, keys, values, soft_probs, soft_weights, upstream):
    groups, query_rows, model_width = queries.shape
    key_rows = keys.shape[1]
    inv_scale = 1.0 / math.sqrt(HD)
    head_query = queries.astype(jnp.float32).reshape(groups, query_rows, H, HD)
    head_key = keys.astype(jnp.float32).reshape(groups, key_rows, H, HD)
    head_value = values.astype(jnp.float32).reshape(groups, key_rows, H, HD)
    head_up = upstream.astype(jnp.float32).reshape(groups, query_rows, H, HD)
    grad_prob = jnp.einsum('gqhe,gkhe->ghqk', head_up, head_value)
    row_delta = lax.optimization_barrier(jnp.sum(soft_probs * grad_prob, axis=-1, keepdims=True))
    grad_score = (soft_probs * (grad_prob - row_delta) * inv_scale).astype(jnp.bfloat16)
    score_f = grad_score.astype(jnp.float32)
    grad_q = jnp.einsum('ghqk,gkhe->gqhe', score_f, head_key).reshape(groups, query_rows, model_width).astype(jnp.bfloat16)
    grad_k = jnp.einsum('ghqk,gqhe->gkhe', score_f, head_query).reshape(groups, key_rows, model_width).astype(jnp.bfloat16)
    grad_v = jnp.einsum('ghqk,gqhe->gkhe', soft_weights.astype(jnp.float32), head_up).reshape(groups, key_rows, model_width).astype(jnp.bfloat16)
    return (grad_q, grad_k, grad_v)

def reference(query_tokens, past_tokens, source_dev, source_slot, kept, w_query, w_key, w_value, w_out, grad_out):
    inv_total = 1.0 / math.sqrt(BATCH * PATCHES * BLK)
    requests = FRAMES * NB
    w_proj = jnp.concatenate([w_query, w_key, w_value], axis=1)
    w_pair = jnp.concatenate([w_key, w_value], axis=1)
    block_index = (source_dev * SLOTS_DEV + source_slot).reshape(PATCHES, requests).astype(jnp.int32)
    live_rows = jnp.concatenate([jnp.ones((PATCHES, BLK), jnp.int32), jnp.repeat(kept.reshape(PATCHES, requests), BLK, axis=1)], axis=1)
    zero_grad = jnp.zeros((D, D), jnp.float32)
    totals = (zero_grad, zero_grad, zero_grad, zero_grad)
    out_list = []
    tok_list = []
    past_list = []
    for sample in range(BATCH):
        past_block = past_tokens[sample]

        def one_patch(running, inputs):
            tokens, grad_tok, index_row, live_row = inputs
            fetched = jnp.take(past_block, index_row, axis=0).reshape(requests * BLK, D)
            own_proj = jnp.dot(tokens, w_proj, preferred_element_type=jnp.float32).astype(jnp.bfloat16)
            far_proj = jnp.dot(fetched, w_pair, preferred_element_type=jnp.float32).astype(jnp.bfloat16)
            queries = own_proj[:, :D]
            all_keys = jnp.concatenate([own_proj[:, D:2 * D], far_proj[:, :D]], axis=0)
            all_values = jnp.concatenate([own_proj[:, 2 * D:], far_proj[:, D:]], axis=0)
            mixed, soft_probs, soft_weights = attend(queries[None], all_keys[None], all_values[None], live_row[None])
            mixed = mixed[0]
            result = jnp.dot(mixed, w_out, preferred_element_type=jnp.float32).astype(jnp.bfloat16)
            upstream = jnp.dot(grad_tok, w_out.T, preferred_element_type=jnp.float32).astype(jnp.bfloat16)
            grad_q, grad_k, grad_v = attend_back(queries[None], all_keys[None], all_values[None], soft_probs, soft_weights, upstream[None])
            grad_q, grad_k, grad_v = (grad_q[0], grad_k[0], grad_v[0])
            grad_tokens = (jnp.dot(grad_q, w_query.T, preferred_element_type=jnp.float32) + jnp.dot(grad_k[:BLK], w_key.T, preferred_element_type=jnp.float32) + jnp.dot(grad_v[:BLK], w_value.T, preferred_element_type=jnp.float32)).astype(jnp.bfloat16)
            far_grad = (jnp.dot(grad_k[BLK:], w_key.T, preferred_element_type=jnp.float32) + jnp.dot(grad_v[BLK:], w_value.T, preferred_element_type=jnp.float32)).astype(jnp.bfloat16)
            grad_wq, grad_wk, grad_wv, grad_wo = running
            grad_wq = grad_wq + jnp.dot(tokens.T, grad_q, preferred_element_type=jnp.float32)
            grad_wk = grad_wk + jnp.dot(tokens.T, grad_k[:BLK], preferred_element_type=jnp.float32) + jnp.dot(fetched.T, grad_k[BLK:], preferred_element_type=jnp.float32)
            grad_wv = grad_wv + jnp.dot(tokens.T, grad_v[:BLK], preferred_element_type=jnp.float32) + jnp.dot(fetched.T, grad_v[BLK:], preferred_element_type=jnp.float32)
            grad_wo = grad_wo + jnp.dot(mixed.T, grad_tok, preferred_element_type=jnp.float32)
            return ((grad_wq, grad_wk, grad_wv, grad_wo), (result, grad_tokens, far_grad.reshape(requests, BLK, D)))
        totals, stacked = lax.scan(one_patch, totals, (query_tokens[sample], grad_out[sample], block_index, live_rows))
        out_list.append(stacked[0])
        tok_list.append(stacked[1])
        past_grad = jax.ops.segment_sum(stacked[2].reshape(PATCHES * requests, BLK, D).astype(jnp.float32), block_index.reshape(PATCHES * requests), num_segments=SLOTS)
        past_list.append(past_grad.astype(jnp.bfloat16))
    return (jnp.stack(out_list), jnp.stack(tok_list), jnp.stack(past_list), totals[0] * inv_total, totals[1] * inv_total, totals[2] * inv_total, totals[3] * inv_total)
```

```python
import math

import jax
import jax.numpy as jnp
from jax import lax
from jax.experimental import pallas as pl
from jax.experimental.pallas import tpu as pltpu
from jax.sharding import PartitionSpec as P

H = 12
HD = 64
F32 = jnp.float32
BF16 = jnp.bfloat16
NN = (((1,), (0,)), ((), ()))
NT = (((1,), (1,)), ((), ()))
TN = (((0,), (0,)), ((), ()))


def mm(a, b, dims=NN):
    return lax.dot_general(a, b, dims, preferred_element_type=F32)


def gather_blocks(source, index):
    count = index.shape[0]

    def kernel(index_ref, source_ref, out_ref, sems):
        def copy(i):
            return pltpu.make_async_copy(
                source_ref.at[index_ref[i]], out_ref.at[i], sems.at[i]
            )

        @pl.loop(0, count)
        def _(i):
            copy(i).start()

        @pl.loop(0, count)
        def _(i):
            copy(i).wait()

    return pl.pallas_call(
        kernel,
        out_shape=jax.ShapeDtypeStruct((count,) + source.shape[1:], source.dtype),
        grid_spec=pltpu.PrefetchScalarGridSpec(
            num_scalar_prefetch=1,
            grid=(),
            in_specs=[pl.BlockSpec(memory_space=pl.ANY)],
            out_specs=pl.BlockSpec(memory_space=pl.ANY),
            scratch_shapes=[pltpu.SemaphoreType.DMA((count,))],
        ),
        name="gather_blocks",
    )(index, source)


def scatter_sum(source, target, used, outputs):
    count, rows, width = source.shape
    step = 8

    def kernel(target_ref, used_ref, source_ref, out_ref, acc):
        t = pl.program_id(0)

        @pl.when(t == 0)
        def _():
            acc[...] = jnp.zeros_like(acc)

        for j in range(step):
            @pl.when(used_ref[t * step + j] > 0)
            def _():
                m = target_ref[t * step + j]
                acc[m] = acc[m] + source_ref[j].astype(F32)

        @pl.when(t == pl.num_programs(0) - 1)
        def _():
            out_ref[...] = acc[...].astype(out_ref.dtype)

    return pl.pallas_call(
        kernel,
        out_shape=jax.ShapeDtypeStruct((outputs, rows, width), source.dtype),
        grid_spec=pltpu.PrefetchScalarGridSpec(
            num_scalar_prefetch=2,
            grid=(count // step,),
            in_specs=[pl.BlockSpec((step, rows, width), lambda t, *_: (t, 0, 0))],
            out_specs=pl.BlockSpec((outputs, rows, width), lambda t, *_: (0, 0, 0)),
            scratch_shapes=[pltpu.VMEM((outputs, rows, width), F32)],
        ),
        compiler_params=pltpu.CompilerParams(vmem_limit_bytes=48 << 20),
        name="scatter_sum",
    )(target, used, source)


def layer(position, live, arrived, tokens, grad_out, w_query, w_pair, w_out, slots):
    patches, block, width = tokens.shape
    requests = position.shape[0] // patches
    far = requests * block
    rows = block + far
    chunks = 4
    chunk = far // chunks
    pairs = width // 128
    parts = requests + 1

    def kernel(
        position_ref, live_ref, arrived_ref, tokens_ref, grad_ref, wq_ref, wkv_ref, wo_ref,
        attn_ref, tokgrad_ref, fargrad_ref, x_ref, dkv_ref, dq_ref, mixed_ref,
        key_s, val_s, q_s, up_s, s_s, dp_s, pb_s, ds_s, fg_s, in_sem, out_sem,
    ):
        p = pl.program_id(0)

        def fetch(r):
            return pltpu.make_async_copy(
                arrived_ref.at[position_ref[p * requests + r]],
                x_ref.at[0, pl.ds(block + r * block, block)],
                in_sem.at[r],
            )

        for r in range(requests):
            fetch(r).start()
        tok = tokens_ref[0]
        x_ref[0, 0:block] = tok
        q_s[...] = mm(tok, wq_ref[...]).astype(BF16)
        own = mm(tok, wkv_ref[...]).astype(BF16)
        key_s[0:block] = own[:, :width]
        val_s[0:block] = own[:, width:]
        up_s[...] = mm(grad_ref[0], wo_ref[...], NT).astype(BF16)
        for r in range(requests):
            fetch(r).wait()

        @pl.loop(0, chunks)
        def _(c):
            at = pl.multiple_of(block + c * chunk, 128)
            x = x_ref[0, pl.ds(at, chunk)]
            key_s[pl.ds(at, chunk)] = mm(x, wkv_ref[:, :width]).astype(BF16)
            val_s[pl.ds(at, chunk)] = mm(x, wkv_ref[:, width:]).astype(BF16)

        low = lax.broadcasted_iota(jnp.int32, (block, 128), 1) < HD
        zero = jnp.zeros((block, 128), BF16)

        @pl.loop(0, pairs)
        def _(j):
            lanes = pl.ds(pl.multiple_of(j * 128, 128), 128)
            k = key_s[:, lanes]
            v = val_s[:, lanes]
            q = q_s[:, lanes] * jnp.asarray(1.0 / math.sqrt(HD), BF16)
            u = up_s[:, lanes]
            q2 = jnp.concatenate([jnp.where(low, q, zero), jnp.where(low, zero, q)], axis=0)
            u2 = jnp.concatenate([jnp.where(low, u, zero), jnp.where(low, zero, u)], axis=0)
            s_s[...] = mm(k, q2, NT)
            dp_s[...] = mm(v, u2, NT)

            def bias(r):
                dead = live_ref[p * requests + jnp.maximum(r - 1, 0)] == 0
                return jnp.where((r > 0) & dead, -jnp.inf, 0.0).astype(F32)

            def part(r):
                return pl.ds(pl.multiple_of(r * block, block), block)

            def largest(r, m):
                s = s_s[part(r)] + bias(r)
                return jnp.maximum(m, jnp.max(s.reshape(block // 8, 8, 2 * block), axis=0))

            m = lax.fori_loop(0, parts, largest, jnp.full((8, 2 * block), -jnp.inf, F32))
            m = jnp.max(m, axis=0, keepdims=True)

            def exps(r, carry):
                total, delta = carry
                e = jnp.exp(s_s[part(r)] + bias(r) - m)
                s_s[part(r)] = e
                g = e * dp_s[part(r)]
                fold = lambda t: jnp.sum(t.reshape(block // 8, 8, 2 * block), axis=0)
                return total + fold(e), delta + fold(g)

            nil = jnp.zeros((8, 2 * block), F32)
            total, delta = lax.fori_loop(0, parts, exps, (nil, nil))
            inverse = 1.0 / jnp.sum(total, axis=0, keepdims=True)
            delta = jnp.sum(delta, axis=0, keepdims=True) * inverse

            @pl.loop(0, parts)
            def _(r):
                prob = s_s[part(r)] * inverse
                pb_s[part(r)] = prob.astype(BF16)
                ds_s[part(r)] = (prob * (dp_s[part(r)] - delta)).astype(BF16)

            pb = pb_s[...]
            ds = ds_s[...]
            dkv_ref[0, :, lanes] = mm(ds, q2).astype(BF16)
            dkv_ref[0, :, pl.ds(pl.multiple_of(width + j * 128, 128), 128)] = mm(pb, u2).astype(BF16)
            o = mm(pb, v, TN)
            mixed_ref[0, :, lanes] = jnp.where(low, o[:block], o[block:]).astype(BF16)
            dq = mm(ds, k, TN)
            dq = jnp.where(low, dq[:block], dq[block:]) * (1.0 / math.sqrt(HD))
            dq_ref[0, :, lanes] = dq.astype(BF16)

        attn_ref[0] = mm(mixed_ref[0], wo_ref[...]).astype(BF16)
        tokgrad_ref[0] = (
            mm(dq_ref[0], wq_ref[...], NT) + mm(dkv_ref[0, 0:block], wkv_ref[...], NT)
        ).astype(BF16)

        @pl.loop(0, chunks)
        def _(c):
            at = pl.multiple_of(block + c * chunk, 128)
            g = mm(dkv_ref[0, pl.ds(at, chunk)], wkv_ref[...], NT).astype(BF16)
            fg_s[pl.ds(pl.multiple_of(c * chunk, 128), chunk)] = g

        def put(r):
            return pltpu.make_async_copy(
                fg_s.at[pl.ds(r * block, block)],
                fargrad_ref.at[position_ref[p * requests + r]],
                out_sem.at[r],
            )

        for r in range(requests):
            put(r).start()
        for r in range(requests):
            put(r).wait()

    per_patch = lambda n, w: pl.BlockSpec((1, n, w), lambda p, *_: (p, 0, 0))
    whole = lambda a: pl.BlockSpec(a.shape, lambda p, *_: (0, 0), pipeline_mode=pl.Buffered(1))
    hbm = pl.BlockSpec(memory_space=pl.ANY)
    shape = lambda *s: jax.ShapeDtypeStruct(s, BF16)
    return pl.pallas_call(
        kernel,
        out_shape=(
            shape(patches, block, width),
            shape(patches, block, width),
            shape(slots, block, width),
            shape(patches, rows, width),
            shape(patches, rows, 2 * width),
            shape(patches, block, width),
            shape(patches, block, width),
        ),
        grid_spec=pltpu.PrefetchScalarGridSpec(
            num_scalar_prefetch=2,
            grid=(patches,),
            in_specs=[
                hbm, per_patch(block, width), per_patch(block, width),
                whole(w_query), whole(w_pair), whole(w_out),
            ],
            out_specs=(
                per_patch(block, width), per_patch(block, width), hbm, per_patch(rows, width),
                per_patch(rows, 2 * width), per_patch(block, width), per_patch(block, width),
            ),
            scratch_shapes=[
                pltpu.VMEM((rows, width), BF16),
                pltpu.VMEM((rows, width), BF16),
                pltpu.VMEM((block, width), BF16),
                pltpu.VMEM((block, width), BF16),
                pltpu.VMEM((rows, 2 * block), F32),
                pltpu.VMEM((rows, 2 * block), F32),
                pltpu.VMEM((rows, 2 * block), BF16),
                pltpu.VMEM((rows, 2 * block), BF16),
                pltpu.VMEM((far, width), BF16),
                pltpu.SemaphoreType.DMA((requests,)),
                pltpu.SemaphoreType.DMA((requests,)),
            ],
        ),
        compiler_params=pltpu.CompilerParams(vmem_limit_bytes=60 << 20),
        name="layer",
    )(position, live, arrived, tokens, grad_out, w_query, w_pair, w_out)


def outer_sum(left, right):
    return lax.dot_general(left, right, TN, preferred_element_type=F32)


def body(
    query_tokens, past_tokens, source_dev, source_slot, kept, w_query, w_key, w_value, w_out,
    grad_out,
):
    _, patches, block, width = query_tokens.shape
    tokens, grads, past = query_tokens[0], grad_out[0], past_tokens[0]
    peers = lax.axis_size("patch")
    device = lax.axis_index("patch")
    per_device = patches * source_dev.shape[1] * source_dev.shape[2]
    cap = 2
    owners = source_dev.reshape(peers, per_device)
    places = source_slot.reshape(peers, per_device)
    order = jnp.arange(per_device)
    matches = (owners[:, :, None] == owners[:, None, :]) & (order[:, None] > order[None, :])
    rank = jnp.sum(matches.astype(jnp.int32), axis=2)
    hit = (rank[:, :, None] == jnp.arange(cap)) & (owners == device)[:, :, None]
    out_place = jnp.sum(jnp.where(hit, places[:, :, None], 0), axis=1).reshape(-1)
    out_used = jnp.sum(hit.astype(jnp.int32), axis=1).reshape(-1)
    mine = owners[device] * cap + rank[device]
    live = kept.reshape(peers, per_device)[device]

    outgoing = gather_blocks(past, out_place)
    arrived = lax.all_to_all(outgoing, "patch", split_axis=0, concat_axis=0, tiled=True)
    w_pair = jnp.concatenate([w_key, w_value], axis=1)
    attn, token_grad, far_grad, x, dkv, dq, mixed = layer(
        mine, live, arrived, tokens, grads, w_query, w_pair, w_out, peers * cap
    )
    returned = lax.all_to_all(far_grad, "patch", split_axis=0, concat_axis=0, tiled=True)
    past_grad = scatter_sum(returned, out_place, out_used, past.shape[0])
    flat = lambda a: a.reshape(-1, a.shape[-1])
    grad_pair = outer_sum(flat(x), flat(dkv))
    grad_wq = outer_sum(flat(tokens), flat(dq))
    grad_wo = outer_sum(flat(mixed), flat(grads))
    grad_pair, grad_wq, grad_wo = lax.psum((grad_pair, grad_wq, grad_wo), ("dp", "patch"))
    scale = 1.0 / math.sqrt(lax.axis_size("dp") * peers * patches * block)
    return (
        attn[None],
        token_grad[None],
        past_grad[None],
        grad_wq * scale,
        grad_pair[:, :width] * scale,
        grad_pair[:, width:] * scale,
        grad_wo * scale,
    )


def solution(mesh):
    split = P("dp", "patch", None, None)
    return jax.shard_map(
        body,
        mesh=mesh,
        in_specs=(split, split, P(), P(), P(), P(), P(), P(), P(), split),
        out_specs=(split, split, split, P(), P(), P(), P()),
        check_vma=False,
    )
```

```python
import math

import jax
import jax.numpy as jnp
from jax import lax
from jax.experimental import pallas as pl
from jax.experimental.pallas import tpu as pltpu
from jax.sharding import PartitionSpec as P

H = 12
HD = 64
F32 = jnp.float32
MESH = pl.DeviceIdType.MESH
BF16 = jnp.bfloat16
NN = (((1,), (0,)), ((), ()))
NT = (((1,), (1,)), ((), ()))
TN = (((0,), (0,)), ((), ()))


def mm(a, b, dims=NN):
    return lax.dot_general(a, b, dims, preferred_element_type=F32)


def place():
    device = lax.axis_index("patch")
    return device // 8, (device // 4) % 2, device % 4, lax.axis_index("dp")


def step_id(y, x, z, dim, hop):
    return ((y + hop * (1 - dim)) % 4) * 8 + x * 4 + (z + hop * dim) % 4


def meet(y, x, z, dp, across):
    barrier = pltpu.get_barrier_semaphore()
    ids = [step_id(y, x, z, dim, hop) for dim in (0, 1) for hop in (1, 2, 3)]
    if across:
        ids.append(y * 8 + (1 - x) * 4 + z)
    for other in ids:
        pl.semaphore_signal(barrier, 1, device_id=(dp, other), device_id_type=MESH)
    pl.semaphore_wait(barrier, len(ids))


def spread(past, table):
    blocks, rows, width = past.shape
    chunk = blocks // 2
    cap = 8

    def kernel(
        table_ref, past_ref, out_ref, have_a, have_b, sel_a, sel_b,
        in_sem, x_send, x_recv, g_send, g_recv, e_send, e_recv, own_sem,
    ):
        y, x, z, dp = place()
        pos = lambda dim, hop=0: (y * (1 - dim) + z * dim + hop) % 4
        have, sel = (have_a, have_b), (sel_a, sel_b)
        half = (x, 1 - x)

        def region(t, hop, c):
            return have[t].at[pl.ds(pos(half[t], hop) * blocks + c * chunk, chunk)]

        local = pltpu.make_async_copy(
            past_ref, have_a.at[pl.ds(pos(half[0]) * blocks, blocks)], in_sem
        )
        local.start()
        meet(y, x, z, dp, True)

        def cross(c):
            at = pl.ds(pos(half[0]) * blocks + c * chunk, chunk)
            return pltpu.make_async_remote_copy(
                past_ref.at[pl.ds(c * chunk, chunk)], have_b.at[at], x_send.at[c], x_recv.at[c],
                device_id=(dp, y * 8 + (1 - x) * 4 + z), device_id_type=MESH,
            )

        def crossed(c):
            at = pl.ds(pos(half[1]) * blocks + c * chunk, chunk)
            return pltpu.make_async_remote_copy(
                past_ref.at[pl.ds(c * chunk, chunk)], have_b.at[at], x_send.at[c], x_recv.at[c],
                device_id=(dp, y * 8 + (1 - x) * 4 + z), device_id_type=MESH,
            )

        ways = ((1, 0, 0), (3, 0, 1), (1, 0, 1), (3, 0, 0), (1, 3, 0), (3, 1, 1))

        def go(t, n):
            way, owner, c = ways[n]
            return pltpu.make_async_remote_copy(
                region(t, owner, c), region(t, owner, c), g_send.at[t, n], g_recv.at[t, n],
                device_id=(dp, step_id(y, x, z, half[t], way)), device_id_type=MESH,
            )

        def came(t, n):
            way, owner, c = ways[n]
            owner = (owner - way) % 4
            return pltpu.make_async_remote_copy(
                region(t, owner, c), region(t, owner, c), g_send.at[t, n], g_recv.at[t, n],
                device_id=(dp, step_id(y, x, z, half[t], way)), device_id_type=MESH,
            )

        def swap(t, hop, arriving=False):
            h = half[t]
            at = h * 4 + pos(1 - h, -hop if arriving else 0)
            return pltpu.make_async_remote_copy(
                sel[t].at[hop], out_ref.at[pl.ds(at * cap, cap)],
                e_send.at[t, hop - 1], e_recv.at[t, hop - 1],
                device_id=(dp, step_id(y, x, z, 1 - h, hop)), device_id_type=MESH,
            )

        def keep(t):
            h = half[t]
            at = h * 4 + pos(1 - h)
            return pltpu.make_async_copy(
                sel[t].at[0], out_ref.at[pl.ds(at * cap, cap)], own_sem.at[t]
            )

        def choose(t):
            h = half[t]
            for hop in (2, 1, 3, 0):
                row = h * 4 + pos(1 - h, hop)

                @pl.loop(0, cap)
                def _(s):
                    sel[t][hop, s] = have[t][table_ref[row * cap + s]]

                if hop:
                    swap(t, hop).start()
                else:
                    keep(t).start()

        cross(0).start()
        cross(1).start()
        local.wait()
        for n in range(4):
            go(0, n).start()
        crossed(0).wait_recv()
        go(1, 0).start()
        go(1, 3).start()
        came(0, 0).wait_recv()
        go(0, 4).start()
        came(0, 1).wait_recv()
        go(0, 5).start()
        crossed(1).wait_recv()
        go(1, 1).start()
        go(1, 2).start()
        for n in (2, 3, 4, 5):
            came(0, n).wait_recv()
        choose(0)
        came(1, 0).wait_recv()
        go(1, 4).start()
        came(1, 1).wait_recv()
        go(1, 5).start()
        for n in (2, 3, 4, 5):
            came(1, n).wait_recv()
        choose(1)
        for t in (0, 1):
            for hop in (1, 2, 3):
                swap(t, hop, True).wait_recv()
            keep(t).wait()
        for t in (0, 1):
            cross(t).wait_send()
            for n in range(6):
                go(t, n).wait_send()
            for hop in (1, 2, 3):
                swap(t, hop).wait_send()

    return pl.pallas_call(
        kernel,
        out_shape=jax.ShapeDtypeStruct((8 * cap, rows, width), past.dtype),
        in_specs=[pl.BlockSpec(memory_space=pltpu.SMEM), pl.BlockSpec(memory_space=pl.ANY)],
        out_specs=pl.BlockSpec(memory_space=pl.ANY),
        scratch_shapes=[
            pltpu.VMEM((4 * blocks, rows, width), past.dtype),
            pltpu.VMEM((4 * blocks, rows, width), past.dtype),
            pltpu.VMEM((4, cap, rows, width), past.dtype),
            pltpu.VMEM((4, cap, rows, width), past.dtype),
            pltpu.SemaphoreType.DMA,
            pltpu.SemaphoreType.DMA((2,)),
            pltpu.SemaphoreType.DMA((2,)),
            pltpu.SemaphoreType.DMA((2, 6)),
            pltpu.SemaphoreType.DMA((2, 6)),
            pltpu.SemaphoreType.DMA((2, 3)),
            pltpu.SemaphoreType.DMA((2, 3)),
            pltpu.SemaphoreType.DMA((2,)),
        ],
        compiler_params=pltpu.CompilerParams(
            collective_id=0, has_side_effects=True, vmem_limit_bytes=48 << 20
        ),
        name="spread",
    )(table, past)


def send_back(grads):
    slots, rows, width = grads.shape
    cap = slots // 8

    def kernel(grad_ref, out_ref, own, send, recv, own_sem):
        y, x, z, dp = place()
        pos = lambda dim, hop=0: (y * (1 - dim) + z * dim + hop) % 4
        part = lambda ref, at: ref.at[pl.ds(at * cap, cap)]

        def swap(h, hop, arriving=False):
            return pltpu.make_async_remote_copy(
                part(grad_ref, h * 4 + pos(1 - h, hop)),
                part(out_ref, h * 4 + pos(1 - h, -hop if arriving else 0)),
                send.at[h, hop - 1], recv.at[h, hop - 1],
                device_id=(dp, step_id(y, x, z, 1 - h, hop)), device_id_type=MESH,
            )

        def load(h):
            return pltpu.make_async_copy(
                part(grad_ref, h * 4 + pos(1 - h)), own.at[h], own_sem.at[h]
            )

        def store(h):
            return pltpu.make_async_copy(
                own.at[h], part(out_ref, h * 4 + pos(1 - h)), own_sem.at[h]
            )

        for h in (0, 1):
            load(h).start()
        meet(y, x, z, dp, False)
        for hop in (2, 1, 3):
            for h in (0, 1):
                swap(h, hop).start()
        for h in (0, 1):
            load(h).wait()
            store(h).start()
        for h in (0, 1):
            store(h).wait()
            for hop in (1, 2, 3):
                swap(h, hop, True).wait_recv()
        for h in (0, 1):
            for hop in (1, 2, 3):
                swap(h, hop).wait_send()

    return pl.pallas_call(
        kernel,
        out_shape=jax.ShapeDtypeStruct(grads.shape, grads.dtype),
        in_specs=[pl.BlockSpec(memory_space=pl.ANY)],
        out_specs=pl.BlockSpec(memory_space=pl.ANY),
        scratch_shapes=[
            pltpu.VMEM((2, cap, rows, width), grads.dtype),
            pltpu.SemaphoreType.DMA((2, 3)),
            pltpu.SemaphoreType.DMA((2, 3)),
            pltpu.SemaphoreType.DMA((2,)),
        ],
        compiler_params=pltpu.CompilerParams(
            collective_id=1, has_side_effects=True, vmem_limit_bytes=32 << 20
        ),
        name="send_back",
    )(grads)


def collect(partial):
    groups, blocks, rows, width = partial.shape
    chunk = blocks // 2

    def kernel(
        part_ref, out_ref, relay, staged, inward, mine, across,
        r_send, r_recv, d_send, d_recv, x_send, x_recv,
    ):
        y, x, z, dp = place()
        pos = lambda dim, hop=0: (y * (1 - dim) + z * dim + hop) % 4
        half = (1 - x, x)
        meet(y, x, z, dp, True)
        ways = (3, 1)

        def row(t, hop):
            return half[t] * 4 + pos(half[t], hop)

        def pass_on(t, side):
            return pltpu.make_async_remote_copy(
                part_ref.at[row(t, 2), pl.ds(side * chunk, chunk)], relay.at[t, side],
                r_send.at[t, side], r_recv.at[t, side],
                device_id=(dp, step_id(y, x, z, half[t], ways[side])), device_id_type=MESH,
            )

        def direct(t, side, summed):
            c = side if summed else 1 - side
            source = (
                staged.at[t, side] if summed
                else part_ref.at[row(t, ways[side]), pl.ds(c * chunk, chunk)]
            )
            return pltpu.make_async_remote_copy(
                source, inward.at[t, side, pl.ds(c * chunk, chunk)],
                d_send.at[t, side, int(summed)], d_recv.at[t, side, int(summed)],
                device_id=(dp, step_id(y, x, z, half[t], ways[side])), device_id_type=MESH,
            )

        def cross(c):
            return pltpu.make_async_remote_copy(
                mine.at[pl.ds(c * chunk, chunk)], across.at[pl.ds(c * chunk, chunk)],
                x_send.at[c], x_recv.at[c],
                device_id=(dp, y * 8 + (1 - x) * 4 + z), device_id_type=MESH,
            )

        def final(t, b):
            return (
                part_ref[row(t, 0), b].astype(F32)
                + inward[t, 0, b].astype(F32)
                + inward[t, 1, b].astype(F32)
            )

        for t in (0, 1):
            for side in (0, 1):
                pass_on(t, side).start()
        for t in (0, 1):
            for side in (0, 1):
                direct(t, side, False).start()
        for t in (0, 1):
            for side in (0, 1):
                pass_on(t, side).wait_recv()

                @pl.loop(0, chunk)
                def _(b):
                    own = part_ref[row(t, ways[side]), side * chunk + b]
                    staged[t, side, b] = (
                        own.astype(F32) + relay[t, side, b].astype(F32)
                    ).astype(staged.dtype)

                direct(t, side, True).start()
        for side in (0, 1):
            for summed in (False, True):
                direct(0, side, summed).wait_recv()
        for c in (0, 1):
            @pl.loop(0, chunk)
            def _(b):
                mine[c * chunk + b] = final(0, c * chunk + b).astype(mine.dtype)

            cross(c).start()
        for side in (0, 1):
            for summed in (False, True):
                direct(1, side, summed).wait_recv()
        for c in (0, 1):
            cross(c).wait_recv()

            @pl.loop(0, chunk)
            def _(b):
                at = c * chunk + b
                out_ref[at] = (final(1, at) + across[at].astype(F32)).astype(out_ref.dtype)

        for t in (0, 1):
            cross(t).wait_send()
            for side in (0, 1):
                pass_on(t, side).wait_send()
                for summed in (False, True):
                    direct(t, side, summed).wait_send()

    shape = lambda *s: pltpu.VMEM(s + (rows, width), partial.dtype)
    return pl.pallas_call(
        kernel,
        out_shape=jax.ShapeDtypeStruct((blocks, rows, width), partial.dtype),
        in_specs=[pl.BlockSpec(memory_space=pltpu.VMEM)],
        out_specs=pl.BlockSpec(memory_space=pltpu.VMEM),
        scratch_shapes=[
            shape(2, 2, chunk), shape(2, 2, chunk), shape(2, 2, blocks), shape(blocks), shape(blocks),
            pltpu.SemaphoreType.DMA((2, 2)),
            pltpu.SemaphoreType.DMA((2, 2)),
            pltpu.SemaphoreType.DMA((2, 2, 2)),
            pltpu.SemaphoreType.DMA((2, 2, 2)),
            pltpu.SemaphoreType.DMA((2,)),
            pltpu.SemaphoreType.DMA((2,)),
        ],
        compiler_params=pltpu.CompilerParams(
            collective_id=2, has_side_effects=True, vmem_limit_bytes=48 << 20
        ),
        name="collect",
    )(partial)


def scatter_sum(source, target, used, outputs):
    count, rows, width = source.shape
    step = 8

    def kernel(target_ref, used_ref, source_ref, out_ref, acc):
        t = pl.program_id(0)

        @pl.when(t == 0)
        def _():
            acc[...] = jnp.zeros_like(acc)

        for j in range(step):
            @pl.when(used_ref[t * step + j] > 0)
            def _():
                m = target_ref[t * step + j]
                acc[m] = acc[m] + source_ref[j].astype(F32)

        @pl.when(t == pl.num_programs(0) - 1)
        def _():
            out_ref[...] = acc[...].astype(out_ref.dtype)

    return pl.pallas_call(
        kernel,
        out_shape=jax.ShapeDtypeStruct((outputs, rows, width), source.dtype),
        grid_spec=pltpu.PrefetchScalarGridSpec(
            num_scalar_prefetch=2,
            grid=(count // step,),
            in_specs=[pl.BlockSpec((step, rows, width), lambda t, *_: (t, 0, 0))],
            out_specs=pl.BlockSpec((outputs, rows, width), lambda t, *_: (0, 0, 0)),
            scratch_shapes=[pltpu.VMEM((outputs, rows, width), F32)],
        ),
        compiler_params=pltpu.CompilerParams(vmem_limit_bytes=48 << 20),
        name="scatter_sum",
    )(target, used, source)


def layer(position, live, arrived, tokens, grad_out, w_query, w_pair, w_out, slots):
    patches, block, width = tokens.shape
    requests = position.shape[0] // patches
    far = requests * block
    rows = block + far
    chunks = 4
    chunk = far // chunks
    pairs = width // 128
    parts = requests + 1

    def kernel(
        position_ref, live_ref, arrived_ref, tokens_ref, grad_ref, wq_ref, wkv_ref, wo_ref,
        attn_ref, tokgrad_ref, fargrad_ref, x_ref, dkv_ref, dq_ref, mixed_ref,
        key_s, val_s, q_s, up_s, s_s, dp_s, pb_s, ds_s, fg_s, in_sem, out_sem,
    ):
        p = pl.program_id(0)

        def fetch(r):
            return pltpu.make_async_copy(
                arrived_ref.at[position_ref[p * requests + r]],
                x_ref.at[0, pl.ds(block + r * block, block)],
                in_sem.at[r],
            )

        for r in range(requests):
            fetch(r).start()
        tok = tokens_ref[0]
        x_ref[0, 0:block] = tok
        q_s[...] = mm(tok, wq_ref[...]).astype(BF16)
        own = mm(tok, wkv_ref[...]).astype(BF16)
        key_s[0:block] = own[:, :width]
        val_s[0:block] = own[:, width:]
        up_s[...] = mm(grad_ref[0], wo_ref[...], NT).astype(BF16)
        for r in range(requests):
            fetch(r).wait()

        @pl.loop(0, chunks)
        def _(c):
            at = pl.multiple_of(block + c * chunk, 128)
            x = x_ref[0, pl.ds(at, chunk)]
            key_s[pl.ds(at, chunk)] = mm(x, wkv_ref[:, :width]).astype(BF16)
            val_s[pl.ds(at, chunk)] = mm(x, wkv_ref[:, width:]).astype(BF16)

        low = lax.broadcasted_iota(jnp.int32, (block, 128), 1) < HD
        zero = jnp.zeros((block, 128), BF16)

        @pl.loop(0, pairs)
        def _(j):
            lanes = pl.ds(pl.multiple_of(j * 128, 128), 128)
            k = key_s[:, lanes]
            v = val_s[:, lanes]
            q = q_s[:, lanes] * jnp.asarray(1.0 / math.sqrt(HD), BF16)
            u = up_s[:, lanes]
            q2 = jnp.concatenate([jnp.where(low, q, zero), jnp.where(low, zero, q)], axis=0)
            u2 = jnp.concatenate([jnp.where(low, u, zero), jnp.where(low, zero, u)], axis=0)
            s_s[...] = mm(k, q2, NT)
            dp_s[...] = mm(v, u2, NT)

            def bias(r):
                dead = live_ref[p * requests + jnp.maximum(r - 1, 0)] == 0
                return jnp.where((r > 0) & dead, -jnp.inf, 0.0).astype(F32)

            def part(r):
                return pl.ds(pl.multiple_of(r * block, block), block)

            def largest(r, m):
                s = s_s[part(r)] + bias(r)
                return jnp.maximum(m, jnp.max(s.reshape(block // 8, 8, 2 * block), axis=0))

            m = lax.fori_loop(0, parts, largest, jnp.full((8, 2 * block), -jnp.inf, F32))
            m = jnp.max(m, axis=0, keepdims=True)

            def exps(r, carry):
                total, delta = carry
                e = jnp.exp(s_s[part(r)] + bias(r) - m)
                s_s[part(r)] = e
                g = e * dp_s[part(r)]
                fold = lambda t: jnp.sum(t.reshape(block // 8, 8, 2 * block), axis=0)
                return total + fold(e), delta + fold(g)

            nil = jnp.zeros((8, 2 * block), F32)
            total, delta = lax.fori_loop(0, parts, exps, (nil, nil))
            inverse = 1.0 / jnp.sum(total, axis=0, keepdims=True)
            delta = jnp.sum(delta, axis=0, keepdims=True) * inverse

            @pl.loop(0, parts)
            def _(r):
                prob = s_s[part(r)] * inverse
                pb_s[part(r)] = prob.astype(BF16)
                ds_s[part(r)] = (prob * (dp_s[part(r)] - delta)).astype(BF16)

            pb = pb_s[...]
            ds = ds_s[...]
            dkv_ref[0, :, lanes] = mm(ds, q2).astype(BF16)
            dkv_ref[0, :, pl.ds(pl.multiple_of(width + j * 128, 128), 128)] = mm(pb, u2).astype(BF16)
            o = mm(pb, v, TN)
            mixed_ref[0, :, lanes] = jnp.where(low, o[:block], o[block:]).astype(BF16)
            dq = mm(ds, k, TN)
            dq = jnp.where(low, dq[:block], dq[block:]) * (1.0 / math.sqrt(HD))
            dq_ref[0, :, lanes] = dq.astype(BF16)

        attn_ref[0] = mm(mixed_ref[0], wo_ref[...]).astype(BF16)
        tokgrad_ref[0] = (
            mm(dq_ref[0], wq_ref[...], NT) + mm(dkv_ref[0, 0:block], wkv_ref[...], NT)
        ).astype(BF16)

        @pl.loop(0, chunks)
        def _(c):
            at = pl.multiple_of(block + c * chunk, 128)
            g = mm(dkv_ref[0, pl.ds(at, chunk)], wkv_ref[...], NT).astype(BF16)
            fg_s[pl.ds(pl.multiple_of(c * chunk, 128), chunk)] = g

        def put(r):
            return pltpu.make_async_copy(
                fg_s.at[pl.ds(r * block, block)],
                fargrad_ref.at[position_ref[p * requests + r]],
                out_sem.at[r],
            )

        for r in range(requests):
            put(r).start()
        for r in range(requests):
            put(r).wait()

    per_patch = lambda n, w: pl.BlockSpec((1, n, w), lambda p, *_: (p, 0, 0))
    whole = lambda a: pl.BlockSpec(a.shape, lambda p, *_: (0, 0), pipeline_mode=pl.Buffered(1))
    hbm = pl.BlockSpec(memory_space=pl.ANY)
    shape = lambda *s: jax.ShapeDtypeStruct(s, BF16)
    return pl.pallas_call(
        kernel,
        out_shape=(
            shape(patches, block, width),
            shape(patches, block, width),
            shape(slots, block, width),
            shape(patches, rows, width),
            shape(patches, rows, 2 * width),
            shape(patches, block, width),
            shape(patches, block, width),
        ),
        grid_spec=pltpu.PrefetchScalarGridSpec(
            num_scalar_prefetch=2,
            grid=(patches,),
            in_specs=[
                hbm, per_patch(block, width), per_patch(block, width),
                whole(w_query), whole(w_pair), whole(w_out),
            ],
            out_specs=(
                per_patch(block, width), per_patch(block, width), hbm, per_patch(rows, width),
                per_patch(rows, 2 * width), per_patch(block, width), per_patch(block, width),
            ),
            scratch_shapes=[
                pltpu.VMEM((rows, width), BF16),
                pltpu.VMEM((rows, width), BF16),
                pltpu.VMEM((block, width), BF16),
                pltpu.VMEM((block, width), BF16),
                pltpu.VMEM((rows, 2 * block), F32),
                pltpu.VMEM((rows, 2 * block), F32),
                pltpu.VMEM((rows, 2 * block), BF16),
                pltpu.VMEM((rows, 2 * block), BF16),
                pltpu.VMEM((far, width), BF16),
                pltpu.SemaphoreType.DMA((requests,)),
                pltpu.SemaphoreType.DMA((requests,)),
            ],
        ),
        compiler_params=pltpu.CompilerParams(vmem_limit_bytes=60 << 20),
        name="layer",
    )(position, live, arrived, tokens, grad_out, w_query, w_pair, w_out)


def outer_sum(left, right):
    return lax.dot_general(left, right, TN, preferred_element_type=F32)


def body(
    query_tokens, past_tokens, source_dev, source_slot, kept, w_query, w_key, w_value, w_out,
    grad_out,
):
    _, patches, block, width = query_tokens.shape
    tokens, grads, past = query_tokens[0], grad_out[0], past_tokens[0]
    peers = lax.axis_size("patch")
    y, x, z, _ = place()
    per_device = patches * source_dev.shape[1] * source_dev.shape[2]
    cap = 8

    grid = lambda a: a.reshape(4, 2, 4, per_device)
    near = lambda a: jnp.concatenate([grid(a)[y, x], grid(a)[:, x, z]], axis=0)
    owner, slot = near(source_dev), near(source_slot)
    from_y, half, from_z = owner // 8, (owner // 4) % 2, owner % 4
    key = half * 4 + jnp.where(half == 0, from_z, from_y)
    number = jnp.where(half == 0, from_y, from_z) * past.shape[0] + slot
    order = jnp.arange(per_device)
    matches = (key[:, :, None] == key[:, None, :]) & (order[:, None] > order[None, :])
    rank = jnp.sum(matches.astype(jnp.int32), axis=2)
    chosen_here = jnp.where(jnp.arange(8) < 4, z, 4 + y)
    hit = (rank[:, :, None] == jnp.arange(cap)) & (key == chosen_here[:, None])[:, :, None]
    table = jnp.sum(jnp.where(hit, number[:, :, None], 0), axis=1)
    used = jnp.sum(hit.astype(jnp.int32), axis=1).reshape(-1)
    target = (table + jnp.where(jnp.arange(8) < 4, 0, 4 * past.shape[0])[:, None]).reshape(-1)
    mine = key[z] * cap + rank[z]
    live = grid(kept)[y, x, z]

    arrived = spread(past, table.reshape(-1))
    w_pair = jnp.concatenate([w_key, w_value], axis=1)
    attn, token_grad, far_grad, seen, dkv, dq, mixed = layer(
        mine, live, arrived, tokens, grads, w_query, w_pair, w_out, 8 * cap
    )
    returned = send_back(far_grad)
    partial = scatter_sum(returned, target, used, 8 * past.shape[0])
    past_grad = collect(partial.reshape((8,) + past.shape))
    flat = lambda a: a.reshape(-1, a.shape[-1])
    grad_pair = outer_sum(flat(seen), flat(dkv))
    grad_wq = outer_sum(flat(tokens), flat(dq))
    grad_wo = outer_sum(flat(mixed), flat(grads))
    grad_pair, grad_wq, grad_wo = lax.psum((grad_pair, grad_wq, grad_wo), ("dp", "patch"))
    scale = 1.0 / math.sqrt(lax.axis_size("dp") * peers * patches * block)
    return (
        attn[None],
        token_grad[None],
        past_grad[None],
        grad_wq * scale,
        grad_pair[:, :width] * scale,
        grad_pair[:, width:] * scale,
        grad_wo * scale,
    )


def solution(mesh):
    split = P("dp", "patch", None, None)
    return jax.shard_map(
        body,
        mesh=mesh,
        in_specs=(split, split, P(), P(), P(), P(), P(), P(), P(), split),
        out_specs=(split, split, split, P(), P(), P(), P()),
        check_vma=False,
    )
```

```python
import math

import jax
import jax.numpy as jnp
from jax import lax
from jax.experimental import pallas as pl
from jax.experimental.pallas import tpu as pltpu
from jax.sharding import PartitionSpec as P

H = 12
HD = 64
F32 = jnp.float32
MESH = pl.DeviceIdType.MESH
BF16 = jnp.bfloat16
NN = (((1,), (0,)), ((), ()))
NT = (((1,), (1,)), ((), ()))
TN = (((0,), (0,)), ((), ()))


def mm(a, b, dims=NN):
    return lax.dot_general(a, b, dims, preferred_element_type=F32)


def place():
    device = lax.axis_index("patch")
    return device // 8, (device // 4) % 2, device % 4, lax.axis_index("dp")


def step_id(y, x, z, dim, hop):
    return ((y + hop * (1 - dim)) % 4) * 8 + x * 4 + (z + hop * dim) % 4


def meet(y, x, z, dp, across):
    barrier = pltpu.get_barrier_semaphore()
    ids = [step_id(y, x, z, dim, hop) for dim in (0, 1) for hop in (1, 2, 3)]
    if across:
        ids.append(y * 8 + (1 - x) * 4 + z)
    for other in ids:
        pl.semaphore_signal(barrier, 1, device_id=(dp, other), device_id_type=MESH)
    pl.semaphore_wait(barrier, len(ids))


def spread(past, table):
    blocks, rows, width = past.shape
    chunk = blocks // 2
    cap = 8

    def kernel(
        table_ref, past_ref, out_ref, have_a, have_b, sel_a, sel_b,
        in_sem, x_send, x_recv, g_send, g_recv, e_send, e_recv, own_sem,
    ):
        y, x, z, dp = place()
        pos = lambda dim, hop=0: (y * (1 - dim) + z * dim + hop) % 4
        have, sel = (have_a, have_b), (sel_a, sel_b)
        half = (x, 1 - x)

        def region(t, hop, c):
            return have[t].at[pl.ds(pos(half[t], hop) * blocks + c * chunk, chunk)]

        local = pltpu.make_async_copy(
            past_ref, have_a.at[pl.ds(pos(half[0]) * blocks, blocks)], in_sem
        )
        local.start()
        meet(y, x, z, dp, True)

        def cross(c):
            at = pl.ds(pos(half[0]) * blocks + c * chunk, chunk)
            return pltpu.make_async_remote_copy(
                past_ref.at[pl.ds(c * chunk, chunk)], have_b.at[at], x_send.at[c], x_recv.at[c],
                device_id=(dp, y * 8 + (1 - x) * 4 + z), device_id_type=MESH,
            )

        def crossed(c):
            at = pl.ds(pos(half[1]) * blocks + c * chunk, chunk)
            return pltpu.make_async_remote_copy(
                past_ref.at[pl.ds(c * chunk, chunk)], have_b.at[at], x_send.at[c], x_recv.at[c],
                device_id=(dp, y * 8 + (1 - x) * 4 + z), device_id_type=MESH,
            )

        ways = ((1, 0, 0), (3, 0, 1), (1, 0, 1), (3, 0, 0), (1, 3, 0), (3, 1, 1))

        def go(t, n):
            way, owner, c = ways[n]
            return pltpu.make_async_remote_copy(
                region(t, owner, c), region(t, owner, c), g_send.at[t, n], g_recv.at[t, n],
                device_id=(dp, step_id(y, x, z, half[t], way)), device_id_type=MESH,
            )

        def came(t, n):
            way, owner, c = ways[n]
            owner = (owner - way) % 4
            return pltpu.make_async_remote_copy(
                region(t, owner, c), region(t, owner, c), g_send.at[t, n], g_recv.at[t, n],
                device_id=(dp, step_id(y, x, z, half[t], way)), device_id_type=MESH,
            )

        def swap(t, hop, arriving=False):
            h = half[t]
            at = h * 4 + pos(1 - h, -hop if arriving else 0)
            return pltpu.make_async_remote_copy(
                sel[t].at[hop], out_ref.at[pl.ds(at * cap, cap)],
                e_send.at[t, hop - 1], e_recv.at[t, hop - 1],
                device_id=(dp, step_id(y, x, z, 1 - h, hop)), device_id_type=MESH,
            )

        def keep(t):
            h = half[t]
            at = h * 4 + pos(1 - h)
            return pltpu.make_async_copy(
                sel[t].at[0], out_ref.at[pl.ds(at * cap, cap)], own_sem.at[t]
            )

        def choose(t):
            h = half[t]
            for hop in (2, 1, 3, 0):
                row = h * 4 + pos(1 - h, hop)

                @pl.loop(0, cap)
                def _(s):
                    sel[t][hop, s] = have[t][table_ref[row * cap + s]]

                if hop:
                    swap(t, hop).start()
                else:
                    keep(t).start()

        cross(0).start()
        cross(1).start()
        local.wait()
        for n in range(4):
            go(0, n).start()
        crossed(0).wait_recv()
        go(1, 0).start()
        go(1, 3).start()
        came(0, 0).wait_recv()
        go(0, 4).start()
        came(0, 1).wait_recv()
        go(0, 5).start()
        crossed(1).wait_recv()
        go(1, 1).start()
        go(1, 2).start()
        for n in (2, 3, 4, 5):
            came(0, n).wait_recv()
        came(1, 0).wait_recv()
        go(1, 4).start()
        came(1, 1).wait_recv()
        go(1, 5).start()
        for n in (2, 3, 4, 5):
            came(1, n).wait_recv()
        choose(0)
        choose(1)
        for t in (0, 1):
            for hop in (1, 2, 3):
                swap(t, hop, True).wait_recv()
            keep(t).wait()
        for t in (0, 1):
            cross(t).wait_send()
            for n in range(6):
                go(t, n).wait_send()
            for hop in (1, 2, 3):
                swap(t, hop).wait_send()

    return pl.pallas_call(
        kernel,
        out_shape=jax.ShapeDtypeStruct((8 * cap, rows, width), past.dtype),
        in_specs=[pl.BlockSpec(memory_space=pltpu.SMEM), pl.BlockSpec(memory_space=pl.ANY)],
        out_specs=pl.BlockSpec(memory_space=pl.ANY),
        scratch_shapes=[
            pltpu.VMEM((4 * blocks, rows, width), past.dtype),
            pltpu.VMEM((4 * blocks, rows, width), past.dtype),
            pltpu.VMEM((4, cap, rows, width), past.dtype),
            pltpu.VMEM((4, cap, rows, width), past.dtype),
            pltpu.SemaphoreType.DMA,
            pltpu.SemaphoreType.DMA((2,)),
            pltpu.SemaphoreType.DMA((2,)),
            pltpu.SemaphoreType.DMA((2, 6)),
            pltpu.SemaphoreType.DMA((2, 6)),
            pltpu.SemaphoreType.DMA((2, 3)),
            pltpu.SemaphoreType.DMA((2, 3)),
            pltpu.SemaphoreType.DMA((2,)),
        ],
        compiler_params=pltpu.CompilerParams(
            collective_id=0, has_side_effects=True, vmem_limit_bytes=48 << 20
        ),
        name="spread",
    )(table, past)


def send_back(grads):
    slots, rows, width = grads.shape
    cap = slots // 8

    def kernel(grad_ref, out_ref, own, send, recv, own_sem):
        y, x, z, dp = place()
        pos = lambda dim, hop=0: (y * (1 - dim) + z * dim + hop) % 4
        part = lambda ref, at: ref.at[pl.ds(at * cap, cap)]

        def swap(h, hop, arriving=False):
            return pltpu.make_async_remote_copy(
                part(grad_ref, h * 4 + pos(1 - h, hop)),
                part(out_ref, h * 4 + pos(1 - h, -hop if arriving else 0)),
                send.at[h, hop - 1], recv.at[h, hop - 1],
                device_id=(dp, step_id(y, x, z, 1 - h, hop)), device_id_type=MESH,
            )

        def load(h):
            return pltpu.make_async_copy(
                part(grad_ref, h * 4 + pos(1 - h)), own.at[h], own_sem.at[h]
            )

        def store(h):
            return pltpu.make_async_copy(
                own.at[h], part(out_ref, h * 4 + pos(1 - h)), own_sem.at[h]
            )

        for h in (0, 1):
            load(h).start()
        meet(y, x, z, dp, False)
        for hop in (2, 1, 3):
            for h in (0, 1):
                swap(h, hop).start()
        for h in (0, 1):
            load(h).wait()
            store(h).start()
        for h in (0, 1):
            store(h).wait()
            for hop in (1, 2, 3):
                swap(h, hop, True).wait_recv()
        for h in (0, 1):
            for hop in (1, 2, 3):
                swap(h, hop).wait_send()

    return pl.pallas_call(
        kernel,
        out_shape=jax.ShapeDtypeStruct(grads.shape, grads.dtype),
        in_specs=[pl.BlockSpec(memory_space=pl.ANY)],
        out_specs=pl.BlockSpec(memory_space=pl.ANY),
        scratch_shapes=[
            pltpu.VMEM((2, cap, rows, width), grads.dtype),
            pltpu.SemaphoreType.DMA((2, 3)),
            pltpu.SemaphoreType.DMA((2, 3)),
            pltpu.SemaphoreType.DMA((2,)),
        ],
        compiler_params=pltpu.CompilerParams(
            collective_id=1, has_side_effects=True, vmem_limit_bytes=32 << 20
        ),
        name="send_back",
    )(grads)


def collect(partial):
    groups, blocks, rows, width = partial.shape
    chunk = blocks // 2

    def kernel(
        part_ref, out_ref, relay, staged, inward, mine, across,
        r_send, r_recv, d_send, d_recv, x_send, x_recv,
    ):
        y, x, z, dp = place()
        pos = lambda dim, hop=0: (y * (1 - dim) + z * dim + hop) % 4
        half = (1 - x, x)
        meet(y, x, z, dp, True)
        ways = (3, 1)

        def row(t, hop):
            return half[t] * 4 + pos(half[t], hop)

        def pass_on(t, side):
            return pltpu.make_async_remote_copy(
                part_ref.at[row(t, 2), pl.ds(side * chunk, chunk)], relay.at[t, side],
                r_send.at[t, side], r_recv.at[t, side],
                device_id=(dp, step_id(y, x, z, half[t], ways[side])), device_id_type=MESH,
            )

        def direct(t, side, summed):
            c = side if summed else 1 - side
            source = (
                staged.at[t, side] if summed
                else part_ref.at[row(t, ways[side]), pl.ds(c * chunk, chunk)]
            )
            return pltpu.make_async_remote_copy(
                source, inward.at[t, side, pl.ds(c * chunk, chunk)],
                d_send.at[t, side, int(summed)], d_recv.at[t, side, int(summed)],
                device_id=(dp, step_id(y, x, z, half[t], ways[side])), device_id_type=MESH,
            )

        def cross(c):
            return pltpu.make_async_remote_copy(
                mine.at[pl.ds(c * chunk, chunk)], across.at[pl.ds(c * chunk, chunk)],
                x_send.at[c], x_recv.at[c],
                device_id=(dp, y * 8 + (1 - x) * 4 + z), device_id_type=MESH,
            )

        def final(t, b):
            return (
                part_ref[row(t, 0), b].astype(F32)
                + inward[t, 0, b].astype(F32)
                + inward[t, 1, b].astype(F32)
            )

        for t in (0, 1):
            for side in (0, 1):
                pass_on(t, side).start()
        for t in (0, 1):
            for side in (0, 1):
                direct(t, side, False).start()
        for t in (0, 1):
            for side in (0, 1):
                pass_on(t, side).wait_recv()

                @pl.loop(0, chunk)
                def _(b):
                    own = part_ref[row(t, ways[side]), side * chunk + b]
                    staged[t, side, b] = (
                        own.astype(F32) + relay[t, side, b].astype(F32)
                    ).astype(staged.dtype)

                direct(t, side, True).start()
        for side in (0, 1):
            for summed in (False, True):
                direct(0, side, summed).wait_recv()
        for c in (0, 1):
            @pl.loop(0, chunk)
            def _(b):
                mine[c * chunk + b] = final(0, c * chunk + b).astype(mine.dtype)

            cross(c).start()
        for side in (0, 1):
            for summed in (False, True):
                direct(1, side, summed).wait_recv()
        for c in (0, 1):
            cross(c).wait_recv()

            @pl.loop(0, chunk)
            def _(b):
                at = c * chunk + b
                out_ref[at] = (final(1, at) + across[at].astype(F32)).astype(out_ref.dtype)

        for t in (0, 1):
            cross(t).wait_send()
            for side in (0, 1):
                pass_on(t, side).wait_send()
                for summed in (False, True):
                    direct(t, side, summed).wait_send()

    shape = lambda *s: pltpu.VMEM(s + (rows, width), partial.dtype)
    return pl.pallas_call(
        kernel,
        out_shape=jax.ShapeDtypeStruct((blocks, rows, width), partial.dtype),
        in_specs=[pl.BlockSpec(memory_space=pltpu.VMEM)],
        out_specs=pl.BlockSpec(memory_space=pltpu.VMEM),
        scratch_shapes=[
            shape(2, 2, chunk), shape(2, 2, chunk), shape(2, 2, blocks), shape(blocks), shape(blocks),
            pltpu.SemaphoreType.DMA((2, 2)),
            pltpu.SemaphoreType.DMA((2, 2)),
            pltpu.SemaphoreType.DMA((2, 2, 2)),
            pltpu.SemaphoreType.DMA((2, 2, 2)),
            pltpu.SemaphoreType.DMA((2,)),
            pltpu.SemaphoreType.DMA((2,)),
        ],
        compiler_params=pltpu.CompilerParams(
            collective_id=2, has_side_effects=True, vmem_limit_bytes=48 << 20
        ),
        name="collect",
    )(partial)


def scatter_sum(source, target, used, outputs):
    count, rows, width = source.shape
    step = 8

    def kernel(target_ref, used_ref, source_ref, out_ref, acc):
        t = pl.program_id(0)

        @pl.when(t == 0)
        def _():
            acc[...] = jnp.zeros_like(acc)

        for j in range(step):
            @pl.when(used_ref[t * step + j] > 0)
            def _():
                m = target_ref[t * step + j]
                acc[m] = acc[m] + source_ref[j].astype(F32)

        @pl.when(t == pl.num_programs(0) - 1)
        def _():
            out_ref[...] = acc[...].astype(out_ref.dtype)

    return pl.pallas_call(
        kernel,
        out_shape=jax.ShapeDtypeStruct((outputs, rows, width), source.dtype),
        grid_spec=pltpu.PrefetchScalarGridSpec(
            num_scalar_prefetch=2,
            grid=(count // step,),
            in_specs=[pl.BlockSpec((step, rows, width), lambda t, *_: (t, 0, 0))],
            out_specs=pl.BlockSpec((outputs, rows, width), lambda t, *_: (0, 0, 0)),
            scratch_shapes=[pltpu.VMEM((outputs, rows, width), F32)],
        ),
        compiler_params=pltpu.CompilerParams(vmem_limit_bytes=48 << 20),
        name="scatter_sum",
    )(target, used, source)


def layer(position, live, arrived, tokens, grad_out, w_query, w_pair, w_out, slots):
    patches, block, width = tokens.shape
    requests = position.shape[0] // patches
    far = requests * block
    rows = block + far
    chunks = 4
    chunk = far // chunks
    pairs = width // 128
    parts = requests + 1

    def kernel(
        position_ref, live_ref, arrived_ref, tokens_ref, grad_ref, wq_ref, wkv_ref, wo_ref,
        attn_ref, tokgrad_ref, fargrad_ref, x_ref, dkv_ref, dq_ref, mixed_ref,
        key_s, val_s, q_s, up_s, s_s, dp_s, pb_s, ds_s, fg_s, in_sem, out_sem,
    ):
        p = pl.program_id(0)

        def fetch(r):
            return pltpu.make_async_copy(
                arrived_ref.at[position_ref[p * requests + r]],
                x_ref.at[0, pl.ds(block + r * block, block)],
                in_sem.at[r],
            )

        for r in range(requests):
            fetch(r).start()
        tok = tokens_ref[0]
        x_ref[0, 0:block] = tok
        q_s[...] = mm(tok, wq_ref[...]).astype(BF16)
        own = mm(tok, wkv_ref[...]).astype(BF16)
        key_s[0:block] = own[:, :width]
        val_s[0:block] = own[:, width:]
        up_s[...] = mm(grad_ref[0], wo_ref[...], NT).astype(BF16)
        for r in range(requests):
            fetch(r).wait()

        @pl.loop(0, chunks)
        def _(c):
            at = pl.multiple_of(block + c * chunk, 128)
            x = x_ref[0, pl.ds(at, chunk)]
            key_s[pl.ds(at, chunk)] = mm(x, wkv_ref[:, :width]).astype(BF16)
            val_s[pl.ds(at, chunk)] = mm(x, wkv_ref[:, width:]).astype(BF16)

        low = lax.broadcasted_iota(jnp.int32, (block, 128), 1) < HD
        zero = jnp.zeros((block, 128), BF16)

        @pl.loop(0, pairs)
        def _(j):
            lanes = pl.ds(pl.multiple_of(j * 128, 128), 128)
            k = key_s[:, lanes]
            v = val_s[:, lanes]
            q = q_s[:, lanes] * jnp.asarray(1.0 / math.sqrt(HD), BF16)
            u = up_s[:, lanes]
            q2 = jnp.concatenate([jnp.where(low, q, zero), jnp.where(low, zero, q)], axis=0)
            u2 = jnp.concatenate([jnp.where(low, u, zero), jnp.where(low, zero, u)], axis=0)
            s_s[...] = mm(k, q2, NT)
            dp_s[...] = mm(v, u2, NT)

            def bias(r):
                dead = live_ref[p * requests + jnp.maximum(r - 1, 0)] == 0
                return jnp.where((r > 0) & dead, -jnp.inf, 0.0).astype(F32)

            def part(r):
                return pl.ds(pl.multiple_of(r * block, block), block)

            def largest(r, m):
                s = s_s[part(r)] + bias(r)
                return jnp.maximum(m, jnp.max(s.reshape(block // 8, 8, 2 * block), axis=0))

            m = lax.fori_loop(0, parts, largest, jnp.full((8, 2 * block), -jnp.inf, F32))
            m = jnp.max(m, axis=0, keepdims=True)

            def exps(r, carry):
                total, delta = carry
                e = jnp.exp(s_s[part(r)] + bias(r) - m)
                s_s[part(r)] = e
                g = e * dp_s[part(r)]
                fold = lambda t: jnp.sum(t.reshape(block // 8, 8, 2 * block), axis=0)
                return total + fold(e), delta + fold(g)

            nil = jnp.zeros((8, 2 * block), F32)
            total, delta = lax.fori_loop(0, parts, exps, (nil, nil))
            inverse = 1.0 / jnp.sum(total, axis=0, keepdims=True)
            delta = jnp.sum(delta, axis=0, keepdims=True) * inverse

            @pl.loop(0, parts)
            def _(r):
                prob = s_s[part(r)] * inverse
                pb_s[part(r)] = prob.astype(BF16)
                ds_s[part(r)] = (prob * (dp_s[part(r)] - delta)).astype(BF16)

            pb = pb_s[...]
            ds = ds_s[...]
            dkv_ref[0, :, lanes] = mm(ds, q2).astype(BF16)
            dkv_ref[0, :, pl.ds(pl.multiple_of(width + j * 128, 128), 128)] = mm(pb, u2).astype(BF16)
            o = mm(pb, v, TN)
            mixed_ref[0, :, lanes] = jnp.where(low, o[:block], o[block:]).astype(BF16)
            dq = mm(ds, k, TN)
            dq = jnp.where(low, dq[:block], dq[block:]) * (1.0 / math.sqrt(HD))
            dq_ref[0, :, lanes] = dq.astype(BF16)

        attn_ref[0] = mm(mixed_ref[0], wo_ref[...]).astype(BF16)
        tokgrad_ref[0] = (
            mm(dq_ref[0], wq_ref[...], NT) + mm(dkv_ref[0, 0:block], wkv_ref[...], NT)
        ).astype(BF16)

        @pl.loop(0, chunks)
        def _(c):
            at = pl.multiple_of(block + c * chunk, 128)
            g = mm(dkv_ref[0, pl.ds(at, chunk)], wkv_ref[...], NT).astype(BF16)
            fg_s[pl.ds(pl.multiple_of(c * chunk, 128), chunk)] = g

        def put(r):
            return pltpu.make_async_copy(
                fg_s.at[pl.ds(r * block, block)],
                fargrad_ref.at[position_ref[p * requests + r]],
                out_sem.at[r],
            )

        for r in range(requests):
            put(r).start()
        for r in range(requests):
            put(r).wait()

    per_patch = lambda n, w: pl.BlockSpec((1, n, w), lambda p, *_: (p, 0, 0))
    whole = lambda a: pl.BlockSpec(a.shape, lambda p, *_: (0, 0), pipeline_mode=pl.Buffered(1))
    hbm = pl.BlockSpec(memory_space=pl.ANY)
    shape = lambda *s: jax.ShapeDtypeStruct(s, BF16)
    return pl.pallas_call(
        kernel,
        out_shape=(
            shape(patches, block, width),
            shape(patches, block, width),
            shape(slots, block, width),
            shape(patches, rows, width),
            shape(patches, rows, 2 * width),
            shape(patches, block, width),
            shape(patches, block, width),
        ),
        grid_spec=pltpu.PrefetchScalarGridSpec(
            num_scalar_prefetch=2,
            grid=(patches,),
            in_specs=[
                hbm, per_patch(block, width), per_patch(block, width),
                whole(w_query), whole(w_pair), whole(w_out),
            ],
            out_specs=(
                per_patch(block, width), per_patch(block, width), hbm, per_patch(rows, width),
                per_patch(rows, 2 * width), per_patch(block, width), per_patch(block, width),
            ),
            scratch_shapes=[
                pltpu.VMEM((rows, width), BF16),
                pltpu.VMEM((rows, width), BF16),
                pltpu.VMEM((block, width), BF16),
                pltpu.VMEM((block, width), BF16),
                pltpu.VMEM((rows, 2 * block), F32),
                pltpu.VMEM((rows, 2 * block), F32),
                pltpu.VMEM((rows, 2 * block), BF16),
                pltpu.VMEM((rows, 2 * block), BF16),
                pltpu.VMEM((far, width), BF16),
                pltpu.SemaphoreType.DMA((requests,)),
                pltpu.SemaphoreType.DMA((requests,)),
            ],
        ),
        compiler_params=pltpu.CompilerParams(vmem_limit_bytes=60 << 20),
        name="layer",
    )(position, live, arrived, tokens, grad_out, w_query, w_pair, w_out)


def outer_sum(left, right):
    return lax.dot_general(left, right, TN, preferred_element_type=F32)


def body(
    query_tokens, past_tokens, source_dev, source_slot, kept, w_query, w_key, w_value, w_out,
    grad_out,
):
    _, patches, block, width = query_tokens.shape
    tokens, grads, past = query_tokens[0], grad_out[0], past_tokens[0]
    peers = lax.axis_size("patch")
    y, x, z, _ = place()
    per_device = patches * source_dev.shape[1] * source_dev.shape[2]
    cap = 8

    grid = lambda a: a.reshape(4, 2, 4, per_device)
    near = lambda a: jnp.concatenate([grid(a)[y, x], grid(a)[:, x, z]], axis=0)
    owner, slot = near(source_dev), near(source_slot)
    from_y, half, from_z = owner // 8, (owner // 4) % 2, owner % 4
    key = half * 4 + jnp.where(half == 0, from_z, from_y)
    number = jnp.where(half == 0, from_y, from_z) * past.shape[0] + slot
    order = jnp.arange(per_device)
    matches = (key[:, :, None] == key[:, None, :]) & (order[:, None] > order[None, :])
    rank = jnp.sum(matches.astype(jnp.int32), axis=2)
    chosen_here = jnp.where(jnp.arange(8) < 4, z, 4 + y)
    hit = (rank[:, :, None] == jnp.arange(cap)) & (key == chosen_here[:, None])[:, :, None]
    table = jnp.sum(jnp.where(hit, number[:, :, None], 0), axis=1)
    used = jnp.sum(hit.astype(jnp.int32), axis=1).reshape(-1)
    target = (table + jnp.where(jnp.arange(8) < 4, 0, 4 * past.shape[0])[:, None]).reshape(-1)
    mine = key[z] * cap + rank[z]
    live = grid(kept)[y, x, z]

    arrived = spread(past, table.reshape(-1))
    w_pair = jnp.concatenate([w_key, w_value], axis=1)
    attn, token_grad, far_grad, seen, dkv, dq, mixed = layer(
        mine, live, arrived, tokens, grads, w_query, w_pair, w_out, 8 * cap
    )
    returned = send_back(far_grad)
    partial = scatter_sum(returned, target, used, 8 * past.shape[0])
    past_grad = collect(partial.reshape((8,) + past.shape))
    flat = lambda a: a.reshape(-1, a.shape[-1])
    scale = 1.0 / math.sqrt(lax.axis_size("dp") * peers * patches * block)
    dkv, seen = flat(dkv), flat(seen)
    grad_wk = outer_sum(seen, dkv[:, :width]) * scale
    grad_wv = outer_sum(seen, dkv[:, width:]) * scale
    grad_wq = outer_sum(flat(tokens), flat(dq)) * scale
    grad_wo = outer_sum(flat(mixed), flat(grads)) * scale
    grad_wq, grad_wk, grad_wv, grad_wo = lax.psum(
        (grad_wq, grad_wk, grad_wv, grad_wo), ("dp", "patch")
    )
    return (
        attn[None],
        token_grad[None],
        past_grad[None],
        grad_wq,
        grad_wk,
        grad_wv,
        grad_wo,
    )


def solution(mesh):
    split = P("dp", "patch", None, None)
    return jax.shard_map(
        body,
        mesh=mesh,
        in_specs=(split, split, P(), P(), P(), P(), P(), P(), P(), split),
        out_specs=(split, split, split, P(), P(), P(), P()),
        check_vma=False,
    )
```

```python
import math

import jax
import jax.numpy as jnp
from jax import lax
from jax.experimental import pallas as pl
from jax.experimental.pallas import tpu as pltpu
from jax.sharding import PartitionSpec as P

H = 12
HD = 64
F32 = jnp.float32
MESH = pl.DeviceIdType.MESH
BF16 = jnp.bfloat16
NN = (((1,), (0,)), ((), ()))
NT = (((1,), (1,)), ((), ()))
TN = (((0,), (0,)), ((), ()))


def mm(a, b, dims=NN):
    return lax.dot_general(a, b, dims, preferred_element_type=F32)


def place():
    device = lax.axis_index("patch")
    return device // 8, (device // 4) % 2, device % 4, lax.axis_index("dp")


def step_id(y, x, z, dim, hop):
    return ((y + hop * (1 - dim)) % 4) * 8 + x * 4 + (z + hop * dim) % 4


def meet(y, x, z, dp, across):
    barrier = pltpu.get_barrier_semaphore()
    ids = [step_id(y, x, z, dim, hop) for dim in (0, 1) for hop in (1, 2, 3)]
    if across:
        ids.append(y * 8 + (1 - x) * 4 + z)
    for other in ids:
        pl.semaphore_signal(barrier, 1, device_id=(dp, other), device_id_type=MESH)
    pl.semaphore_wait(barrier, len(ids))


def spread(past, table):
    blocks, rows, width = past.shape
    parts = 4
    chunk = blocks // parts
    cap = 8

    def kernel(
        table_ref, past_ref, out_ref, have_a, have_b, sel_a, sel_b,
        in_sem, x_send, x_recv, g_send, g_recv, e_send, e_recv, own_sem,
    ):
        y, x, z, dp = place()
        pos = lambda dim, hop=0: (y * (1 - dim) + z * dim + hop) % 4
        have, sel = (have_a, have_b), (sel_a, sel_b)
        half = (x, 1 - x)

        def region(t, hop, c):
            return have[t].at[pl.ds(pos(half[t], hop) * blocks + c * chunk, chunk)]

        local = pltpu.make_async_copy(
            past_ref, have_a.at[pl.ds(pos(half[0]) * blocks, blocks)], in_sem
        )
        local.start()
        meet(y, x, z, dp, True)

        def cross(c):
            at = pl.ds(pos(half[0]) * blocks + c * chunk, chunk)
            return pltpu.make_async_remote_copy(
                past_ref.at[pl.ds(c * chunk, chunk)], have_b.at[at], x_send.at[c], x_recv.at[c],
                device_id=(dp, y * 8 + (1 - x) * 4 + z), device_id_type=MESH,
            )

        def crossed(c):
            at = pl.ds(pos(half[1]) * blocks + c * chunk, chunk)
            return pltpu.make_async_remote_copy(
                past_ref.at[pl.ds(c * chunk, chunk)], have_b.at[at], x_send.at[c], x_recv.at[c],
                device_id=(dp, y * 8 + (1 - x) * 4 + z), device_id_type=MESH,
            )

        turn = (0, 2, 1, 3)
        ways = [(way, 0, c) for c in turn for way in ((1, 3) if c < 2 else (3, 1))]
        ways += [(1, 3, c) if c < 2 else (3, 1, c) for c in turn]

        def go(t, n):
            way, owner, c = ways[n]
            return pltpu.make_async_remote_copy(
                region(t, owner, c), region(t, owner, c), g_send.at[t, n], g_recv.at[t, n],
                device_id=(dp, step_id(y, x, z, half[t], way)), device_id_type=MESH,
            )

        def came(t, n):
            way, owner, c = ways[n]
            owner = (owner - way) % 4
            return pltpu.make_async_remote_copy(
                region(t, owner, c), region(t, owner, c), g_send.at[t, n], g_recv.at[t, n],
                device_id=(dp, step_id(y, x, z, half[t], way)), device_id_type=MESH,
            )

        def swap(t, hop, arriving=False):
            h = half[t]
            at = h * 4 + pos(1 - h, -hop if arriving else 0)
            return pltpu.make_async_remote_copy(
                sel[t].at[hop], out_ref.at[pl.ds(at * cap, cap)],
                e_send.at[t, hop - 1], e_recv.at[t, hop - 1],
                device_id=(dp, step_id(y, x, z, 1 - h, hop)), device_id_type=MESH,
            )

        def keep(t):
            h = half[t]
            at = h * 4 + pos(1 - h)
            return pltpu.make_async_copy(
                sel[t].at[0], out_ref.at[pl.ds(at * cap, cap)], own_sem.at[t]
            )

        def choose(t):
            h = half[t]
            for hop in (2, 1, 3, 0):
                row = h * 4 + pos(1 - h, hop)

                @pl.loop(0, cap)
                def _(s):
                    sel[t][hop, s] = have[t][table_ref[row * cap + s]]

                if hop:
                    swap(t, hop).start()
                else:
                    keep(t).start()

        for c in turn:
            cross(c).start()
        local.wait()
        for n in range(2 * parts):
            go(0, n).start()

        def relay(t, i):
            came(t, 2 * i).wait_recv()
            go(t, 2 * parts + i).start()

        for i in range(parts):
            crossed(turn[i]).wait_recv()
            go(1, 2 * i).start()
            go(1, 2 * i + 1).start()
            relay(0, i)
        for i in range(parts):
            relay(1, i)
        for t in (0, 1):
            for n in range(2 * parts):
                if n % 2:
                    came(t, n).wait_recv()
            for n in range(2 * parts, 3 * parts):
                came(t, n).wait_recv()
        choose(0)
        choose(1)
        for t in (0, 1):
            for hop in (1, 2, 3):
                swap(t, hop, True).wait_recv()
            keep(t).wait()
        for c in turn:
            cross(c).wait_send()
        for t in (0, 1):
            for n in range(3 * parts):
                go(t, n).wait_send()
            for hop in (1, 2, 3):
                swap(t, hop).wait_send()

    return pl.pallas_call(
        kernel,
        out_shape=jax.ShapeDtypeStruct((8 * cap, rows, width), past.dtype),
        in_specs=[pl.BlockSpec(memory_space=pltpu.SMEM), pl.BlockSpec(memory_space=pl.ANY)],
        out_specs=pl.BlockSpec(memory_space=pl.ANY),
        scratch_shapes=[
            pltpu.VMEM((4 * blocks, rows, width), past.dtype),
            pltpu.VMEM((4 * blocks, rows, width), past.dtype),
            pltpu.VMEM((4, cap, rows, width), past.dtype),
            pltpu.VMEM((4, cap, rows, width), past.dtype),
            pltpu.SemaphoreType.DMA,
            pltpu.SemaphoreType.DMA((parts,)),
            pltpu.SemaphoreType.DMA((parts,)),
            pltpu.SemaphoreType.DMA((2, 3 * parts)),
            pltpu.SemaphoreType.DMA((2, 3 * parts)),
            pltpu.SemaphoreType.DMA((2, 3)),
            pltpu.SemaphoreType.DMA((2, 3)),
            pltpu.SemaphoreType.DMA((2,)),
        ],
        compiler_params=pltpu.CompilerParams(
            collective_id=0, has_side_effects=True, vmem_limit_bytes=48 << 20
        ),
        name="spread",
    )(table, past)


def send_back(grads):
    slots, rows, width = grads.shape
    cap = slots // 8

    def kernel(grad_ref, out_ref, own, send, recv, own_sem):
        y, x, z, dp = place()
        pos = lambda dim, hop=0: (y * (1 - dim) + z * dim + hop) % 4
        part = lambda ref, at: ref.at[pl.ds(at * cap, cap)]

        def swap(h, hop, arriving=False):
            return pltpu.make_async_remote_copy(
                part(grad_ref, h * 4 + pos(1 - h, hop)),
                part(out_ref, h * 4 + pos(1 - h, -hop if arriving else 0)),
                send.at[h, hop - 1], recv.at[h, hop - 1],
                device_id=(dp, step_id(y, x, z, 1 - h, hop)), device_id_type=MESH,
            )

        def load(h):
            return pltpu.make_async_copy(
                part(grad_ref, h * 4 + pos(1 - h)), own.at[h], own_sem.at[h]
            )

        def store(h):
            return pltpu.make_async_copy(
                own.at[h], part(out_ref, h * 4 + pos(1 - h)), own_sem.at[h]
            )

        for h in (0, 1):
            load(h).start()
        meet(y, x, z, dp, False)
        for hop in (2, 1, 3):
            for h in (0, 1):
                swap(h, hop).start()
        for h in (0, 1):
            load(h).wait()
            store(h).start()
        for h in (0, 1):
            store(h).wait()
            for hop in (1, 2, 3):
                swap(h, hop, True).wait_recv()
        for h in (0, 1):
            for hop in (1, 2, 3):
                swap(h, hop).wait_send()

    return pl.pallas_call(
        kernel,
        out_shape=jax.ShapeDtypeStruct(grads.shape, grads.dtype),
        in_specs=[pl.BlockSpec(memory_space=pl.ANY)],
        out_specs=pl.BlockSpec(memory_space=pl.ANY),
        scratch_shapes=[
            pltpu.VMEM((2, cap, rows, width), grads.dtype),
            pltpu.SemaphoreType.DMA((2, 3)),
            pltpu.SemaphoreType.DMA((2, 3)),
            pltpu.SemaphoreType.DMA((2,)),
        ],
        compiler_params=pltpu.CompilerParams(
            collective_id=1, has_side_effects=True, vmem_limit_bytes=32 << 20
        ),
        name="send_back",
    )(grads)


def collect(partial):
    groups, blocks, rows, width = partial.shape
    chunk = blocks // 2

    def kernel(
        part_ref, out_ref, relay, staged, inward, mine, across,
        r_send, r_recv, d_send, d_recv, x_send, x_recv,
    ):
        y, x, z, dp = place()
        pos = lambda dim, hop=0: (y * (1 - dim) + z * dim + hop) % 4
        half = (1 - x, x)
        meet(y, x, z, dp, True)
        ways = (3, 1)

        def row(t, hop):
            return half[t] * 4 + pos(half[t], hop)

        def pass_on(t, side):
            return pltpu.make_async_remote_copy(
                part_ref.at[row(t, 2), pl.ds(side * chunk, chunk)], relay.at[t, side],
                r_send.at[t, side], r_recv.at[t, side],
                device_id=(dp, step_id(y, x, z, half[t], ways[side])), device_id_type=MESH,
            )

        def direct(t, side, summed):
            c = side if summed else 1 - side
            source = (
                staged.at[t, side] if summed
                else part_ref.at[row(t, ways[side]), pl.ds(c * chunk, chunk)]
            )
            return pltpu.make_async_remote_copy(
                source, inward.at[t, side, pl.ds(c * chunk, chunk)],
                d_send.at[t, side, int(summed)], d_recv.at[t, side, int(summed)],
                device_id=(dp, step_id(y, x, z, half[t], ways[side])), device_id_type=MESH,
            )

        def cross(c):
            return pltpu.make_async_remote_copy(
                mine.at[pl.ds(c * chunk, chunk)], across.at[pl.ds(c * chunk, chunk)],
                x_send.at[c], x_recv.at[c],
                device_id=(dp, y * 8 + (1 - x) * 4 + z), device_id_type=MESH,
            )

        def final(t, b):
            return (
                part_ref[row(t, 0), b].astype(F32)
                + inward[t, 0, b].astype(F32)
                + inward[t, 1, b].astype(F32)
            )

        for t in (0, 1):
            for side in (0, 1):
                pass_on(t, side).start()
        for t in (0, 1):
            for side in (0, 1):
                direct(t, side, False).start()
        for t in (0, 1):
            for side in (0, 1):
                pass_on(t, side).wait_recv()

                @pl.loop(0, chunk)
                def _(b):
                    own = part_ref[row(t, ways[side]), side * chunk + b]
                    staged[t, side, b] = (
                        own.astype(F32) + relay[t, side, b].astype(F32)
                    ).astype(staged.dtype)

                direct(t, side, True).start()
        for side in (0, 1):
            for summed in (False, True):
                direct(0, side, summed).wait_recv()
        for c in (0, 1):
            @pl.loop(0, chunk)
            def _(b):
                mine[c * chunk + b] = final(0, c * chunk + b).astype(mine.dtype)

            cross(c).start()
        for side in (0, 1):
            for summed in (False, True):
                direct(1, side, summed).wait_recv()
        for c in (0, 1):
            cross(c).wait_recv()

            @pl.loop(0, chunk)
            def _(b):
                at = c * chunk + b
                out_ref[at] = (final(1, at) + across[at].astype(F32)).astype(out_ref.dtype)

        for t in (0, 1):
            cross(t).wait_send()
            for side in (0, 1):
                pass_on(t, side).wait_send()
                for summed in (False, True):
                    direct(t, side, summed).wait_send()

    shape = lambda *s: pltpu.VMEM(s + (rows, width), partial.dtype)
    return pl.pallas_call(
        kernel,
        out_shape=jax.ShapeDtypeStruct((blocks, rows, width), partial.dtype),
        in_specs=[pl.BlockSpec(memory_space=pltpu.VMEM)],
        out_specs=pl.BlockSpec(memory_space=pltpu.VMEM),
        scratch_shapes=[
            shape(2, 2, chunk), shape(2, 2, chunk), shape(2, 2, blocks), shape(blocks), shape(blocks),
            pltpu.SemaphoreType.DMA((2, 2)),
            pltpu.SemaphoreType.DMA((2, 2)),
            pltpu.SemaphoreType.DMA((2, 2, 2)),
            pltpu.SemaphoreType.DMA((2, 2, 2)),
            pltpu.SemaphoreType.DMA((2,)),
            pltpu.SemaphoreType.DMA((2,)),
        ],
        compiler_params=pltpu.CompilerParams(
            collective_id=2, has_side_effects=True, vmem_limit_bytes=48 << 20
        ),
        name="collect",
    )(partial)


def reduce_weights(grads):
    rows, width = grads[0].shape
    block = rows // 24
    half = 48

    def kernel(
        a_ref, b_ref, c_ref, d_ref, out_ref, acc, stage, peer, mid, in_a, mid_b, in_b, in_c, got_b, full,
        core_send, core_recv, send, recv, back_send, back_recv, out_sem,
    ):
        y, x_low, z, dp = place()
        core = dp % 2
        spot = {"x": (dp // 2) * 2 + x_low, "y": y, "z": z}
        orders = ("xyz", "yzx", "zxy")

        def there(axis, hop):
            at = dict(spot)
            at[axis] = (at[axis] + hop) % 4
            return (
                (at["x"] // 2) * 2 + core,
                at["y"] * 8 + (at["x"] % 2) * 4 + at["z"],
            )

        other = (dp + 1 - 2 * core, y * 8 + x_low * 4 + z)
        barrier = pltpu.get_barrier_semaphore()
        for axis in "xyz":
            for hop in (1, 2, 3):
                pl.semaphore_signal(barrier, 1, device_id=there(axis, hop), device_id_type=MESH)
        pl.semaphore_signal(barrier, 1, device_id=other, device_id_type=MESH)

        def take(keep, give):
            for i in (0, 1):
                @pl.loop(0, half // 2)
                def _(n):
                    at = pl.ds(pl.multiple_of(n * block, block), block)
                    stage[i * (half // 2) + n] = give[i][at].astype(BF16)
                    acc[i * (half // 2) + n] = keep[i][at]

        @pl.when(core == 0)
        def _():
            take((a_ref, b_ref), (c_ref, d_ref))

        @pl.when(core == 1)
        def _():
            take((c_ref, d_ref), (a_ref, b_ref))

        pl.semaphore_wait(barrier, 10)

        def pair(p):
            at = pl.ds(p * 16, 16)
            return pltpu.make_async_remote_copy(
                stage.at[at], peer.at[at], core_send.at[p], core_recv.at[p],
                device_id=other, device_id_type=MESH,
            )

        def copy(source, target, phase, p, hop, sems=None):
            s, r = sems or (send, recv)
            return pltpu.make_async_remote_copy(
                source, target, s.at[phase, p, hop - 1], r.at[phase, p, hop - 1],
                device_id=there(orders[p][(0, 1, 2, 1, 0)[phase]], hop), device_id_type=MESH,
            )

        def at_axis(p, phase, hop=0):
            return (spot[orders[p][phase]] + hop) % 4

        def scatter_a(p, hop):
            at = pl.ds(p * 16 + at_axis(p, 0, hop) * 4, 4)
            return copy(mid.at[at], in_a.at[p, hop - 1], 0, p, hop)

        def scatter_b(p, hop):
            return copy(mid_b.at[p, at_axis(p, 1, hop)], in_b.at[p, hop - 1], 1, p, hop)

        def swap_c(p, hop, arriving=False):
            to = at_axis(p, 2, -hop if arriving else 0)
            return copy(in_c.at[p, at_axis(p, 2)], in_c.at[p, to], 2, p, hop)

        def spread_b(p, hop, arriving=False):
            to = at_axis(p, 1, -hop if arriving else 0)
            return copy(got_b.at[p, at_axis(p, 1)], got_b.at[p, to], 3, p, hop)

        def spread_a(p, hop, arriving=False):
            row = lambda back: pl.ds(core * half + p * 16 + at_axis(p, 0, back) * 4, 4)
            return copy(
                full.at[row(0)], full.at[row(-hop if arriving else 0)], 4, p, hop
            )

        def final(p, arriving=False):
            side = 1 - core if arriving else core
            at = pl.ds(side * half + p * 16, 16)
            return pltpu.make_async_remote_copy(
                full.at[at], full.at[at], back_send.at[p], back_recv.at[p],
                device_id=other, device_id_type=MESH,
            )

        hops = (2, 1, 3)
        for p in range(3):
            pair(p).start()
        for p in range(3):
            pair(p).wait_recv()

            @pl.loop(0, 16)
            def _(n):
                total = acc[p * 16 + n] + peer[p * 16 + n].astype(F32)
                acc[p * 16 + n] = total
                mid[p * 16 + n] = total.astype(BF16)

            for hop in hops:
                scatter_a(p, hop).start()
        for p in range(3):
            for hop in hops:
                scatter_a(p, hop).wait_recv()

            @pl.loop(0, 4)
            def _(n):
                at = p * 16 + at_axis(p, 0) * 4 + n
                total = acc[at]
                for i in range(3):
                    total = total + in_a[p, i, n].astype(F32)
                acc[at] = total
                mid_b[p, n] = total.astype(BF16)

            for hop in hops:
                scatter_b(p, hop).start()
        for p in range(3):
            for hop in hops:
                scatter_b(p, hop).wait_recv()
            total = acc[p * 16 + at_axis(p, 0) * 4 + at_axis(p, 1)]
            for i in range(3):
                total = total + in_b[p, i].astype(F32)
            in_c[p, at_axis(p, 2)] = total.astype(BF16)
            for hop in hops:
                swap_c(p, hop).start()
        for p in range(3):
            for hop in hops:
                swap_c(p, hop, True).wait_recv()
            total = in_c[p, 0].astype(F32)
            for i in range(1, 4):
                total = total + in_c[p, i].astype(F32)
            got_b[p, at_axis(p, 1)] = total.astype(BF16)
            for hop in hops:
                spread_b(p, hop).start()
        for p in range(3):
            for hop in hops:
                spread_b(p, hop, True).wait_recv()

            @pl.loop(0, 4)
            def _(n):
                full[core * half + p * 16 + at_axis(p, 0) * 4 + n] = got_b[p, n]

            for hop in hops:
                spread_a(p, hop).start()
        for p in range(3):
            for hop in hops:
                spread_a(p, hop, True).wait_recv()
            final(p).start()
        for p in range(3):
            final(p, True).wait_recv()
        done = pltpu.make_async_copy(full, out_ref, out_sem)
        done.start()
        for p in range(3):
            pair(p).wait_send()
            final(p).wait_send()
            for hop in hops:
                scatter_a(p, hop).wait_send()
                scatter_b(p, hop).wait_send()
                swap_c(p, hop).wait_send()
                spread_b(p, hop).wait_send()
                spread_a(p, hop).wait_send()
        done.wait()

    bf = lambda *s: pltpu.VMEM(s + (block, width), BF16)
    dma = lambda *s: pltpu.SemaphoreType.DMA(s)
    out = pl.pallas_call(
        kernel,
        out_shape=jax.ShapeDtypeStruct((2 * half, block, width), BF16),
        in_specs=[pl.BlockSpec(memory_space=pltpu.VMEM)] * 4,
        out_specs=pl.BlockSpec(memory_space=pl.ANY),
        scratch_shapes=[
            pltpu.VMEM((half, block, width), F32),
            bf(half), bf(half), bf(half), bf(3, 3, 4), bf(3, 4), bf(3, 3), bf(3, 4), bf(3, 4), bf(2 * half),
            dma(3), dma(3), dma(5, 3, 3), dma(5, 3, 3), dma(3), dma(3), pltpu.SemaphoreType.DMA,
        ],
        compiler_params=pltpu.CompilerParams(
            collective_id=3, has_side_effects=True, vmem_limit_bytes=48 << 20
        ),
        name="reduce_weights",
    )(*grads)
    return out.reshape(4, rows, width)


def scatter_sum(source, target, used, outputs):
    count, rows, width = source.shape
    step = 8

    def kernel(target_ref, used_ref, source_ref, out_ref, acc):
        t = pl.program_id(0)

        @pl.when(t == 0)
        def _():
            acc[...] = jnp.zeros_like(acc)

        for j in range(step):
            @pl.when(used_ref[t * step + j] > 0)
            def _():
                m = target_ref[t * step + j]
                acc[m] = acc[m] + source_ref[j].astype(F32)

        @pl.when(t == pl.num_programs(0) - 1)
        def _():
            out_ref[...] = acc[...].astype(out_ref.dtype)

    return pl.pallas_call(
        kernel,
        out_shape=jax.ShapeDtypeStruct((outputs, rows, width), source.dtype),
        grid_spec=pltpu.PrefetchScalarGridSpec(
            num_scalar_prefetch=2,
            grid=(count // step,),
            in_specs=[pl.BlockSpec((step, rows, width), lambda t, *_: (t, 0, 0))],
            out_specs=pl.BlockSpec((outputs, rows, width), lambda t, *_: (0, 0, 0)),
            scratch_shapes=[pltpu.VMEM((outputs, rows, width), F32)],
        ),
        compiler_params=pltpu.CompilerParams(vmem_limit_bytes=48 << 20),
        name="scatter_sum",
    )(target, used, source)


def layer(position, live, arrived, tokens, grad_out, w_query, w_pair, w_out, slots):
    patches, block, width = tokens.shape
    requests = position.shape[0] // patches
    far = requests * block
    rows = block + far
    chunks = 4
    chunk = far // chunks
    pairs = width // 128
    parts = requests + 1

    def kernel(
        position_ref, live_ref, arrived_ref, tokens_ref, grad_ref, wq_ref, wkv_ref, wo_ref,
        attn_ref, tokgrad_ref, fargrad_ref, x_ref, dkv_ref, dq_ref, mixed_ref,
        key_s, val_s, q_s, up_s, s_s, dp_s, pb_s, ds_s, fg_s, in_sem, out_sem,
    ):
        p = pl.program_id(0)

        def fetch(r):
            return pltpu.make_async_copy(
                arrived_ref.at[position_ref[p * requests + r]],
                x_ref.at[0, pl.ds(block + r * block, block)],
                in_sem.at[r],
            )

        for r in range(requests):
            fetch(r).start()
        tok = tokens_ref[0]
        x_ref[0, 0:block] = tok
        q_s[...] = mm(tok, wq_ref[...]).astype(BF16)
        own = mm(tok, wkv_ref[...]).astype(BF16)
        key_s[0:block] = own[:, :width]
        val_s[0:block] = own[:, width:]
        up_s[...] = mm(grad_ref[0], wo_ref[...], NT).astype(BF16)
        for r in range(requests):
            fetch(r).wait()

        @pl.loop(0, chunks)
        def _(c):
            at = pl.multiple_of(block + c * chunk, 128)
            x = x_ref[0, pl.ds(at, chunk)]
            key_s[pl.ds(at, chunk)] = mm(x, wkv_ref[:, :width]).astype(BF16)
            val_s[pl.ds(at, chunk)] = mm(x, wkv_ref[:, width:]).astype(BF16)

        low = lax.broadcasted_iota(jnp.int32, (block, 128), 1) < HD
        zero = jnp.zeros((block, 128), BF16)

        @pl.loop(0, pairs)
        def _(j):
            lanes = pl.ds(pl.multiple_of(j * 128, 128), 128)
            k = key_s[:, lanes]
            v = val_s[:, lanes]
            q = q_s[:, lanes] * jnp.asarray(1.0 / math.sqrt(HD), BF16)
            u = up_s[:, lanes]
            q2 = jnp.concatenate([jnp.where(low, q, zero), jnp.where(low, zero, q)], axis=0)
            u2 = jnp.concatenate([jnp.where(low, u, zero), jnp.where(low, zero, u)], axis=0)
            s_s[...] = mm(k, q2, NT)
            dp_s[...] = mm(v, u2, NT)

            def bias(r):
                dead = live_ref[p * requests + jnp.maximum(r - 1, 0)] == 0
                return jnp.where((r > 0) & dead, -jnp.inf, 0.0).astype(F32)

            def part(r):
                return pl.ds(pl.multiple_of(r * block, block), block)

            def largest(r, m):
                s = s_s[part(r)] + bias(r)
                return jnp.maximum(m, jnp.max(s.reshape(block // 8, 8, 2 * block), axis=0))

            m = lax.fori_loop(0, parts, largest, jnp.full((8, 2 * block), -jnp.inf, F32))
            m = jnp.max(m, axis=0, keepdims=True)

            def exps(r, carry):
                total, delta = carry
                e = jnp.exp(s_s[part(r)] + bias(r) - m)
                s_s[part(r)] = e
                g = e * dp_s[part(r)]
                fold = lambda t: jnp.sum(t.reshape(block // 8, 8, 2 * block), axis=0)
                return total + fold(e), delta + fold(g)

            nil = jnp.zeros((8, 2 * block), F32)
            total, delta = lax.fori_loop(0, parts, exps, (nil, nil))
            inverse = 1.0 / jnp.sum(total, axis=0, keepdims=True)
            delta = jnp.sum(delta, axis=0, keepdims=True) * inverse

            @pl.loop(0, parts)
            def _(r):
                prob = s_s[part(r)] * inverse
                pb_s[part(r)] = prob.astype(BF16)
                ds_s[part(r)] = (prob * (dp_s[part(r)] - delta)).astype(BF16)

            pb = pb_s[...]
            ds = ds_s[...]
            dkv_ref[0, :, lanes] = mm(ds, q2).astype(BF16)
            dkv_ref[0, :, pl.ds(pl.multiple_of(width + j * 128, 128), 128)] = mm(pb, u2).astype(BF16)
            o = mm(pb, v, TN)
            mixed_ref[0, :, lanes] = jnp.where(low, o[:block], o[block:]).astype(BF16)
            dq = mm(ds, k, TN)
            dq = jnp.where(low, dq[:block], dq[block:]) * (1.0 / math.sqrt(HD))
            dq_ref[0, :, lanes] = dq.astype(BF16)

        attn_ref[0] = mm(mixed_ref[0], wo_ref[...]).astype(BF16)
        tokgrad_ref[0] = (
            mm(dq_ref[0], wq_ref[...], NT) + mm(dkv_ref[0, 0:block], wkv_ref[...], NT)
        ).astype(BF16)

        @pl.loop(0, chunks)
        def _(c):
            at = pl.multiple_of(block + c * chunk, 128)
            g = mm(dkv_ref[0, pl.ds(at, chunk)], wkv_ref[...], NT).astype(BF16)
            fg_s[pl.ds(pl.multiple_of(c * chunk, 128), chunk)] = g

        def put(r):
            return pltpu.make_async_copy(
                fg_s.at[pl.ds(r * block, block)],
                fargrad_ref.at[position_ref[p * requests + r]],
                out_sem.at[r],
            )

        for r in range(requests):
            put(r).start()
        for r in range(requests):
            put(r).wait()

    per_patch = lambda n, w: pl.BlockSpec((1, n, w), lambda p, *_: (p, 0, 0))
    whole = lambda a: pl.BlockSpec(a.shape, lambda p, *_: (0, 0), pipeline_mode=pl.Buffered(1))
    hbm = pl.BlockSpec(memory_space=pl.ANY)
    shape = lambda *s: jax.ShapeDtypeStruct(s, BF16)
    return pl.pallas_call(
        kernel,
        out_shape=(
            shape(patches, block, width),
            shape(patches, block, width),
            shape(slots, block, width),
            shape(patches, rows, width),
            shape(patches, rows, 2 * width),
            shape(patches, block, width),
            shape(patches, block, width),
        ),
        grid_spec=pltpu.PrefetchScalarGridSpec(
            num_scalar_prefetch=2,
            grid=(patches,),
            in_specs=[
                hbm, per_patch(block, width), per_patch(block, width),
                whole(w_query), whole(w_pair), whole(w_out),
            ],
            out_specs=(
                per_patch(block, width), per_patch(block, width), hbm, per_patch(rows, width),
                per_patch(rows, 2 * width), per_patch(block, width), per_patch(block, width),
            ),
            scratch_shapes=[
                pltpu.VMEM((rows, width), BF16),
                pltpu.VMEM((rows, width), BF16),
                pltpu.VMEM((block, width), BF16),
                pltpu.VMEM((block, width), BF16),
                pltpu.VMEM((rows, 2 * block), F32),
                pltpu.VMEM((rows, 2 * block), F32),
                pltpu.VMEM((rows, 2 * block), BF16),
                pltpu.VMEM((rows, 2 * block), BF16),
                pltpu.VMEM((far, width), BF16),
                pltpu.SemaphoreType.DMA((requests,)),
                pltpu.SemaphoreType.DMA((requests,)),
            ],
        ),
        compiler_params=pltpu.CompilerParams(vmem_limit_bytes=60 << 20),
        name="layer",
    )(position, live, arrived, tokens, grad_out, w_query, w_pair, w_out)


def outer_sum(left, right):
    return lax.dot_general(left, right, TN, preferred_element_type=F32)


def body(
    query_tokens, past_tokens, source_dev, source_slot, kept, w_query, w_key, w_value, w_out,
    grad_out,
):
    _, patches, block, width = query_tokens.shape
    tokens, grads, past = query_tokens[0], grad_out[0], past_tokens[0]
    peers = lax.axis_size("patch")
    y, x, z, _ = place()
    per_device = patches * source_dev.shape[1] * source_dev.shape[2]
    cap = 8

    grid = lambda a: a.reshape(4, 2, 4, per_device)
    near = lambda a: jnp.concatenate([grid(a)[y, x], grid(a)[:, x, z]], axis=0)
    owner, slot = near(source_dev), near(source_slot)
    from_y, half, from_z = owner // 8, (owner // 4) % 2, owner % 4
    key = half * 4 + jnp.where(half == 0, from_z, from_y)
    number = jnp.where(half == 0, from_y, from_z) * past.shape[0] + slot
    order = jnp.arange(per_device)
    matches = (key[:, :, None] == key[:, None, :]) & (order[:, None] > order[None, :])
    rank = jnp.sum(matches.astype(jnp.int32), axis=2)
    chosen_here = jnp.where(jnp.arange(8) < 4, z, 4 + y)
    hit = (rank[:, :, None] == jnp.arange(cap)) & (key == chosen_here[:, None])[:, :, None]
    table = jnp.sum(jnp.where(hit, number[:, :, None], 0), axis=1)
    used = jnp.sum(hit.astype(jnp.int32), axis=1).reshape(-1)
    target = (table + jnp.where(jnp.arange(8) < 4, 0, 4 * past.shape[0])[:, None]).reshape(-1)
    mine = key[z] * cap + rank[z]
    live = grid(kept)[y, x, z]

    arrived = spread(past, table.reshape(-1))
    w_pair = jnp.concatenate([w_key, w_value], axis=1)
    attn, token_grad, far_grad, seen, dkv, dq, mixed = layer(
        mine, live, arrived, tokens, grads, w_query, w_pair, w_out, 8 * cap
    )
    returned = send_back(far_grad)
    partial = scatter_sum(returned, target, used, 8 * past.shape[0])
    past_grad = collect(partial.reshape((8,) + past.shape))
    flat = lambda a: a.reshape(-1, a.shape[-1])
    scale = 1.0 / math.sqrt(lax.axis_size("dp") * peers * patches * block)
    dkv, seen = flat(dkv), flat(seen)
    grad_wk = outer_sum(seen, dkv[:, :width]) * scale
    grad_wv = outer_sum(seen, dkv[:, width:]) * scale
    grad_wq = outer_sum(flat(tokens), flat(dq)) * scale
    grad_wo = outer_sum(flat(mixed), flat(grads)) * scale
    weights = reduce_weights((grad_wq, grad_wk, grad_wv, grad_wo)).astype(F32)
    return (
        attn[None],
        token_grad[None],
        past_grad[None],
        weights[0],
        weights[1],
        weights[2],
        weights[3],
    )


def solution(mesh):
    split = P("dp", "patch", None, None)
    return jax.shard_map(
        body,
        mesh=mesh,
        in_specs=(split, split, P(), P(), P(), P(), P(), P(), P(), split),
        out_specs=(split, split, split, P(), P(), P(), P()),
        check_vma=False,
    )
```

```python
import math

import jax
import jax.numpy as jnp
from jax import lax
from jax.experimental import pallas as pl
from jax.experimental.pallas import tpu as pltpu
from jax.sharding import PartitionSpec as P

H = 12
HD = 64
F32 = jnp.float32
MESH = pl.DeviceIdType.MESH
BF16 = jnp.bfloat16
NN = (((1,), (0,)), ((), ()))
NT = (((1,), (1,)), ((), ()))
TN = (((0,), (0,)), ((), ()))


def mm(a, b, dims=NN):
    return lax.dot_general(a, b, dims, preferred_element_type=F32)


def place():
    device = lax.axis_index("patch")
    return device // 8, (device // 4) % 2, device % 4, lax.axis_index("dp")


def step_id(y, x, z, dim, hop):
    return ((y + hop * (1 - dim)) % 4) * 8 + x * 4 + (z + hop * dim) % 4


def meet(y, x, z, dp, across):
    barrier = pltpu.get_barrier_semaphore()
    ids = [step_id(y, x, z, dim, hop) for dim in (0, 1) for hop in (1, 2, 3)]
    if across:
        ids.append(y * 8 + (1 - x) * 4 + z)
    for other in ids:
        pl.semaphore_signal(barrier, 1, device_id=(dp, other), device_id_type=MESH)
    pl.semaphore_wait(barrier, len(ids))


def spread(past, table):
    blocks, rows, width = past.shape
    parts = 4
    chunk = blocks // parts
    cap = 8

    def kernel(
        table_ref, past_ref, out_ref, have_a, have_b, sel_a, sel_b,
        in_sem, x_send, x_recv, g_send, g_recv, e_send, e_recv, own_sem,
    ):
        y, x, z, dp = place()
        pos = lambda dim, hop=0: (y * (1 - dim) + z * dim + hop) % 4
        have, sel = (have_a, have_b), (sel_a, sel_b)
        half = (x, 1 - x)

        def region(t, hop, c):
            return have[t].at[pl.ds(pos(half[t], hop) * blocks + c * chunk, chunk)]

        local = pltpu.make_async_copy(
            past_ref, have_a.at[pl.ds(pos(half[0]) * blocks, blocks)], in_sem
        )
        local.start()
        meet(y, x, z, dp, True)

        def cross(c):
            at = pl.ds(pos(half[0]) * blocks + c * chunk, chunk)
            return pltpu.make_async_remote_copy(
                past_ref.at[pl.ds(c * chunk, chunk)], have_b.at[at], x_send.at[c], x_recv.at[c],
                device_id=(dp, y * 8 + (1 - x) * 4 + z), device_id_type=MESH,
            )

        def crossed(c):
            at = pl.ds(pos(half[1]) * blocks + c * chunk, chunk)
            return pltpu.make_async_remote_copy(
                past_ref.at[pl.ds(c * chunk, chunk)], have_b.at[at], x_send.at[c], x_recv.at[c],
                device_id=(dp, y * 8 + (1 - x) * 4 + z), device_id_type=MESH,
            )

        turn = (0, 2, 1, 3)
        ways = [(way, 0, c) for c in turn for way in ((1, 3) if c < 2 else (3, 1))]
        ways += [(1, 3, c) if c < 2 else (3, 1, c) for c in turn]

        def go(t, n):
            way, owner, c = ways[n]
            return pltpu.make_async_remote_copy(
                region(t, owner, c), region(t, owner, c), g_send.at[t, n], g_recv.at[t, n],
                device_id=(dp, step_id(y, x, z, half[t], way)), device_id_type=MESH,
            )

        def came(t, n):
            way, owner, c = ways[n]
            owner = (owner - way) % 4
            return pltpu.make_async_remote_copy(
                region(t, owner, c), region(t, owner, c), g_send.at[t, n], g_recv.at[t, n],
                device_id=(dp, step_id(y, x, z, half[t], way)), device_id_type=MESH,
            )

        def swap(t, hop, arriving=False):
            h = half[t]
            at = h * 4 + pos(1 - h, -hop if arriving else 0)
            return pltpu.make_async_remote_copy(
                sel[t].at[hop], out_ref.at[pl.ds(at * cap, cap)],
                e_send.at[t, hop - 1], e_recv.at[t, hop - 1],
                device_id=(dp, step_id(y, x, z, 1 - h, hop)), device_id_type=MESH,
            )

        def keep(t):
            h = half[t]
            at = h * 4 + pos(1 - h)
            return pltpu.make_async_copy(
                sel[t].at[0], out_ref.at[pl.ds(at * cap, cap)], own_sem.at[t]
            )

        def choose(t):
            h = half[t]
            for hop in (2, 1, 3, 0):
                row = h * 4 + pos(1 - h, hop)

                @pl.loop(0, cap)
                def _(s):
                    sel[t][hop, s] = have[t][table_ref[row * cap + s]]

                if hop:
                    swap(t, hop).start()
                else:
                    keep(t).start()

        for c in turn:
            cross(c).start()
        local.wait()
        for n in range(2 * parts):
            go(0, n).start()

        def relay(t, i):
            came(t, 2 * i).wait_recv()
            go(t, 2 * parts + i).start()

        for i in range(parts):
            crossed(turn[i]).wait_recv()
            go(1, 2 * i).start()
            go(1, 2 * i + 1).start()
            relay(0, i)
        for i in range(parts):
            relay(1, i)
        for t in (0, 1):
            for n in range(2 * parts):
                if n % 2:
                    came(t, n).wait_recv()
            for n in range(2 * parts, 3 * parts):
                came(t, n).wait_recv()
        choose(0)
        choose(1)
        for t in (0, 1):
            for hop in (1, 2, 3):
                swap(t, hop, True).wait_recv()
            keep(t).wait()
        for c in turn:
            cross(c).wait_send()
        for t in (0, 1):
            for n in range(3 * parts):
                go(t, n).wait_send()
            for hop in (1, 2, 3):
                swap(t, hop).wait_send()

    return pl.pallas_call(
        kernel,
        out_shape=jax.ShapeDtypeStruct((8 * cap, rows, width), past.dtype),
        in_specs=[pl.BlockSpec(memory_space=pltpu.SMEM), pl.BlockSpec(memory_space=pl.ANY)],
        out_specs=pl.BlockSpec(memory_space=pl.ANY),
        scratch_shapes=[
            pltpu.VMEM((4 * blocks, rows, width), past.dtype),
            pltpu.VMEM((4 * blocks, rows, width), past.dtype),
            pltpu.VMEM((4, cap, rows, width), past.dtype),
            pltpu.VMEM((4, cap, rows, width), past.dtype),
            pltpu.SemaphoreType.DMA,
            pltpu.SemaphoreType.DMA((parts,)),
            pltpu.SemaphoreType.DMA((parts,)),
            pltpu.SemaphoreType.DMA((2, 3 * parts)),
            pltpu.SemaphoreType.DMA((2, 3 * parts)),
            pltpu.SemaphoreType.DMA((2, 3)),
            pltpu.SemaphoreType.DMA((2, 3)),
            pltpu.SemaphoreType.DMA((2,)),
        ],
        compiler_params=pltpu.CompilerParams(
            collective_id=0, has_side_effects=True, vmem_limit_bytes=48 << 20
        ),
        name="spread",
    )(table, past)


def send_back(grads, tokens, grad_out, seen, dkv, dq, mixed):
    slots, rows, width = grads.shape
    cap = slots // 8
    total = seen.shape[0]
    chunk = total // 8

    def kernel(
        grad_ref, tok_ref, gout_ref, seen_ref, dkv_ref, dq_ref, mixed_ref,
        out_ref, wq_ref, wk_ref, wv_ref, wo_ref, own, send, recv, own_sem,
    ):
        y, x, z, dp = place()
        pos = lambda dim, hop=0: (y * (1 - dim) + z * dim + hop) % 4
        part = lambda ref, at: ref.at[pl.ds(at * cap, cap)]

        def swap(h, hop, arriving=False):
            return pltpu.make_async_remote_copy(
                part(grad_ref, h * 4 + pos(1 - h, hop)),
                part(out_ref, h * 4 + pos(1 - h, -hop if arriving else 0)),
                send.at[h, hop - 1], recv.at[h, hop - 1],
                device_id=(dp, step_id(y, x, z, 1 - h, hop)), device_id_type=MESH,
            )

        def load(h):
            return pltpu.make_async_copy(
                part(grad_ref, h * 4 + pos(1 - h)), own.at[h], own_sem.at[h]
            )

        def store(h):
            return pltpu.make_async_copy(
                own.at[h], part(out_ref, h * 4 + pos(1 - h)), own_sem.at[h]
            )

        for h in (0, 1):
            load(h).start()
        meet(y, x, z, dp, False)
        for hop in (2, 1, 3):
            for h in (0, 1):
                swap(h, hop).start()
        for h in (0, 1):
            load(h).wait()
            store(h).start()
        wq_ref[...] = mm(tok_ref[...], dq_ref[...], TN)
        wo_ref[...] = mm(mixed_ref[...], gout_ref[...], TN)
        wk_ref[...] = jnp.zeros_like(wk_ref)
        wv_ref[...] = jnp.zeros_like(wv_ref)

        @pl.loop(0, total // chunk)
        def _(n):
            at = pl.ds(pl.multiple_of(n * chunk, 16), chunk)
            left = seen_ref[at]
            wk_ref[...] += mm(left, dkv_ref[at, :width], TN)
            wv_ref[...] += mm(left, dkv_ref[at, width:], TN)

        for h in (0, 1):
            store(h).wait()
            for hop in (1, 2, 3):
                swap(h, hop, True).wait_recv()
        for h in (0, 1):
            for hop in (1, 2, 3):
                swap(h, hop).wait_send()

    return pl.pallas_call(
        kernel,
        out_shape=(jax.ShapeDtypeStruct(grads.shape, grads.dtype),)
        + (jax.ShapeDtypeStruct((width, width), F32),) * 4,
        in_specs=[pl.BlockSpec(memory_space=pl.ANY)] + [pl.BlockSpec(memory_space=pltpu.VMEM)] * 6,
        out_specs=(pl.BlockSpec(memory_space=pl.ANY),) + (pl.BlockSpec(memory_space=pltpu.VMEM),) * 4,
        scratch_shapes=[
            pltpu.VMEM((2, cap, rows, width), grads.dtype),
            pltpu.SemaphoreType.DMA((2, 3)),
            pltpu.SemaphoreType.DMA((2, 3)),
            pltpu.SemaphoreType.DMA((2,)),
        ],
        compiler_params=pltpu.CompilerParams(
            collective_id=1, has_side_effects=True, vmem_limit_bytes=56 << 20
        ),
        name="send_back",
    )(grads, tokens, grad_out, seen, dkv, dq, mixed)


def collect(partial, grads, scale):
    groups, blocks, rows, width = partial.shape
    chunk = blocks // 2
    w_rows = grads[0].shape[0]
    block = w_rows // 24
    half_w = 48

    def collect_steps(
        part_ref, out_ref, relay, staged, inward, mine, across,
        r_send, r_recv, d_send, d_recv, x_send, x_recv,
    ):
        y, x, z, dp = place()
        pos = lambda dim, hop=0: (y * (1 - dim) + z * dim + hop) % 4
        half = (1 - x, x)
        ways = (3, 1)

        def row(t, hop):
            return half[t] * 4 + pos(half[t], hop)

        def pass_on(t, side):
            return pltpu.make_async_remote_copy(
                part_ref.at[row(t, 2), pl.ds(side * chunk, chunk)], relay.at[t, side],
                r_send.at[t, side], r_recv.at[t, side],
                device_id=(dp, step_id(y, x, z, half[t], ways[side])), device_id_type=MESH,
            )

        def direct(t, side, summed):
            c = side if summed else 1 - side
            source = (
                staged.at[t, side] if summed
                else part_ref.at[row(t, ways[side]), pl.ds(c * chunk, chunk)]
            )
            return pltpu.make_async_remote_copy(
                source, inward.at[t, side, pl.ds(c * chunk, chunk)],
                d_send.at[t, side, int(summed)], d_recv.at[t, side, int(summed)],
                device_id=(dp, step_id(y, x, z, half[t], ways[side])), device_id_type=MESH,
            )

        def cross(c):
            return pltpu.make_async_remote_copy(
                mine.at[pl.ds(c * chunk, chunk)], across.at[pl.ds(c * chunk, chunk)],
                x_send.at[c], x_recv.at[c],
                device_id=(dp, y * 8 + (1 - x) * 4 + z), device_id_type=MESH,
            )

        def final(t, b):
            return (
                part_ref[row(t, 0), b].astype(F32)
                + inward[t, 0, b].astype(F32)
                + inward[t, 1, b].astype(F32)
            )

        for t in (0, 1):
            for side in (0, 1):
                pass_on(t, side).start()
        for t in (0, 1):
            for side in (0, 1):
                direct(t, side, False).start()
        yield
        for t in (0, 1):
            for side in (0, 1):
                pass_on(t, side).wait_recv()

                @pl.loop(0, chunk)
                def _(b):
                    own = part_ref[row(t, ways[side]), side * chunk + b]
                    staged[t, side, b] = (
                        own.astype(F32) + relay[t, side, b].astype(F32)
                    ).astype(staged.dtype)

                direct(t, side, True).start()
        yield
        for side in (0, 1):
            for summed in (False, True):
                direct(0, side, summed).wait_recv()
        for c in (0, 1):
            @pl.loop(0, chunk)
            def _(b):
                mine[c * chunk + b] = final(0, c * chunk + b).astype(mine.dtype)

            cross(c).start()
        yield
        for side in (0, 1):
            for summed in (False, True):
                direct(1, side, summed).wait_recv()
        for c in (0, 1):
            cross(c).wait_recv()

            @pl.loop(0, chunk)
            def _(b):
                at = c * chunk + b
                out_ref[at] = (final(1, at) + across[at].astype(F32)).astype(out_ref.dtype)

        yield
        for t in (0, 1):
            cross(t).wait_send()
            for side in (0, 1):
                pass_on(t, side).wait_send()
                for summed in (False, True):
                    direct(t, side, summed).wait_send()

    def reduce_steps(
        a_ref, b_ref, c_ref, d_ref, out_ref, acc, stage, peer, mid, in_a, mid_b, in_b, in_c, got_b, full,
        core_send, core_recv, send, recv, back_send, back_recv, out_sem,
    ):
        y, x_low, z, dp = place()
        core = dp % 2
        spot = {"x": (dp // 2) * 2 + x_low, "y": y, "z": z}
        orders = ("xyz", "yzx", "zxy")

        def there(axis, hop):
            at = dict(spot)
            at[axis] = (at[axis] + hop) % 4
            return (
                (at["x"] // 2) * 2 + core,
                at["y"] * 8 + (at["x"] % 2) * 4 + at["z"],
            )

        other = (dp + 1 - 2 * core, y * 8 + x_low * 4 + z)
        barrier = pltpu.get_barrier_semaphore()
        for axis in "xyz":
            for hop in (1, 2, 3):
                pl.semaphore_signal(barrier, 1, device_id=there(axis, hop), device_id_type=MESH)
        pl.semaphore_signal(barrier, 1, device_id=other, device_id_type=MESH)
        pl.semaphore_wait(barrier, 10)
        yield

        def take(keep, give):
            for i in (0, 1):
                @pl.loop(0, half_w // 2)
                def _(n):
                    at = pl.ds(pl.multiple_of(n * block, block), block)
                    stage[i * (half_w // 2) + n] = (give[i][at] * scale).astype(BF16)
                    acc[i * (half_w // 2) + n] = keep[i][at] * scale

        @pl.when(core == 0)
        def _():
            take((a_ref, b_ref), (c_ref, d_ref))

        @pl.when(core == 1)
        def _():
            take((c_ref, d_ref), (a_ref, b_ref))

        def pair(p):
            at = pl.ds(p * 16, 16)
            return pltpu.make_async_remote_copy(
                stage.at[at], peer.at[at], core_send.at[p], core_recv.at[p],
                device_id=other, device_id_type=MESH,
            )

        def copy(source, target, phase, p, hop, sems=None):
            s, r = sems or (send, recv)
            return pltpu.make_async_remote_copy(
                source, target, s.at[phase, p, hop - 1], r.at[phase, p, hop - 1],
                device_id=there(orders[p][(0, 1, 2, 1, 0)[phase]], hop), device_id_type=MESH,
            )

        def at_axis(p, phase, hop=0):
            return (spot[orders[p][phase]] + hop) % 4

        def scatter_a(p, hop):
            at = pl.ds(p * 16 + at_axis(p, 0, hop) * 4, 4)
            return copy(mid.at[at], in_a.at[p, hop - 1], 0, p, hop)

        def scatter_b(p, hop):
            return copy(mid_b.at[p, at_axis(p, 1, hop)], in_b.at[p, hop - 1], 1, p, hop)

        def swap_c(p, hop, arriving=False):
            to = at_axis(p, 2, -hop if arriving else 0)
            return copy(in_c.at[p, at_axis(p, 2)], in_c.at[p, to], 2, p, hop)

        def spread_b(p, hop, arriving=False):
            to = at_axis(p, 1, -hop if arriving else 0)
            return copy(got_b.at[p, at_axis(p, 1)], got_b.at[p, to], 3, p, hop)

        def spread_a(p, hop, arriving=False):
            row = lambda back: pl.ds(core * half_w + p * 16 + at_axis(p, 0, back) * 4, 4)
            return copy(
                full.at[row(0)], full.at[row(-hop if arriving else 0)], 4, p, hop
            )

        def final(p, arriving=False):
            side = 1 - core if arriving else core
            at = pl.ds(side * half_w + p * 16, 16)
            return pltpu.make_async_remote_copy(
                full.at[at], full.at[at], back_send.at[p], back_recv.at[p],
                device_id=other, device_id_type=MESH,
            )

        hops = (2, 1, 3)
        for p in range(3):
            pair(p).start()
        yield
        for p in range(3):
            pair(p).wait_recv()

            @pl.loop(0, 16)
            def _(n):
                total = acc[p * 16 + n] + peer[p * 16 + n].astype(F32)
                acc[p * 16 + n] = total
                mid[p * 16 + n] = total.astype(BF16)

            for hop in hops:
                scatter_a(p, hop).start()
        yield
        for p in range(3):
            for hop in hops:
                scatter_a(p, hop).wait_recv()

            @pl.loop(0, 4)
            def _(n):
                at = p * 16 + at_axis(p, 0) * 4 + n
                total = acc[at]
                for i in range(3):
                    total = total + in_a[p, i, n].astype(F32)
                acc[at] = total
                mid_b[p, n] = total.astype(BF16)

            for hop in hops:
                scatter_b(p, hop).start()
        yield
        for p in range(3):
            for hop in hops:
                scatter_b(p, hop).wait_recv()
            total = acc[p * 16 + at_axis(p, 0) * 4 + at_axis(p, 1)]
            for i in range(3):
                total = total + in_b[p, i].astype(F32)
            in_c[p, at_axis(p, 2)] = total.astype(BF16)
            for hop in hops:
                swap_c(p, hop).start()
        yield
        for p in range(3):
            for hop in hops:
                swap_c(p, hop, True).wait_recv()
            total = in_c[p, 0].astype(F32)
            for i in range(1, 4):
                total = total + in_c[p, i].astype(F32)
            got_b[p, at_axis(p, 1)] = total.astype(BF16)
            for hop in hops:
                spread_b(p, hop).start()
        yield
        for p in range(3):
            for hop in hops:
                spread_b(p, hop, True).wait_recv()

            @pl.loop(0, 4)
            def _(n):
                full[core * half_w + p * 16 + at_axis(p, 0) * 4 + n] = got_b[p, n]

            for hop in hops:
                spread_a(p, hop).start()
        yield
        for p in range(3):
            for hop in hops:
                spread_a(p, hop, True).wait_recv()
            final(p).start()
        yield
        for p in range(3):
            final(p, True).wait_recv()
        done = pltpu.make_async_copy(full, out_ref, out_sem)
        done.start()
        yield
        for p in range(3):
            pair(p).wait_send()
            final(p).wait_send()
            for hop in hops:
                scatter_a(p, hop).wait_send()
                scatter_b(p, hop).wait_send()
                swap_c(p, hop).wait_send()
                spread_b(p, hop).wait_send()
                spread_a(p, hop).wait_send()
        done.wait()

    def kernel(part_ref, a, b, c, d, out_ref, weights_ref, *scratch):
        weights = reduce_steps(a, b, c, d, weights_ref, *scratch[11:])
        blocks_back = collect_steps(part_ref, out_ref, *scratch[:11])
        for step in "wbwwbwwbwwwbwbw":
            next(weights if step == "w" else blocks_back, None)

    shape = lambda *s: pltpu.VMEM(s + (rows, width), partial.dtype)
    bf = lambda *s: pltpu.VMEM(s + (block, width), BF16)
    dma = lambda *s: pltpu.SemaphoreType.DMA(s)
    vmem = pl.BlockSpec(memory_space=pltpu.VMEM)
    past_grad, weights = pl.pallas_call(
        kernel,
        out_shape=(
            jax.ShapeDtypeStruct((blocks, rows, width), partial.dtype),
            jax.ShapeDtypeStruct((2 * half_w, block, width), BF16),
        ),
        in_specs=[vmem] * 5,
        out_specs=(vmem, pl.BlockSpec(memory_space=pl.ANY)),
        scratch_shapes=[
            shape(2, 2, chunk), shape(2, 2, chunk), shape(2, 2, blocks), shape(blocks), shape(blocks),
            dma(2, 2), dma(2, 2), dma(2, 2, 2), dma(2, 2, 2), dma(2), dma(2),
            pltpu.VMEM((half_w, block, width), F32),
            bf(half_w), bf(half_w), bf(half_w), bf(3, 3, 4), bf(3, 4), bf(3, 3), bf(3, 4), bf(3, 4),
            bf(2 * half_w),
            dma(3), dma(3), dma(5, 3, 3), dma(5, 3, 3), dma(3), dma(3), pltpu.SemaphoreType.DMA,
        ],
        compiler_params=pltpu.CompilerParams(
            collective_id=2, has_side_effects=True, vmem_limit_bytes=62 << 20
        ),
        name="collect",
    )(partial, *grads)
    return past_grad, weights.reshape(4, w_rows, width)


def scatter_sum(source, target, used, outputs):
    count, rows, width = source.shape
    step = 8

    def kernel(target_ref, used_ref, source_ref, out_ref, acc):
        t = pl.program_id(0)

        @pl.when(t == 0)
        def _():
            acc[...] = jnp.zeros_like(acc)

        for j in range(step):
            @pl.when(used_ref[t * step + j] > 0)
            def _():
                m = target_ref[t * step + j]
                acc[m] = acc[m] + source_ref[j].astype(F32)

        @pl.when(t == pl.num_programs(0) - 1)
        def _():
            out_ref[...] = acc[...].astype(out_ref.dtype)

    return pl.pallas_call(
        kernel,
        out_shape=jax.ShapeDtypeStruct((outputs, rows, width), source.dtype),
        grid_spec=pltpu.PrefetchScalarGridSpec(
            num_scalar_prefetch=2,
            grid=(count // step,),
            in_specs=[pl.BlockSpec((step, rows, width), lambda t, *_: (t, 0, 0))],
            out_specs=pl.BlockSpec((outputs, rows, width), lambda t, *_: (0, 0, 0)),
            scratch_shapes=[pltpu.VMEM((outputs, rows, width), F32)],
        ),
        compiler_params=pltpu.CompilerParams(vmem_limit_bytes=48 << 20),
        name="scatter_sum",
    )(target, used, source)


def layer(position, live, arrived, tokens, grad_out, w_query, w_pair, w_out, slots):
    patches, block, width = tokens.shape
    requests = position.shape[0] // patches
    far = requests * block
    rows = block + far
    chunks = 4
    chunk = far // chunks
    pairs = width // 128
    parts = requests + 1

    def kernel(
        position_ref, live_ref, arrived_ref, tokens_ref, grad_ref, wq_ref, wkv_ref, wo_ref,
        attn_ref, tokgrad_ref, fargrad_ref, x_ref, dkv_ref, dq_ref, mixed_ref,
        key_s, val_s, q_s, up_s, s_s, dp_s, pb_s, ds_s, fg_s, in_sem, out_sem,
    ):
        p = pl.program_id(0)

        def fetch(r):
            return pltpu.make_async_copy(
                arrived_ref.at[position_ref[p * requests + r]],
                x_ref.at[0, pl.ds(block + r * block, block)],
                in_sem.at[r],
            )

        for r in range(requests):
            fetch(r).start()
        tok = tokens_ref[0]
        x_ref[0, 0:block] = tok
        q_s[...] = mm(tok, wq_ref[...]).astype(BF16)
        own = mm(tok, wkv_ref[...]).astype(BF16)
        key_s[0:block] = own[:, :width]
        val_s[0:block] = own[:, width:]
        up_s[...] = mm(grad_ref[0], wo_ref[...], NT).astype(BF16)
        for r in range(requests):
            fetch(r).wait()

        @pl.loop(0, chunks)
        def _(c):
            at = pl.multiple_of(block + c * chunk, 128)
            x = x_ref[0, pl.ds(at, chunk)]
            key_s[pl.ds(at, chunk)] = mm(x, wkv_ref[:, :width]).astype(BF16)
            val_s[pl.ds(at, chunk)] = mm(x, wkv_ref[:, width:]).astype(BF16)

        low = lax.broadcasted_iota(jnp.int32, (block, 128), 1) < HD
        zero = jnp.zeros((block, 128), BF16)

        @pl.loop(0, pairs)
        def _(j):
            lanes = pl.ds(pl.multiple_of(j * 128, 128), 128)
            k = key_s[:, lanes]
            v = val_s[:, lanes]
            q = q_s[:, lanes] * jnp.asarray(1.0 / math.sqrt(HD), BF16)
            u = up_s[:, lanes]
            q2 = jnp.concatenate([jnp.where(low, q, zero), jnp.where(low, zero, q)], axis=0)
            u2 = jnp.concatenate([jnp.where(low, u, zero), jnp.where(low, zero, u)], axis=0)
            s_s[...] = mm(k, q2, NT)
            dp_s[...] = mm(v, u2, NT)

            def bias(r):
                dead = live_ref[p * requests + jnp.maximum(r - 1, 0)] == 0
                return jnp.where((r > 0) & dead, -jnp.inf, 0.0).astype(F32)

            def part(r):
                return pl.ds(pl.multiple_of(r * block, block), block)

            def largest(r, m):
                s = s_s[part(r)] + bias(r)
                return jnp.maximum(m, jnp.max(s.reshape(block // 8, 8, 2 * block), axis=0))

            m = lax.fori_loop(0, parts, largest, jnp.full((8, 2 * block), -jnp.inf, F32))
            m = jnp.max(m, axis=0, keepdims=True)

            def exps(r, carry):
                total, delta = carry
                e = jnp.exp(s_s[part(r)] + bias(r) - m)
                s_s[part(r)] = e
                g = e * dp_s[part(r)]
                fold = lambda t: jnp.sum(t.reshape(block // 8, 8, 2 * block), axis=0)
                return total + fold(e), delta + fold(g)

            nil = jnp.zeros((8, 2 * block), F32)
            total, delta = lax.fori_loop(0, parts, exps, (nil, nil))
            inverse = 1.0 / jnp.sum(total, axis=0, keepdims=True)
            delta = jnp.sum(delta, axis=0, keepdims=True) * inverse

            @pl.loop(0, parts)
            def _(r):
                prob = s_s[part(r)] * inverse
                pb_s[part(r)] = prob.astype(BF16)
                ds_s[part(r)] = (prob * (dp_s[part(r)] - delta)).astype(BF16)

            pb = pb_s[...]
            ds = ds_s[...]
            dkv_ref[0, :, lanes] = mm(ds, q2).astype(BF16)
            dkv_ref[0, :, pl.ds(pl.multiple_of(width + j * 128, 128), 128)] = mm(pb, u2).astype(BF16)
            o = mm(pb, v, TN)
            mixed_ref[0, :, lanes] = jnp.where(low, o[:block], o[block:]).astype(BF16)
            dq = mm(ds, k, TN)
            dq = jnp.where(low, dq[:block], dq[block:]) * (1.0 / math.sqrt(HD))
            dq_ref[0, :, lanes] = dq.astype(BF16)

        attn_ref[0] = mm(mixed_ref[0], wo_ref[...]).astype(BF16)
        tokgrad_ref[0] = (
            mm(dq_ref[0], wq_ref[...], NT) + mm(dkv_ref[0, 0:block], wkv_ref[...], NT)
        ).astype(BF16)

        @pl.loop(0, chunks)
        def _(c):
            at = pl.multiple_of(block + c * chunk, 128)
            g = mm(dkv_ref[0, pl.ds(at, chunk)], wkv_ref[...], NT).astype(BF16)
            fg_s[pl.ds(pl.multiple_of(c * chunk, 128), chunk)] = g

        def put(r):
            return pltpu.make_async_copy(
                fg_s.at[pl.ds(r * block, block)],
                fargrad_ref.at[position_ref[p * requests + r]],
                out_sem.at[r],
            )

        for r in range(requests):
            put(r).start()
        for r in range(requests):
            put(r).wait()

    per_patch = lambda n, w: pl.BlockSpec((1, n, w), lambda p, *_: (p, 0, 0))
    whole = lambda a: pl.BlockSpec(a.shape, lambda p, *_: (0, 0), pipeline_mode=pl.Buffered(1))
    hbm = pl.BlockSpec(memory_space=pl.ANY)
    shape = lambda *s: jax.ShapeDtypeStruct(s, BF16)
    return pl.pallas_call(
        kernel,
        out_shape=(
            shape(patches, block, width),
            shape(patches, block, width),
            shape(slots, block, width),
            shape(patches, rows, width),
            shape(patches, rows, 2 * width),
            shape(patches, block, width),
            shape(patches, block, width),
        ),
        grid_spec=pltpu.PrefetchScalarGridSpec(
            num_scalar_prefetch=2,
            grid=(patches,),
            in_specs=[
                hbm, per_patch(block, width), per_patch(block, width),
                whole(w_query), whole(w_pair), whole(w_out),
            ],
            out_specs=(
                per_patch(block, width), per_patch(block, width), hbm, per_patch(rows, width),
                per_patch(rows, 2 * width), per_patch(block, width), per_patch(block, width),
            ),
            scratch_shapes=[
                pltpu.VMEM((rows, width), BF16),
                pltpu.VMEM((rows, width), BF16),
                pltpu.VMEM((block, width), BF16),
                pltpu.VMEM((block, width), BF16),
                pltpu.VMEM((rows, 2 * block), F32),
                pltpu.VMEM((rows, 2 * block), F32),
                pltpu.VMEM((rows, 2 * block), BF16),
                pltpu.VMEM((rows, 2 * block), BF16),
                pltpu.VMEM((far, width), BF16),
                pltpu.SemaphoreType.DMA((requests,)),
                pltpu.SemaphoreType.DMA((requests,)),
            ],
        ),
        compiler_params=pltpu.CompilerParams(vmem_limit_bytes=60 << 20),
        name="layer",
    )(position, live, arrived, tokens, grad_out, w_query, w_pair, w_out)


def body(
    query_tokens, past_tokens, source_dev, source_slot, kept, w_query, w_key, w_value, w_out,
    grad_out,
):
    _, patches, block, width = query_tokens.shape
    tokens, grads, past = query_tokens[0], grad_out[0], past_tokens[0]
    peers = lax.axis_size("patch")
    y, x, z, _ = place()
    per_device = patches * source_dev.shape[1] * source_dev.shape[2]
    cap = 8

    grid = lambda a: a.reshape(4, 2, 4, per_device)
    near = lambda a: jnp.concatenate([grid(a)[y, x], grid(a)[:, x, z]], axis=0)
    owner, slot = near(source_dev), near(source_slot)
    from_y, half, from_z = owner // 8, (owner // 4) % 2, owner % 4
    key = half * 4 + jnp.where(half == 0, from_z, from_y)
    number = jnp.where(half == 0, from_y, from_z) * past.shape[0] + slot
    order = jnp.arange(per_device)
    matches = (key[:, :, None] == key[:, None, :]) & (order[:, None] > order[None, :])
    rank = jnp.sum(matches.astype(jnp.int32), axis=2)
    chosen_here = jnp.where(jnp.arange(8) < 4, z, 4 + y)
    hit = (rank[:, :, None] == jnp.arange(cap)) & (key == chosen_here[:, None])[:, :, None]
    table = jnp.sum(jnp.where(hit, number[:, :, None], 0), axis=1)
    used = jnp.sum(hit.astype(jnp.int32), axis=1).reshape(-1)
    target = (table + jnp.where(jnp.arange(8) < 4, 0, 4 * past.shape[0])[:, None]).reshape(-1)
    mine = key[z] * cap + rank[z]
    live = grid(kept)[y, x, z]

    arrived = spread(past, table.reshape(-1))
    w_pair = jnp.concatenate([w_key, w_value], axis=1)
    attn, token_grad, far_grad, seen, dkv, dq, mixed = layer(
        mine, live, arrived, tokens, grads, w_query, w_pair, w_out, 8 * cap
    )
    flat = lambda a: a.reshape(-1, a.shape[-1])
    returned, *weight_grads = send_back(
        far_grad, flat(tokens), flat(grads), flat(seen), flat(dkv), flat(dq), flat(mixed)
    )
    partial = scatter_sum(returned, target, used, 8 * past.shape[0])
    scale = 1.0 / math.sqrt(lax.axis_size("dp") * peers * patches * block)
    past_grad, weights = collect(partial.reshape((8,) + past.shape), weight_grads, scale)
    weights = weights.astype(F32)
    return (
        attn[None],
        token_grad[None],
        past_grad[None],
        weights[0],
        weights[1],
        weights[2],
        weights[3],
    )


def solution(mesh):
    split = P("dp", "patch", None, None)
    return jax.shard_map(
        body,
        mesh=mesh,
        in_specs=(split, split, P(), P(), P(), P(), P(), P(), P(), split),
        out_specs=(split, split, split, P(), P(), P(), P()),
        check_vma=False,
    )
```

```python
import math

import jax
import jax.numpy as jnp
from jax import lax
from jax.experimental import pallas as pl
from jax.experimental.pallas import tpu as pltpu
from jax.sharding import PartitionSpec as P

H = 12
HD = 64
F32 = jnp.float32
MESH = pl.DeviceIdType.MESH
BF16 = jnp.bfloat16
NN = (((1,), (0,)), ((), ()))
NT = (((1,), (1,)), ((), ()))
TN = (((0,), (0,)), ((), ()))


def mm(a, b, dims=NN):
    return lax.dot_general(a, b, dims, preferred_element_type=F32)


def place():
    device = lax.axis_index("patch")
    return device // 8, (device // 4) % 2, device % 4, lax.axis_index("dp")


def step_id(y, x, z, dim, hop):
    return ((y + hop * (1 - dim)) % 4) * 8 + x * 4 + (z + hop * dim) % 4


def meet(y, x, z, dp, across):
    barrier = pltpu.get_barrier_semaphore()
    ids = [step_id(y, x, z, dim, hop) for dim in (0, 1) for hop in (1, 2, 3)]
    if across:
        ids.append(y * 8 + (1 - x) * 4 + z)
    for other in ids:
        pl.semaphore_signal(barrier, 1, device_id=(dp, other), device_id_type=MESH)
    pl.semaphore_wait(barrier, len(ids))


def spread(past, table, ident):
    blocks, rows, width = past.shape
    parts = 4
    chunk = blocks // parts
    cap = table.shape[0] // 8

    def kernel(
        table_ref, past_ref, out_ref, have_a, have_b, sel_a, sel_b,
        in_sem, x_send, x_recv, g_send, g_recv, e_send, e_recv, own_sem,
    ):
        y, x, z, dp = place()
        pos = lambda dim, hop=0: (y * (1 - dim) + z * dim + hop) % 4
        have, sel = (have_a, have_b), (sel_a, sel_b)
        half = (x, 1 - x)

        def region(t, hop, c):
            return have[t].at[pl.ds(pos(half[t], hop) * blocks + c * chunk, chunk)]

        local = pltpu.make_async_copy(
            past_ref, have_a.at[pl.ds(pos(half[0]) * blocks, blocks)], in_sem
        )
        local.start()
        meet(y, x, z, dp, True)

        def cross(c):
            at = pl.ds(pos(half[0]) * blocks + c * chunk, chunk)
            return pltpu.make_async_remote_copy(
                past_ref.at[pl.ds(c * chunk, chunk)], have_b.at[at], x_send.at[c], x_recv.at[c],
                device_id=(dp, y * 8 + (1 - x) * 4 + z), device_id_type=MESH,
            )

        def crossed(c):
            at = pl.ds(pos(half[1]) * blocks + c * chunk, chunk)
            return pltpu.make_async_remote_copy(
                past_ref.at[pl.ds(c * chunk, chunk)], have_b.at[at], x_send.at[c], x_recv.at[c],
                device_id=(dp, y * 8 + (1 - x) * 4 + z), device_id_type=MESH,
            )

        turn = (0, 2, 1, 3)
        ways = [(way, 0, c) for c in turn for way in ((1, 3) if c < 2 else (3, 1))]
        ways += [(1, 3, c) if c < 2 else (3, 1, c) for c in turn]

        def go(t, n):
            way, owner, c = ways[n]
            return pltpu.make_async_remote_copy(
                region(t, owner, c), region(t, owner, c), g_send.at[t, n], g_recv.at[t, n],
                device_id=(dp, step_id(y, x, z, half[t], way)), device_id_type=MESH,
            )

        def came(t, n):
            way, owner, c = ways[n]
            owner = (owner - way) % 4
            return pltpu.make_async_remote_copy(
                region(t, owner, c), region(t, owner, c), g_send.at[t, n], g_recv.at[t, n],
                device_id=(dp, step_id(y, x, z, half[t], way)), device_id_type=MESH,
            )

        def swap(t, hop, arriving=False):
            h = half[t]
            at = h * 4 + pos(1 - h, -hop if arriving else 0)
            return pltpu.make_async_remote_copy(
                sel[t].at[hop], out_ref.at[pl.ds(at * cap, cap)],
                e_send.at[t, hop - 1], e_recv.at[t, hop - 1],
                device_id=(dp, step_id(y, x, z, 1 - h, hop)), device_id_type=MESH,
            )

        def keep(t):
            h = half[t]
            at = h * 4 + pos(1 - h)
            return pltpu.make_async_copy(
                sel[t].at[0], out_ref.at[pl.ds(at * cap, cap)], own_sem.at[t]
            )

        def choose(t):
            h = half[t]
            for hop in (2, 1, 3, 0):
                row = h * 4 + pos(1 - h, hop)

                @pl.loop(0, cap)
                def _(s):
                    sel[t][hop, s] = have[t][table_ref[row * cap + s]]

                if hop:
                    swap(t, hop).start()
                else:
                    keep(t).start()

        for c in turn:
            cross(c).start()
        local.wait()
        for n in range(2 * parts):
            go(0, n).start()

        def relay(t, i):
            came(t, 2 * i).wait_recv()
            go(t, 2 * parts + i).start()

        for i in range(parts):
            crossed(turn[i]).wait_recv()
            go(1, 2 * i).start()
            go(1, 2 * i + 1).start()
            relay(0, i)
        for i in range(parts):
            relay(1, i)
        for t in (0, 1):
            for n in range(2 * parts):
                if n % 2:
                    came(t, n).wait_recv()
            for n in range(2 * parts, 3 * parts):
                came(t, n).wait_recv()
        choose(0)
        choose(1)
        for t in (0, 1):
            for hop in (1, 2, 3):
                swap(t, hop, True).wait_recv()
            keep(t).wait()
        for c in turn:
            cross(c).wait_send()
        for t in (0, 1):
            for n in range(3 * parts):
                go(t, n).wait_send()
            for hop in (1, 2, 3):
                swap(t, hop).wait_send()

    return pl.pallas_call(
        kernel,
        out_shape=jax.ShapeDtypeStruct((8 * cap, rows, width), past.dtype),
        in_specs=[pl.BlockSpec(memory_space=pltpu.SMEM), pl.BlockSpec(memory_space=pl.ANY)],
        out_specs=pl.BlockSpec(memory_space=pl.ANY),
        scratch_shapes=[
            pltpu.VMEM((4 * blocks, rows, width), past.dtype),
            pltpu.VMEM((4 * blocks, rows, width), past.dtype),
            pltpu.VMEM((4, cap, rows, width), past.dtype),
            pltpu.VMEM((4, cap, rows, width), past.dtype),
            pltpu.SemaphoreType.DMA,
            pltpu.SemaphoreType.DMA((parts,)),
            pltpu.SemaphoreType.DMA((parts,)),
            pltpu.SemaphoreType.DMA((2, 3 * parts)),
            pltpu.SemaphoreType.DMA((2, 3 * parts)),
            pltpu.SemaphoreType.DMA((2, 3)),
            pltpu.SemaphoreType.DMA((2, 3)),
            pltpu.SemaphoreType.DMA((2,)),
        ],
        compiler_params=pltpu.CompilerParams(
            collective_id=ident, has_side_effects=True, vmem_limit_bytes=48 << 20
        ),
        name="spread",
    )(table, past)


def send_back(grads, tokens, grad_out, seen, dkv, dq, mixed, ident):
    slots, rows, width = grads.shape
    cap = slots // 8
    total = seen.shape[0]
    chunk = total // 8

    def kernel(
        grad_ref, tok_in, gout_in, seen_in, dkv_in, dq_in, mixed_in,
        out_ref, wq_ref, wk_ref, wv_ref, wo_ref, own, send, recv, own_sem,
        tok_ref, gout_ref, seen_ref, dkv_ref, dq_ref, mixed_ref, op_sem,
    ):
        pairs = (
            (tok_in, tok_ref), (dq_in, dq_ref), (mixed_in, mixed_ref), (gout_in, gout_ref),
            (seen_in, seen_ref), (dkv_in, dkv_ref),
        )
        operands = [pltpu.make_async_copy(a, b, op_sem.at[i]) for i, (a, b) in enumerate(pairs)]
        y, x, z, dp = place()
        pos = lambda dim, hop=0: (y * (1 - dim) + z * dim + hop) % 4
        part = lambda ref, at: ref.at[pl.ds(at * cap, cap)]

        def swap(h, hop, arriving=False):
            return pltpu.make_async_remote_copy(
                part(grad_ref, h * 4 + pos(1 - h, hop)),
                part(out_ref, h * 4 + pos(1 - h, -hop if arriving else 0)),
                send.at[h, hop - 1], recv.at[h, hop - 1],
                device_id=(dp, step_id(y, x, z, 1 - h, hop)), device_id_type=MESH,
            )

        def load(h):
            return pltpu.make_async_copy(
                part(grad_ref, h * 4 + pos(1 - h)), own.at[h], own_sem.at[h]
            )

        def store(h):
            return pltpu.make_async_copy(
                own.at[h], part(out_ref, h * 4 + pos(1 - h)), own_sem.at[h]
            )

        for h in (0, 1):
            load(h).start()
        meet(y, x, z, dp, False)
        for hop in (2, 1, 3):
            for h in (0, 1):
                swap(h, hop).start()
        for h in (0, 1):
            load(h).wait()
            store(h).start()
        for operand in operands:
            operand.start()
        for operand in operands:
            operand.wait()
        wq_ref[...] = mm(tok_ref[...], dq_ref[...], TN)
        wo_ref[...] = mm(mixed_ref[...], gout_ref[...], TN)
        wk_ref[...] = jnp.zeros_like(wk_ref)
        wv_ref[...] = jnp.zeros_like(wv_ref)

        @pl.loop(0, total // chunk)
        def _(n):
            at = pl.ds(pl.multiple_of(n * chunk, 16), chunk)
            left = seen_ref[at]
            wk_ref[...] += mm(left, dkv_ref[at, :width], TN)
            wv_ref[...] += mm(left, dkv_ref[at, width:], TN)

        for h in (0, 1):
            store(h).wait()
            for hop in (1, 2, 3):
                swap(h, hop, True).wait_recv()
        for h in (0, 1):
            for hop in (1, 2, 3):
                swap(h, hop).wait_send()

    return pl.pallas_call(
        kernel,
        out_shape=(jax.ShapeDtypeStruct(grads.shape, grads.dtype),)
        + (jax.ShapeDtypeStruct((width, width), F32),) * 4,
        in_specs=[pl.BlockSpec(memory_space=pl.ANY)] * 7,
        out_specs=(pl.BlockSpec(memory_space=pl.ANY),) + (pl.BlockSpec(memory_space=pltpu.VMEM),) * 4,
        scratch_shapes=[
            pltpu.VMEM((2, cap, rows, width), grads.dtype),
            pltpu.SemaphoreType.DMA((2, 3)),
            pltpu.SemaphoreType.DMA((2, 3)),
            pltpu.SemaphoreType.DMA((2,)),
        ]
        + [pltpu.VMEM(a.shape, a.dtype) for a in (tokens, grad_out, seen, dkv, dq, mixed)]
        + [pltpu.SemaphoreType.DMA((6,))],
        compiler_params=pltpu.CompilerParams(
            collective_id=ident, has_side_effects=True, vmem_limit_bytes=56 << 20
        ),
        name="send_back",
    )(grads, tokens, grad_out, seen, dkv, dq, mixed)


def collect(partial, grads, scale):
    groups, blocks, rows, width = partial.shape
    chunk = blocks // 2
    w_rows = grads[0].shape[0]
    block = w_rows // 24
    half_w = 48

    def collect_steps(
        part_in, part_ref, part_sem, out_ref, relay, staged, inward, mine, across,
        r_send, r_recv, d_send, d_recv, x_send, x_recv,
    ):
        y, x, z, dp = place()
        pos = lambda dim, hop=0: (y * (1 - dim) + z * dim + hop) % 4
        half = (1 - x, x)
        held = pltpu.make_async_copy(part_in, part_ref, part_sem)
        held.start()
        ways = (3, 1)

        def row(t, hop):
            return half[t] * 4 + pos(half[t], hop)

        def pass_on(t, side):
            return pltpu.make_async_remote_copy(
                part_in.at[row(t, 2), pl.ds(side * chunk, chunk)], relay.at[t, side],
                r_send.at[t, side], r_recv.at[t, side],
                device_id=(dp, step_id(y, x, z, half[t], ways[side])), device_id_type=MESH,
            )

        def direct(t, side, summed):
            c = side if summed else 1 - side
            source = (
                staged.at[t, side] if summed
                else part_in.at[row(t, ways[side]), pl.ds(c * chunk, chunk)]
            )
            return pltpu.make_async_remote_copy(
                source, inward.at[t, side, pl.ds(c * chunk, chunk)],
                d_send.at[t, side, int(summed)], d_recv.at[t, side, int(summed)],
                device_id=(dp, step_id(y, x, z, half[t], ways[side])), device_id_type=MESH,
            )

        def cross(c):
            return pltpu.make_async_remote_copy(
                mine.at[pl.ds(c * chunk, chunk)], across.at[pl.ds(c * chunk, chunk)],
                x_send.at[c], x_recv.at[c],
                device_id=(dp, y * 8 + (1 - x) * 4 + z), device_id_type=MESH,
            )

        def final(t, b):
            return (
                part_ref[row(t, 0), b].astype(F32)
                + inward[t, 0, b].astype(F32)
                + inward[t, 1, b].astype(F32)
            )

        for t in (0, 1):
            for side in (0, 1):
                pass_on(t, side).start()
        for t in (0, 1):
            for side in (0, 1):
                direct(t, side, False).start()
        yield
        held.wait()
        for t in (0, 1):
            for side in (0, 1):
                pass_on(t, side).wait_recv()

                @pl.loop(0, chunk)
                def _(b):
                    own = part_ref[row(t, ways[side]), side * chunk + b]
                    staged[t, side, b] = (
                        own.astype(F32) + relay[t, side, b].astype(F32)
                    ).astype(staged.dtype)

                direct(t, side, True).start()
        yield
        for side in (0, 1):
            for summed in (False, True):
                direct(0, side, summed).wait_recv()
        for c in (0, 1):
            @pl.loop(0, chunk)
            def _(b):
                mine[c * chunk + b] = final(0, c * chunk + b).astype(mine.dtype)

            cross(c).start()
        yield
        for side in (0, 1):
            for summed in (False, True):
                direct(1, side, summed).wait_recv()
        for c in (0, 1):
            cross(c).wait_recv()

            @pl.loop(0, chunk)
            def _(b):
                at = c * chunk + b
                out_ref[at] = (final(1, at) + across[at].astype(F32)).astype(out_ref.dtype)

        yield
        for t in (0, 1):
            cross(t).wait_send()
            for side in (0, 1):
                pass_on(t, side).wait_send()
                for summed in (False, True):
                    direct(t, side, summed).wait_send()

    def reduce_steps(
        given, refs, grad_sem, out_ref, acc, stage, peer, mid, in_a, mid_b, in_b, in_c, got_b, full,
        core_send, core_recv, send, recv, back_send, back_recv, out_sem,
    ):
        y, x_low, z, dp = place()
        core = dp % 2
        spot = {"x": (dp // 2) * 2 + x_low, "y": y, "z": z}
        orders = ("xyz", "yzx", "zxy")
        a_ref, b_ref, c_ref, d_ref = refs
        loads = [pltpu.make_async_copy(given[i], refs[i], grad_sem.at[i]) for i in range(4)]
        for load in loads:
            load.start()

        def there(axis, hop):
            at = dict(spot)
            at[axis] = (at[axis] + hop) % 4
            return (
                (at["x"] // 2) * 2 + core,
                at["y"] * 8 + (at["x"] % 2) * 4 + at["z"],
            )

        other = (dp + 1 - 2 * core, y * 8 + x_low * 4 + z)
        barrier = pltpu.get_barrier_semaphore()
        for axis in "xyz":
            for hop in (1, 2, 3):
                pl.semaphore_signal(barrier, 1, device_id=there(axis, hop), device_id_type=MESH)
        pl.semaphore_signal(barrier, 1, device_id=other, device_id_type=MESH)
        pl.semaphore_wait(barrier, 10)
        yield
        for load in loads:
            load.wait()

        def take(keep, give):
            for i in (0, 1):
                @pl.loop(0, half_w // 2)
                def _(n):
                    at = pl.ds(pl.multiple_of(n * block, block), block)
                    stage[i * (half_w // 2) + n] = (give[i][at] * scale).astype(BF16)
                    acc[i * (half_w // 2) + n] = keep[i][at] * scale

        @pl.when(core == 0)
        def _():
            take((a_ref, b_ref), (c_ref, d_ref))

        @pl.when(core == 1)
        def _():
            take((c_ref, d_ref), (a_ref, b_ref))

        def pair(p):
            at = pl.ds(p * 16, 16)
            return pltpu.make_async_remote_copy(
                stage.at[at], peer.at[at], core_send.at[p], core_recv.at[p],
                device_id=other, device_id_type=MESH,
            )

        def copy(source, target, phase, p, hop, sems=None):
            s, r = sems or (send, recv)
            return pltpu.make_async_remote_copy(
                source, target, s.at[phase, p, hop - 1], r.at[phase, p, hop - 1],
                device_id=there(orders[p][(0, 1, 2, 1, 0)[phase]], hop), device_id_type=MESH,
            )

        def at_axis(p, phase, hop=0):
            return (spot[orders[p][phase]] + hop) % 4

        def scatter_a(p, hop):
            at = pl.ds(p * 16 + at_axis(p, 0, hop) * 4, 4)
            return copy(mid.at[at], in_a.at[p, hop - 1], 0, p, hop)

        def scatter_b(p, hop):
            return copy(mid_b.at[p, at_axis(p, 1, hop)], in_b.at[p, hop - 1], 1, p, hop)

        def swap_c(p, hop, arriving=False):
            to = at_axis(p, 2, -hop if arriving else 0)
            return copy(in_c.at[p, at_axis(p, 2)], in_c.at[p, to], 2, p, hop)

        def spread_b(p, hop, arriving=False):
            to = at_axis(p, 1, -hop if arriving else 0)
            return copy(got_b.at[p, at_axis(p, 1)], got_b.at[p, to], 3, p, hop)

        def spread_a(p, hop, arriving=False):
            row = lambda back: pl.ds(core * half_w + p * 16 + at_axis(p, 0, back) * 4, 4)
            return copy(
                full.at[row(0)], full.at[row(-hop if arriving else 0)], 4, p, hop
            )

        def final(p, arriving=False):
            side = 1 - core if arriving else core
            at = pl.ds(side * half_w + p * 16, 16)
            return pltpu.make_async_remote_copy(
                full.at[at], full.at[at], back_send.at[p], back_recv.at[p],
                device_id=other, device_id_type=MESH,
            )

        hops = (2, 1, 3)
        for p in range(3):
            pair(p).start()
        yield
        for p in range(3):
            pair(p).wait_recv()

            @pl.loop(0, 16)
            def _(n):
                total = acc[p * 16 + n] + peer[p * 16 + n].astype(F32)
                acc[p * 16 + n] = total
                mid[p * 16 + n] = total.astype(BF16)

            for hop in hops:
                scatter_a(p, hop).start()
        yield
        for p in range(3):
            for hop in hops:
                scatter_a(p, hop).wait_recv()

            @pl.loop(0, 4)
            def _(n):
                at = p * 16 + at_axis(p, 0) * 4 + n
                total = acc[at]
                for i in range(3):
                    total = total + in_a[p, i, n].astype(F32)
                acc[at] = total
                mid_b[p, n] = total.astype(BF16)

            for hop in hops:
                scatter_b(p, hop).start()
        yield
        for p in range(3):
            for hop in hops:
                scatter_b(p, hop).wait_recv()
            total = acc[p * 16 + at_axis(p, 0) * 4 + at_axis(p, 1)]
            for i in range(3):
                total = total + in_b[p, i].astype(F32)
            in_c[p, at_axis(p, 2)] = total.astype(BF16)
            for hop in hops:
                swap_c(p, hop).start()
        yield
        for p in range(3):
            for hop in hops:
                swap_c(p, hop, True).wait_recv()
            total = in_c[p, 0].astype(F32)
            for i in range(1, 4):
                total = total + in_c[p, i].astype(F32)
            got_b[p, at_axis(p, 1)] = total.astype(BF16)
            for hop in hops:
                spread_b(p, hop).start()
        yield
        for p in range(3):
            for hop in hops:
                spread_b(p, hop, True).wait_recv()

            @pl.loop(0, 4)
            def _(n):
                full[core * half_w + p * 16 + at_axis(p, 0) * 4 + n] = got_b[p, n]

            for hop in hops:
                spread_a(p, hop).start()
        yield
        for p in range(3):
            for hop in hops:
                spread_a(p, hop, True).wait_recv()
            final(p).start()
        yield
        for p in range(3):
            final(p, True).wait_recv()
        done = pltpu.make_async_copy(full, out_ref, out_sem)
        done.start()
        yield
        for p in range(3):
            pair(p).wait_send()
            final(p).wait_send()
            for hop in hops:
                scatter_a(p, hop).wait_send()
                scatter_b(p, hop).wait_send()
                swap_c(p, hop).wait_send()
                spread_b(p, hop).wait_send()
                spread_a(p, hop).wait_send()
        done.wait()

    def kernel(part_in, a, b, c, d, out_ref, weights_ref, part_ref, part_sem, *scratch):
        weights = reduce_steps(
            (a, b, c, d), scratch[:4], scratch[4], weights_ref, *scratch[16:]
        )
        blocks_back = collect_steps(part_in, part_ref, part_sem, out_ref, *scratch[5:16])
        for step in "wbwwbwwbwwwbwbw":
            next(weights if step == "w" else blocks_back, None)

    shape = lambda *s: pltpu.VMEM(s + (rows, width), partial.dtype)
    bf = lambda *s: pltpu.VMEM(s + (block, width), BF16)
    dma = lambda *s: pltpu.SemaphoreType.DMA(s)
    vmem = pl.BlockSpec(memory_space=pltpu.VMEM)
    past_grad, weights = pl.pallas_call(
        kernel,
        out_shape=(
            jax.ShapeDtypeStruct((blocks, rows, width), partial.dtype),
            jax.ShapeDtypeStruct((2 * half_w, block, width), BF16),
        ),
        in_specs=[pl.BlockSpec(memory_space=pl.ANY)] * 5,
        out_specs=(vmem, pl.BlockSpec(memory_space=pl.ANY)),
        scratch_shapes=[
            shape(groups, blocks), pltpu.SemaphoreType.DMA,
            *[pltpu.VMEM(a.shape, a.dtype) for a in grads], dma(4),
            shape(2, 2, chunk), shape(2, 2, chunk), shape(2, 2, blocks), shape(blocks), shape(blocks),
            dma(2, 2), dma(2, 2), dma(2, 2, 2), dma(2, 2, 2), dma(2), dma(2),
            pltpu.VMEM((half_w, block, width), F32),
            bf(half_w), bf(half_w), bf(half_w), bf(3, 3, 4), bf(3, 4), bf(3, 3), bf(3, 4), bf(3, 4),
            bf(2 * half_w),
            dma(3), dma(3), dma(5, 3, 3), dma(5, 3, 3), dma(3), dma(3), pltpu.SemaphoreType.DMA,
        ],
        compiler_params=pltpu.CompilerParams(
            collective_id=2, has_side_effects=True, vmem_limit_bytes=62 << 20
        ),
        name="collect",
    )(partial, *grads)
    return past_grad, weights.reshape(4, w_rows, width)


def scatter_sum(source, target, used, outputs):
    count, rows, width = source.shape
    step = 8

    def kernel(target_ref, used_ref, source_ref, out_ref, acc):
        t = pl.program_id(0)

        @pl.when(t == 0)
        def _():
            acc[...] = jnp.zeros_like(acc)

        for j in range(step):
            @pl.when(used_ref[t * step + j] > 0)
            def _():
                m = target_ref[t * step + j]
                acc[m] = acc[m] + source_ref[j].astype(F32)

        @pl.when(t == pl.num_programs(0) - 1)
        def _():
            out_ref[...] = acc[...].astype(out_ref.dtype)

    return pl.pallas_call(
        kernel,
        out_shape=jax.ShapeDtypeStruct((outputs, rows, width), source.dtype),
        grid_spec=pltpu.PrefetchScalarGridSpec(
            num_scalar_prefetch=2,
            grid=(count // step,),
            in_specs=[pl.BlockSpec((step, rows, width), lambda t, *_: (t, 0, 0))],
            out_specs=pl.BlockSpec((outputs, rows, width), lambda t, *_: (0, 0, 0)),
            scratch_shapes=[pltpu.VMEM((outputs, rows, width), F32)],
        ),
        compiler_params=pltpu.CompilerParams(vmem_limit_bytes=48 << 20),
        name="scatter_sum",
    )(target, used, source)


def layer(position, live, arrived, tokens, grad_out, w_query, w_pair, w_out, slots):
    patches, block, width = tokens.shape
    requests = position.shape[0] // patches
    far = requests * block
    rows = block + far
    chunks = 4
    chunk = far // chunks
    pairs = width // 128
    parts = requests + 1

    def kernel(
        position_ref, live_ref, arrived_ref, tokens_ref, grad_ref, wq_ref, wkv_ref, wo_ref,
        attn_ref, tokgrad_ref, fargrad_ref, x_ref, dkv_ref, dq_ref, mixed_ref,
        key_s, val_s, q_s, up_s, s_s, dp_s, pb_s, ds_s, fg_s, in_sem, out_sem,
    ):
        p = pl.program_id(0)

        def fetch(r):
            return pltpu.make_async_copy(
                arrived_ref.at[position_ref[p * requests + r]],
                x_ref.at[0, pl.ds(block + r * block, block)],
                in_sem.at[r],
            )

        for r in range(requests):
            fetch(r).start()
        tok = tokens_ref[0]
        x_ref[0, 0:block] = tok
        q_s[...] = mm(tok, wq_ref[...]).astype(BF16)
        own = mm(tok, wkv_ref[...]).astype(BF16)
        key_s[0:block] = own[:, :width]
        val_s[0:block] = own[:, width:]
        up_s[...] = mm(grad_ref[0], wo_ref[...], NT).astype(BF16)
        for r in range(requests):
            fetch(r).wait()

        @pl.loop(0, chunks)
        def _(c):
            at = pl.multiple_of(block + c * chunk, 128)
            x = x_ref[0, pl.ds(at, chunk)]
            key_s[pl.ds(at, chunk)] = mm(x, wkv_ref[:, :width]).astype(BF16)
            val_s[pl.ds(at, chunk)] = mm(x, wkv_ref[:, width:]).astype(BF16)

        low = lax.broadcasted_iota(jnp.int32, (block, 128), 1) < HD
        zero = jnp.zeros((block, 128), BF16)

        @pl.loop(0, pairs)
        def _(j):
            lanes = pl.ds(pl.multiple_of(j * 128, 128), 128)
            k = key_s[:, lanes]
            v = val_s[:, lanes]
            q = q_s[:, lanes] * jnp.asarray(1.0 / math.sqrt(HD), BF16)
            u = up_s[:, lanes]
            q2 = jnp.concatenate([jnp.where(low, q, zero), jnp.where(low, zero, q)], axis=0)
            u2 = jnp.concatenate([jnp.where(low, u, zero), jnp.where(low, zero, u)], axis=0)
            s_s[...] = mm(k, q2, NT)
            dp_s[...] = mm(v, u2, NT)

            def bias(r):
                dead = live_ref[p * requests + jnp.maximum(r - 1, 0)] == 0
                return jnp.where((r > 0) & dead, -jnp.inf, 0.0).astype(F32)

            def part(r):
                return pl.ds(pl.multiple_of(r * block, block), block)

            def largest(r, m):
                s = s_s[part(r)] + bias(r)
                return jnp.maximum(m, jnp.max(s.reshape(block // 8, 8, 2 * block), axis=0))

            m = lax.fori_loop(0, parts, largest, jnp.full((8, 2 * block), -jnp.inf, F32))
            m = jnp.max(m, axis=0, keepdims=True)

            def exps(r, carry):
                total, delta = carry
                e = jnp.exp(s_s[part(r)] + bias(r) - m)
                s_s[part(r)] = e
                g = e * dp_s[part(r)]
                fold = lambda t: jnp.sum(t.reshape(block // 8, 8, 2 * block), axis=0)
                return total + fold(e), delta + fold(g)

            nil = jnp.zeros((8, 2 * block), F32)
            total, delta = lax.fori_loop(0, parts, exps, (nil, nil))
            inverse = 1.0 / jnp.sum(total, axis=0, keepdims=True)
            delta = jnp.sum(delta, axis=0, keepdims=True) * inverse

            @pl.loop(0, parts)
            def _(r):
                prob = s_s[part(r)] * inverse
                pb_s[part(r)] = prob.astype(BF16)
                ds_s[part(r)] = (prob * (dp_s[part(r)] - delta)).astype(BF16)

            pb = pb_s[...]
            ds = ds_s[...]
            dkv_ref[0, :, lanes] = mm(ds, q2).astype(BF16)
            dkv_ref[0, :, pl.ds(pl.multiple_of(width + j * 128, 128), 128)] = mm(pb, u2).astype(BF16)
            o = mm(pb, v, TN)
            mixed_ref[0, :, lanes] = jnp.where(low, o[:block], o[block:]).astype(BF16)
            dq = mm(ds, k, TN)
            dq = jnp.where(low, dq[:block], dq[block:]) * (1.0 / math.sqrt(HD))
            dq_ref[0, :, lanes] = dq.astype(BF16)

        attn_ref[0] = mm(mixed_ref[0], wo_ref[...]).astype(BF16)
        tokgrad_ref[0] = (
            mm(dq_ref[0], wq_ref[...], NT) + mm(dkv_ref[0, 0:block], wkv_ref[...], NT)
        ).astype(BF16)

        @pl.loop(0, chunks)
        def _(c):
            at = pl.multiple_of(block + c * chunk, 128)
            g = mm(dkv_ref[0, pl.ds(at, chunk)], wkv_ref[...], NT).astype(BF16)
            fg_s[pl.ds(pl.multiple_of(c * chunk, 128), chunk)] = g

        def put(r):
            return pltpu.make_async_copy(
                fg_s.at[pl.ds(r * block, block)],
                fargrad_ref.at[position_ref[p * requests + r]],
                out_sem.at[r],
            )

        for r in range(requests):
            @pl.when(live_ref[p * requests + r] > 0)
            def _():
                put(r).start()

        for r in range(requests):
            @pl.when(live_ref[p * requests + r] > 0)
            def _():
                put(r).wait()

    per_patch = lambda n, w: pl.BlockSpec((1, n, w), lambda p, *_: (p, 0, 0))
    whole = lambda a: pl.BlockSpec(a.shape, lambda p, *_: (0, 0), pipeline_mode=pl.Buffered(1))
    hbm = pl.BlockSpec(memory_space=pl.ANY)
    shape = lambda *s: jax.ShapeDtypeStruct(s, BF16)
    return pl.pallas_call(
        kernel,
        out_shape=(
            shape(patches, block, width),
            shape(patches, block, width),
            shape(slots, block, width),
            shape(patches, rows, width),
            shape(patches, rows, 2 * width),
            shape(patches, block, width),
            shape(patches, block, width),
        ),
        grid_spec=pltpu.PrefetchScalarGridSpec(
            num_scalar_prefetch=2,
            grid=(patches,),
            in_specs=[
                hbm, per_patch(block, width), per_patch(block, width),
                whole(w_query), whole(w_pair), whole(w_out),
            ],
            out_specs=(
                per_patch(block, width), per_patch(block, width), hbm, per_patch(rows, width),
                per_patch(rows, 2 * width), per_patch(block, width), per_patch(block, width),
            ),
            scratch_shapes=[
                pltpu.VMEM((rows, width), BF16),
                pltpu.VMEM((rows, width), BF16),
                pltpu.VMEM((block, width), BF16),
                pltpu.VMEM((block, width), BF16),
                pltpu.VMEM((rows, 2 * block), F32),
                pltpu.VMEM((rows, 2 * block), F32),
                pltpu.VMEM((rows, 2 * block), BF16),
                pltpu.VMEM((rows, 2 * block), BF16),
                pltpu.VMEM((far, width), BF16),
                pltpu.SemaphoreType.DMA((requests,)),
                pltpu.SemaphoreType.DMA((requests,)),
            ],
        ),
        compiler_params=pltpu.CompilerParams(vmem_limit_bytes=60 << 20),
        name="layer",
    )(position, live, arrived, tokens, grad_out, w_query, w_pair, w_out)


def body(
    query_tokens, past_tokens, source_dev, source_slot, kept, w_query, w_key, w_value, w_out,
    grad_out,
):
    _, patches, block, width = query_tokens.shape
    tokens, grads, past = query_tokens[0], grad_out[0], past_tokens[0]
    peers = lax.axis_size("patch")
    y, x, z, _ = place()
    per_device = patches * source_dev.shape[1] * source_dev.shape[2]
    blocks = past.shape[0]

    grid = lambda a: a.reshape(4, 2, 4, per_device)
    near = lambda a: jnp.concatenate([grid(a)[y, x], grid(a)[:, x, z]], axis=0)
    owner, slot, kept = (a.reshape(peers, per_device) for a in (source_dev, source_slot, kept))
    from_y, half, from_z = owner // 8, (owner // 4) % 2, owner % 4
    key = half * 4 + jnp.where(half == 0, from_z, from_y)
    number = jnp.where(half == 0, from_y, from_z) * blocks + slot
    key = jnp.where(kept > 0, key, 8)
    most = jnp.max(jnp.sum((key[:, None, :] == jnp.arange(8)[None, :, None]).astype(jnp.int32), axis=2))
    key, number = near(key), near(number)
    order = jnp.arange(per_device)
    matches = (key[:, :, None] == key[:, None, :]) & (order[:, None] > order[None, :])
    rank = jnp.sum(matches.astype(jnp.int32), axis=2)
    chosen_here = jnp.where(jnp.arange(8) < 4, z, 4 + y)
    live = grid(kept)[y, x, z]
    w_pair = jnp.concatenate([w_key, w_value], axis=1)
    flat = lambda a: a.reshape(-1, a.shape[-1])

    def exchange(cap, ident):
        hit = (rank[:, :, None] == jnp.arange(cap)) & (key == chosen_here[:, None])[:, :, None]
        table = jnp.sum(jnp.where(hit, number[:, :, None], 0), axis=1)
        used = jnp.sum(hit.astype(jnp.int32), axis=1).reshape(-1)
        target = (table + jnp.where(jnp.arange(8) < 4, 0, 4 * blocks)[:, None]).reshape(-1)
        mine = jnp.where(live > 0, key[z] * cap + rank[z], 0)
        arrived = spread(past, table.reshape(-1), ident)
        attn, token_grad, far_grad, seen, dkv, dq, mixed = layer(
            mine, live, arrived, tokens, grads, w_query, w_pair, w_out, 8 * cap
        )
        returned, *weight_grads = send_back(
            far_grad, flat(tokens), flat(grads), flat(seen), flat(dkv), flat(dq), flat(mixed), ident + 1
        )
        partial = scatter_sum(returned, target, used, 8 * blocks)
        return attn, token_grad, partial, tuple(weight_grads)

    attn, token_grad, partial, weight_grads = lax.cond(
        most <= 6, lambda: exchange(6, 0), lambda: exchange(8, 3)
    )
    scale = 1.0 / math.sqrt(lax.axis_size("dp") * peers * patches * block)
    past_grad, weights = collect(partial.reshape((8,) + past.shape), weight_grads, scale)
    weights = weights.astype(F32)
    return (
        attn[None],
        token_grad[None],
        past_grad[None],
        weights[0],
        weights[1],
        weights[2],
        weights[3],
    )


def solution(mesh):
    split = P("dp", "patch", None, None)
    return jax.shard_map(
        body,
        mesh=mesh,
        in_specs=(split, split, P(), P(), P(), P(), P(), P(), P(), split),
        out_specs=(split, split, split, P(), P(), P(), P()),
        check_vma=False,
    )
```

```python
import math

import jax
import jax.numpy as jnp
from jax import lax
from jax.experimental import pallas as pl
from jax.experimental.pallas import tpu as pltpu
from jax.sharding import PartitionSpec as P

H = 12
HD = 64
F32 = jnp.float32
MESH = pl.DeviceIdType.MESH
BF16 = jnp.bfloat16
NN = (((1,), (0,)), ((), ()))
NT = (((1,), (1,)), ((), ()))
TN = (((0,), (0,)), ((), ()))


def mm(a, b, dims=NN):
    return lax.dot_general(a, b, dims, preferred_element_type=F32)


def place():
    device = lax.axis_index("patch")
    return device // 8, (device // 4) % 2, device % 4, lax.axis_index("dp")


def step_id(y, x, z, dim, hop):
    return ((y + hop * (1 - dim)) % 4) * 8 + x * 4 + (z + hop * dim) % 4


def meet(y, x, z, dp, across):
    barrier = pltpu.get_barrier_semaphore()
    ids = [step_id(y, x, z, dim, hop) for dim in (0, 1) for hop in (1, 2, 3)]
    if across:
        ids.append(y * 8 + (1 - x) * 4 + z)
    for other in ids:
        pl.semaphore_signal(barrier, 1, device_id=(dp, other), device_id_type=MESH)
    pl.semaphore_wait(barrier, len(ids))


def spread(past, table, ident):
    blocks, rows, width = past.shape
    parts = 4
    chunk = blocks // parts
    cap = table.shape[0] // 8

    def kernel(
        table_ref, past_ref, out_ref, have_a, have_b, sel_a, sel_b,
        in_sem, x_send, x_recv, g_send, g_recv, e_send, e_recv, own_sem,
    ):
        y, x, z, dp = place()
        pos = lambda dim, hop=0: (y * (1 - dim) + z * dim + hop) % 4
        have, sel = (have_a, have_b), (sel_a, sel_b)
        half = (x, 1 - x)

        def region(t, hop, c):
            return have[t].at[pl.ds(pos(half[t], hop) * blocks + c * chunk, chunk)]

        local = pltpu.make_async_copy(
            past_ref, have_a.at[pl.ds(pos(half[0]) * blocks, blocks)], in_sem
        )
        local.start()
        meet(y, x, z, dp, True)

        def cross(c):
            at = pl.ds(pos(half[0]) * blocks + c * chunk, chunk)
            return pltpu.make_async_remote_copy(
                past_ref.at[pl.ds(c * chunk, chunk)], have_b.at[at], x_send.at[c], x_recv.at[c],
                device_id=(dp, y * 8 + (1 - x) * 4 + z), device_id_type=MESH,
            )

        def crossed(c):
            at = pl.ds(pos(half[1]) * blocks + c * chunk, chunk)
            return pltpu.make_async_remote_copy(
                past_ref.at[pl.ds(c * chunk, chunk)], have_b.at[at], x_send.at[c], x_recv.at[c],
                device_id=(dp, y * 8 + (1 - x) * 4 + z), device_id_type=MESH,
            )

        turn = (0, 2, 1, 3)
        ways = [(way, 0, c) for c in turn for way in ((1, 3) if c < 2 else (3, 1))]
        ways += [(1, 3, c) if c < 2 else (3, 1, c) for c in turn]

        def go(t, n):
            way, owner, c = ways[n]
            return pltpu.make_async_remote_copy(
                region(t, owner, c), region(t, owner, c), g_send.at[t, n], g_recv.at[t, n],
                device_id=(dp, step_id(y, x, z, half[t], way)), device_id_type=MESH,
            )

        def came(t, n):
            way, owner, c = ways[n]
            owner = (owner - way) % 4
            return pltpu.make_async_remote_copy(
                region(t, owner, c), region(t, owner, c), g_send.at[t, n], g_recv.at[t, n],
                device_id=(dp, step_id(y, x, z, half[t], way)), device_id_type=MESH,
            )

        def swap(t, hop, arriving=False):
            h = half[t]
            at = h * 4 + pos(1 - h, -hop if arriving else 0)
            return pltpu.make_async_remote_copy(
                sel[t].at[hop], out_ref.at[pl.ds(at * cap, cap)],
                e_send.at[t, hop - 1], e_recv.at[t, hop - 1],
                device_id=(dp, step_id(y, x, z, 1 - h, hop)), device_id_type=MESH,
            )

        def keep(t):
            h = half[t]
            at = h * 4 + pos(1 - h)
            return pltpu.make_async_copy(
                sel[t].at[0], out_ref.at[pl.ds(at * cap, cap)], own_sem.at[t]
            )

        def choose(t):
            h = half[t]
            for hop in (2, 1, 3, 0):
                row = h * 4 + pos(1 - h, hop)

                @pl.loop(0, cap)
                def _(s):
                    sel[t][hop, s] = have[t][table_ref[row * cap + s]]

                if hop:
                    swap(t, hop).start()
                else:
                    keep(t).start()

        for c in turn:
            cross(c).start()
        local.wait()
        for n in range(2 * parts):
            go(0, n).start()

        def relay(t, i):
            came(t, 2 * i).wait_recv()
            go(t, 2 * parts + i).start()

        for i in range(parts):
            crossed(turn[i]).wait_recv()
            go(1, 2 * i).start()
            go(1, 2 * i + 1).start()
            relay(0, i)
        for i in range(parts):
            relay(1, i)
        for t in (0, 1):
            for n in range(2 * parts):
                if n % 2:
                    came(t, n).wait_recv()
            for n in range(2 * parts, 3 * parts):
                came(t, n).wait_recv()
        choose(0)
        choose(1)
        for t in (0, 1):
            for hop in (1, 2, 3):
                swap(t, hop, True).wait_recv()
            keep(t).wait()
        for c in turn:
            cross(c).wait_send()
        for t in (0, 1):
            for n in range(3 * parts):
                go(t, n).wait_send()
            for hop in (1, 2, 3):
                swap(t, hop).wait_send()

    return pl.pallas_call(
        kernel,
        out_shape=jax.ShapeDtypeStruct((8 * cap, rows, width), past.dtype),
        in_specs=[pl.BlockSpec(memory_space=pltpu.SMEM), pl.BlockSpec(memory_space=pl.ANY)],
        out_specs=pl.BlockSpec(memory_space=pl.ANY),
        scratch_shapes=[
            pltpu.VMEM((4 * blocks, rows, width), past.dtype),
            pltpu.VMEM((4 * blocks, rows, width), past.dtype),
            pltpu.VMEM((4, cap, rows, width), past.dtype),
            pltpu.VMEM((4, cap, rows, width), past.dtype),
            pltpu.SemaphoreType.DMA,
            pltpu.SemaphoreType.DMA((parts,)),
            pltpu.SemaphoreType.DMA((parts,)),
            pltpu.SemaphoreType.DMA((2, 3 * parts)),
            pltpu.SemaphoreType.DMA((2, 3 * parts)),
            pltpu.SemaphoreType.DMA((2, 3)),
            pltpu.SemaphoreType.DMA((2, 3)),
            pltpu.SemaphoreType.DMA((2,)),
        ],
        compiler_params=pltpu.CompilerParams(
            collective_id=ident, has_side_effects=True, vmem_limit_bytes=48 << 20
        ),
        name="spread",
    )(table, past)


def send_back(grads, tokens, grad_out, seen, dkv, dq, mixed, ident):
    slots, rows, width = grads.shape
    cap = slots // 8
    total = seen.shape[0]
    chunk = total // 8

    def kernel(
        grad_ref, tok_in, gout_in, seen_in, dkv_in, dq_in, mixed_in,
        out_ref, wq_ref, wk_ref, wv_ref, wo_ref, own, send, recv, own_sem,
        tok_ref, gout_ref, seen_ref, dkv_ref, dq_ref, mixed_ref, op_sem,
    ):
        pairs = (
            (tok_in, tok_ref), (dq_in, dq_ref), (mixed_in, mixed_ref), (gout_in, gout_ref),
            (seen_in, seen_ref), (dkv_in, dkv_ref),
        )
        operands = [pltpu.make_async_copy(a, b, op_sem.at[i]) for i, (a, b) in enumerate(pairs)]
        y, x, z, dp = place()
        pos = lambda dim, hop=0: (y * (1 - dim) + z * dim + hop) % 4
        part = lambda ref, at: ref.at[pl.ds(at * cap, cap)]

        def swap(h, hop, arriving=False):
            return pltpu.make_async_remote_copy(
                part(grad_ref, h * 4 + pos(1 - h, hop)),
                part(out_ref, h * 4 + pos(1 - h, -hop if arriving else 0)),
                send.at[h, hop - 1], recv.at[h, hop - 1],
                device_id=(dp, step_id(y, x, z, 1 - h, hop)), device_id_type=MESH,
            )

        def load(h):
            return pltpu.make_async_copy(
                part(grad_ref, h * 4 + pos(1 - h)), own.at[h], own_sem.at[h]
            )

        def store(h):
            return pltpu.make_async_copy(
                own.at[h], part(out_ref, h * 4 + pos(1 - h)), own_sem.at[h]
            )

        for h in (0, 1):
            load(h).start()
        meet(y, x, z, dp, False)
        for hop in (2, 1, 3):
            for h in (0, 1):
                swap(h, hop).start()
        for h in (0, 1):
            load(h).wait()
            store(h).start()
        for operand in operands:
            operand.start()
        for operand in operands:
            operand.wait()
        wq_ref[...] = mm(tok_ref[...], dq_ref[...], TN)
        wo_ref[...] = mm(mixed_ref[...], gout_ref[...], TN)
        wk_ref[...] = jnp.zeros_like(wk_ref)
        wv_ref[...] = jnp.zeros_like(wv_ref)

        @pl.loop(0, total // chunk)
        def _(n):
            at = pl.ds(pl.multiple_of(n * chunk, 16), chunk)
            left = seen_ref[at]
            wk_ref[...] += mm(left, dkv_ref[at, :width], TN)
            wv_ref[...] += mm(left, dkv_ref[at, width:], TN)

        for h in (0, 1):
            store(h).wait()
            for hop in (1, 2, 3):
                swap(h, hop, True).wait_recv()
        for h in (0, 1):
            for hop in (1, 2, 3):
                swap(h, hop).wait_send()

    return pl.pallas_call(
        kernel,
        out_shape=(jax.ShapeDtypeStruct(grads.shape, grads.dtype),)
        + (jax.ShapeDtypeStruct((width, width), F32),) * 4,
        in_specs=[pl.BlockSpec(memory_space=pl.ANY)] * 7,
        out_specs=(pl.BlockSpec(memory_space=pl.ANY),) + (pl.BlockSpec(memory_space=pltpu.VMEM),) * 4,
        scratch_shapes=[
            pltpu.VMEM((2, cap, rows, width), grads.dtype),
            pltpu.SemaphoreType.DMA((2, 3)),
            pltpu.SemaphoreType.DMA((2, 3)),
            pltpu.SemaphoreType.DMA((2,)),
        ]
        + [pltpu.VMEM(a.shape, a.dtype) for a in (tokens, grad_out, seen, dkv, dq, mixed)]
        + [pltpu.SemaphoreType.DMA((6,))],
        compiler_params=pltpu.CompilerParams(
            collective_id=ident, has_side_effects=True, vmem_limit_bytes=56 << 20
        ),
        name="send_back",
    )(grads, tokens, grad_out, seen, dkv, dq, mixed)


def collect(partial, grads, scale):
    groups, blocks, rows, width = partial.shape
    chunk = blocks // 4
    w_rows = grads[0].shape[0]
    block = w_rows // 24
    half_w = 48

    def collect_steps(
        part_in, part_ref, part_sem, out_ref, relay, staged, inward, mine, across,
        r_send, r_recv, d_send, d_recv, x_send, x_recv,
    ):
        y, x, z, dp = place()
        pos = lambda dim, hop=0: (y * (1 - dim) + z * dim + hop) % 4
        half = (1 - x, x)
        held = pltpu.make_async_copy(part_in, part_ref, part_sem)
        held.start()
        ways = (3, 1)
        side_of = (0, 0, 1, 1)

        def row(t, hop):
            return half[t] * 4 + pos(half[t], hop)

        def span(c):
            return pl.ds(c * chunk, chunk)

        def send_to(source, target, sends, recvs, t, side):
            return pltpu.make_async_remote_copy(
                source, target, sends, recvs,
                device_id=(dp, step_id(y, x, z, half[t], ways[side])), device_id_type=MESH,
            )

        def pass_on(t, c):
            return send_to(
                part_in.at[row(t, 2), span(c)], relay.at[t, span(c)],
                r_send.at[t, c], r_recv.at[t, c], t, side_of[c],
            )

        def plain(t, c):
            side = 1 - side_of[c]
            return send_to(
                part_in.at[row(t, ways[side]), span(c)], inward.at[t, side, span(c)],
                d_send.at[t, c, 0], d_recv.at[t, c, 0], t, side,
            )

        def summed(t, c):
            side = side_of[c]
            return send_to(
                staged.at[t, span(c)], inward.at[t, side, span(c)],
                d_send.at[t, c, 1], d_recv.at[t, c, 1], t, side,
            )

        def cross(c):
            return pltpu.make_async_remote_copy(
                mine.at[span(c)], across.at[span(c)], x_send.at[c], x_recv.at[c],
                device_id=(dp, y * 8 + (1 - x) * 4 + z), device_id_type=MESH,
            )

        def final(t, b):
            return (
                part_ref[row(t, 0), b].astype(F32)
                + inward[t, 0, b].astype(F32)
                + inward[t, 1, b].astype(F32)
            )

        def join(t, c):
            pass_on(t, c).wait_recv()

            @pl.loop(c * chunk, c * chunk + chunk)
            def _(b):
                own = part_ref[row(t, ways[side_of[c]]), b]
                staged[t, b] = (own.astype(F32) + relay[t, b].astype(F32)).astype(staged.dtype)

            summed(t, c).start()

        def arrive(t, c):
            plain(t, c).wait_recv()
            summed(t, c).wait_recv()

        def finish_other(c):
            arrive(0, c)

            @pl.loop(c * chunk, c * chunk + chunk)
            def _(b):
                mine[b] = final(0, b).astype(mine.dtype)

            cross(c).start()

        for c in (0, 2, 1, 3):
            for t in (0, 1):
                pass_on(t, c).start()
        for c in (2, 0):
            for t in (0, 1):
                plain(t, c).start()
        yield
        held.wait()
        for c in (0, 2):
            for t in (0, 1):
                join(t, c)
                plain(t, 3 - c).start()
        yield
        for c in (1, 3):
            for t in (0, 1):
                join(t, c)
        yield
        for c in (0, 2):
            finish_other(c)
        yield
        for c in (1, 3):
            finish_other(c)
        yield
        for c in (0, 2, 1, 3):
            arrive(1, c)
            cross(c).wait_recv()

            @pl.loop(c * chunk, c * chunk + chunk)
            def _(b):
                out_ref[b] = (final(1, b) + across[b].astype(F32)).astype(out_ref.dtype)

        yield
        for c in range(4):
            cross(c).wait_send()
            for t in (0, 1):
                pass_on(t, c).wait_send()
                plain(t, c).wait_send()
                summed(t, c).wait_send()

    def reduce_steps(
        given, refs, grad_sem, out_ref, acc, stage, peer, mid, in_a, mid_b, in_b, in_c, got_b, full,
        core_send, core_recv, send, recv, back_send, back_recv, out_sem,
    ):
        y, x_low, z, dp = place()
        core = dp % 2
        spot = {"x": (dp // 2) * 2 + x_low, "y": y, "z": z}
        orders = ("xyz", "yzx", "zxy")
        a_ref, b_ref, c_ref, d_ref = refs
        loads = [pltpu.make_async_copy(given[i], refs[i], grad_sem.at[i]) for i in range(4)]
        for load in loads:
            load.start()

        def there(axis, hop):
            at = dict(spot)
            at[axis] = (at[axis] + hop) % 4
            return (
                (at["x"] // 2) * 2 + core,
                at["y"] * 8 + (at["x"] % 2) * 4 + at["z"],
            )

        other = (dp + 1 - 2 * core, y * 8 + x_low * 4 + z)
        barrier = pltpu.get_barrier_semaphore()
        for axis in "xyz":
            for hop in (1, 2, 3):
                pl.semaphore_signal(barrier, 1, device_id=there(axis, hop), device_id_type=MESH)
        pl.semaphore_signal(barrier, 1, device_id=other, device_id_type=MESH)
        pl.semaphore_wait(barrier, 10)
        yield
        for load in loads:
            load.wait()

        def take(keep, give):
            for i in (0, 1):
                @pl.loop(0, half_w // 2)
                def _(n):
                    at = pl.ds(pl.multiple_of(n * block, block), block)
                    stage[i * (half_w // 2) + n] = (give[i][at] * scale).astype(BF16)
                    acc[i * (half_w // 2) + n] = keep[i][at] * scale

        @pl.when(core == 0)
        def _():
            take((a_ref, b_ref), (c_ref, d_ref))

        @pl.when(core == 1)
        def _():
            take((c_ref, d_ref), (a_ref, b_ref))

        def pair(p):
            at = pl.ds(p * 16, 16)
            return pltpu.make_async_remote_copy(
                stage.at[at], peer.at[at], core_send.at[p], core_recv.at[p],
                device_id=other, device_id_type=MESH,
            )

        def copy(source, target, phase, p, hop, sems=None):
            s, r = sems or (send, recv)
            return pltpu.make_async_remote_copy(
                source, target, s.at[phase, p, hop - 1], r.at[phase, p, hop - 1],
                device_id=there(orders[p][(0, 1, 2, 1, 0)[phase]], hop), device_id_type=MESH,
            )

        def at_axis(p, phase, hop=0):
            return (spot[orders[p][phase]] + hop) % 4

        def scatter_a(p, hop):
            at = pl.ds(p * 16 + at_axis(p, 0, hop) * 4, 4)
            return copy(mid.at[at], in_a.at[p, hop - 1], 0, p, hop)

        def scatter_b(p, hop):
            return copy(mid_b.at[p, at_axis(p, 1, hop)], in_b.at[p, hop - 1], 1, p, hop)

        def swap_c(p, hop, arriving=False):
            to = at_axis(p, 2, -hop if arriving else 0)
            return copy(in_c.at[p, at_axis(p, 2)], in_c.at[p, to], 2, p, hop)

        def spread_b(p, hop, arriving=False):
            to = at_axis(p, 1, -hop if arriving else 0)
            return copy(got_b.at[p, at_axis(p, 1)], got_b.at[p, to], 3, p, hop)

        def spread_a(p, hop, arriving=False):
            row = lambda back: pl.ds(core * half_w + p * 16 + at_axis(p, 0, back) * 4, 4)
            return copy(
                full.at[row(0)], full.at[row(-hop if arriving else 0)], 4, p, hop
            )

        def final(p, arriving=False):
            side = 1 - core if arriving else core
            at = pl.ds(side * half_w + p * 16, 16)
            return pltpu.make_async_remote_copy(
                full.at[at], full.at[at], back_send.at[p], back_recv.at[p],
                device_id=other, device_id_type=MESH,
            )

        hops = (2, 1, 3)
        for p in range(3):
            pair(p).start()
        yield
        for p in range(3):
            pair(p).wait_recv()

            @pl.loop(0, 16)
            def _(n):
                total = acc[p * 16 + n] + peer[p * 16 + n].astype(F32)
                acc[p * 16 + n] = total
                mid[p * 16 + n] = total.astype(BF16)

            for hop in hops:
                scatter_a(p, hop).start()
        yield
        for p in range(3):
            for hop in hops:
                scatter_a(p, hop).wait_recv()

            @pl.loop(0, 4)
            def _(n):
                at = p * 16 + at_axis(p, 0) * 4 + n
                total = acc[at]
                for i in range(3):
                    total = total + in_a[p, i, n].astype(F32)
                acc[at] = total
                mid_b[p, n] = total.astype(BF16)

            for hop in hops:
                scatter_b(p, hop).start()
        yield
        for p in range(3):
            for hop in hops:
                scatter_b(p, hop).wait_recv()
            total = acc[p * 16 + at_axis(p, 0) * 4 + at_axis(p, 1)]
            for i in range(3):
                total = total + in_b[p, i].astype(F32)
            in_c[p, at_axis(p, 2)] = total.astype(BF16)
            for hop in hops:
                swap_c(p, hop).start()
        yield
        for p in range(3):
            for hop in hops:
                swap_c(p, hop, True).wait_recv()
            total = in_c[p, 0].astype(F32)
            for i in range(1, 4):
                total = total + in_c[p, i].astype(F32)
            got_b[p, at_axis(p, 1)] = total.astype(BF16)
            for hop in hops:
                spread_b(p, hop).start()
        yield
        for p in range(3):
            for hop in hops:
                spread_b(p, hop, True).wait_recv()

            @pl.loop(0, 4)
            def _(n):
                full[core * half_w + p * 16 + at_axis(p, 0) * 4 + n] = got_b[p, n]

            for hop in hops:
                spread_a(p, hop).start()
        yield
        for p in range(3):
            for hop in hops:
                spread_a(p, hop, True).wait_recv()
            final(p).start()
        yield
        for p in range(3):
            final(p, True).wait_recv()
        done = pltpu.make_async_copy(full, out_ref, out_sem)
        done.start()
        yield
        for p in range(3):
            pair(p).wait_send()
            final(p).wait_send()
            for hop in hops:
                scatter_a(p, hop).wait_send()
                scatter_b(p, hop).wait_send()
                swap_c(p, hop).wait_send()
                spread_b(p, hop).wait_send()
                spread_a(p, hop).wait_send()
        done.wait()

    def kernel(part_in, a, b, c, d, out_ref, weights_ref, part_ref, part_sem, *scratch):
        weights = reduce_steps(
            (a, b, c, d), scratch[:4], scratch[4], weights_ref, *scratch[16:]
        )
        blocks_back = collect_steps(part_in, part_ref, part_sem, out_ref, *scratch[5:16])
        for step in "wbwwbwbbwbwwwbwbw":
            next(weights if step == "w" else blocks_back, None)

    shape = lambda *s: pltpu.VMEM(s + (rows, width), partial.dtype)
    bf = lambda *s: pltpu.VMEM(s + (block, width), BF16)
    dma = lambda *s: pltpu.SemaphoreType.DMA(s)
    vmem = pl.BlockSpec(memory_space=pltpu.VMEM)
    past_grad, weights = pl.pallas_call(
        kernel,
        out_shape=(
            jax.ShapeDtypeStruct((blocks, rows, width), partial.dtype),
            jax.ShapeDtypeStruct((2 * half_w, block, width), BF16),
        ),
        in_specs=[pl.BlockSpec(memory_space=pl.ANY)] * 5,
        out_specs=(vmem, pl.BlockSpec(memory_space=pl.ANY)),
        scratch_shapes=[
            shape(groups, blocks), pltpu.SemaphoreType.DMA,
            *[pltpu.VMEM(a.shape, a.dtype) for a in grads], dma(4),
            shape(2, blocks), shape(2, blocks), shape(2, 2, blocks), shape(blocks), shape(blocks),
            dma(2, 4), dma(2, 4), dma(2, 4, 2), dma(2, 4, 2), dma(4), dma(4),
            pltpu.VMEM((half_w, block, width), F32),
            bf(half_w), bf(half_w), bf(half_w), bf(3, 3, 4), bf(3, 4), bf(3, 3), bf(3, 4), bf(3, 4),
            bf(2 * half_w),
            dma(3), dma(3), dma(5, 3, 3), dma(5, 3, 3), dma(3), dma(3), pltpu.SemaphoreType.DMA,
        ],
        compiler_params=pltpu.CompilerParams(
            collective_id=2, has_side_effects=True, vmem_limit_bytes=62 << 20
        ),
        name="collect",
    )(partial, *grads)
    return past_grad, weights.reshape(4, w_rows, width)


def scatter_sum(source, target, used, outputs):
    count, rows, width = source.shape
    step = 8

    def kernel(target_ref, used_ref, source_ref, out_ref, acc):
        t = pl.program_id(0)

        @pl.when(t == 0)
        def _():
            acc[...] = jnp.zeros_like(acc)

        for j in range(step):
            @pl.when(used_ref[t * step + j] > 0)
            def _():
                m = target_ref[t * step + j]
                acc[m] = acc[m] + source_ref[j].astype(F32)

        @pl.when(t == pl.num_programs(0) - 1)
        def _():
            out_ref[...] = acc[...].astype(out_ref.dtype)

    return pl.pallas_call(
        kernel,
        out_shape=jax.ShapeDtypeStruct((outputs, rows, width), source.dtype),
        grid_spec=pltpu.PrefetchScalarGridSpec(
            num_scalar_prefetch=2,
            grid=(count // step,),
            in_specs=[pl.BlockSpec((step, rows, width), lambda t, *_: (t, 0, 0))],
            out_specs=pl.BlockSpec((outputs, rows, width), lambda t, *_: (0, 0, 0)),
            scratch_shapes=[pltpu.VMEM((outputs, rows, width), F32)],
        ),
        compiler_params=pltpu.CompilerParams(vmem_limit_bytes=48 << 20),
        name="scatter_sum",
    )(target, used, source)


def layer(position, live, arrived, tokens, grad_out, w_query, w_pair, w_out, slots):
    patches, block, width = tokens.shape
    requests = position.shape[0] // patches
    far = requests * block
    rows = block + far
    chunks = 1
    chunk = far // chunks
    pairs = width // 128
    parts = requests + 1

    def kernel(
        position_ref, live_ref, arrived_ref, tokens_ref, grad_ref, wq_ref, wkv_ref, wo_ref,
        attn_ref, tokgrad_ref, fargrad_ref, x_ref, dkv_ref, dq_ref, mixed_ref,
        key_s, val_s, q_s, up_s, s_s, dp_s, pb_s, ds_s, fg_s, in_sem, out_sem,
    ):
        p = pl.program_id(0)

        def fetch(r):
            return pltpu.make_async_copy(
                arrived_ref.at[position_ref[p * requests + r]],
                x_ref.at[0, pl.ds(block + r * block, block)],
                in_sem.at[r],
            )

        for r in range(requests):
            fetch(r).start()
        tok = tokens_ref[0]
        x_ref[0, 0:block] = tok
        q_s[...] = mm(tok, wq_ref[...]).astype(BF16)
        own = mm(tok, wkv_ref[...]).astype(BF16)
        key_s[0:block] = own[:, :width]
        val_s[0:block] = own[:, width:]
        up_s[...] = mm(grad_ref[0], wo_ref[...], NT).astype(BF16)
        for r in range(requests):
            fetch(r).wait()

        @pl.loop(0, chunks)
        def _(c):
            at = pl.multiple_of(block + c * chunk, 128)
            x = x_ref[0, pl.ds(at, chunk)]
            key_s[pl.ds(at, chunk)] = mm(x, wkv_ref[:, :width]).astype(BF16)
            val_s[pl.ds(at, chunk)] = mm(x, wkv_ref[:, width:]).astype(BF16)

        low = lax.broadcasted_iota(jnp.int32, (block, 128), 1) < HD
        zero = jnp.zeros((block, 128), BF16)

        @pl.loop(0, pairs)
        def _(j):
            lanes = pl.ds(pl.multiple_of(j * 128, 128), 128)
            k = key_s[:, lanes]
            v = val_s[:, lanes]
            q = q_s[:, lanes] * jnp.asarray(1.0 / math.sqrt(HD), BF16)
            u = up_s[:, lanes]
            q2 = jnp.concatenate([jnp.where(low, q, zero), jnp.where(low, zero, q)], axis=0)
            u2 = jnp.concatenate([jnp.where(low, u, zero), jnp.where(low, zero, u)], axis=0)
            s_s[...] = mm(k, q2, NT)
            dp_s[...] = mm(v, u2, NT)

            def bias(r):
                dead = live_ref[p * requests + jnp.maximum(r - 1, 0)] == 0
                return jnp.where((r > 0) & dead, -jnp.inf, 0.0).astype(F32)

            def part(r):
                return pl.ds(pl.multiple_of(r * block, block), block)

            def largest(r, m):
                s = s_s[part(r)] + bias(r)
                return jnp.maximum(m, jnp.max(s.reshape(block // 8, 8, 2 * block), axis=0))

            m = lax.fori_loop(0, parts, largest, jnp.full((8, 2 * block), -jnp.inf, F32), unroll=True)
            m = jnp.max(m, axis=0, keepdims=True)

            def exps(r, carry):
                total, delta = carry
                e = jnp.exp(s_s[part(r)] + bias(r) - m)
                s_s[part(r)] = e
                g = e * dp_s[part(r)]
                fold = lambda t: jnp.sum(t.reshape(block // 8, 8, 2 * block), axis=0)
                return total + fold(e), delta + fold(g)

            nil = jnp.zeros((8, 2 * block), F32)
            total, delta = lax.fori_loop(0, parts, exps, (nil, nil), unroll=True)
            inverse = 1.0 / jnp.sum(total, axis=0, keepdims=True)
            delta = jnp.sum(delta, axis=0, keepdims=True) * inverse

            @pl.loop(0, parts, unroll=True)
            def _(r):
                prob = s_s[part(r)] * inverse
                pb_s[part(r)] = prob.astype(BF16)
                ds_s[part(r)] = (prob * (dp_s[part(r)] - delta)).astype(BF16)

            pb = pb_s[...]
            ds = ds_s[...]
            dkv_ref[0, :, lanes] = mm(ds, q2).astype(BF16)
            dkv_ref[0, :, pl.ds(pl.multiple_of(width + j * 128, 128), 128)] = mm(pb, u2).astype(BF16)
            o = mm(pb, v, TN)
            mixed_ref[0, :, lanes] = jnp.where(low, o[:block], o[block:]).astype(BF16)
            dq = mm(ds, k, TN)
            dq = jnp.where(low, dq[:block], dq[block:]) * (1.0 / math.sqrt(HD))
            dq_ref[0, :, lanes] = dq.astype(BF16)

        attn_ref[0] = mm(mixed_ref[0], wo_ref[...]).astype(BF16)
        tokgrad_ref[0] = (
            mm(dq_ref[0], wq_ref[...], NT) + mm(dkv_ref[0, 0:block], wkv_ref[...], NT)
        ).astype(BF16)

        @pl.loop(0, chunks)
        def _(c):
            at = pl.multiple_of(block + c * chunk, 128)
            g = mm(dkv_ref[0, pl.ds(at, chunk)], wkv_ref[...], NT).astype(BF16)
            fg_s[pl.ds(pl.multiple_of(c * chunk, 128), chunk)] = g

        def put(r):
            return pltpu.make_async_copy(
                fg_s.at[pl.ds(r * block, block)],
                fargrad_ref.at[position_ref[p * requests + r]],
                out_sem.at[r],
            )

        for r in range(requests):
            @pl.when(live_ref[p * requests + r] > 0)
            def _():
                put(r).start()

        for r in range(requests):
            @pl.when(live_ref[p * requests + r] > 0)
            def _():
                put(r).wait()

    per_patch = lambda n, w: pl.BlockSpec((1, n, w), lambda p, *_: (p, 0, 0))
    whole = lambda a: pl.BlockSpec(a.shape, lambda p, *_: (0, 0), pipeline_mode=pl.Buffered(1))
    hbm = pl.BlockSpec(memory_space=pl.ANY)
    shape = lambda *s: jax.ShapeDtypeStruct(s, BF16)
    return pl.pallas_call(
        kernel,
        out_shape=(
            shape(patches, block, width),
            shape(patches, block, width),
            shape(slots, block, width),
            shape(patches, rows, width),
            shape(patches, rows, 2 * width),
            shape(patches, block, width),
            shape(patches, block, width),
        ),
        grid_spec=pltpu.PrefetchScalarGridSpec(
            num_scalar_prefetch=2,
            grid=(patches,),
            in_specs=[
                hbm, per_patch(block, width), per_patch(block, width),
                whole(w_query), whole(w_pair), whole(w_out),
            ],
            out_specs=(
                per_patch(block, width), per_patch(block, width), hbm, per_patch(rows, width),
                per_patch(rows, 2 * width), per_patch(block, width), per_patch(block, width),
            ),
            scratch_shapes=[
                pltpu.VMEM((rows, width), BF16),
                pltpu.VMEM((rows, width), BF16),
                pltpu.VMEM((block, width), BF16),
                pltpu.VMEM((block, width), BF16),
                pltpu.VMEM((rows, 2 * block), F32),
                pltpu.VMEM((rows, 2 * block), F32),
                pltpu.VMEM((rows, 2 * block), BF16),
                pltpu.VMEM((rows, 2 * block), BF16),
                pltpu.VMEM((far, width), BF16),
                pltpu.SemaphoreType.DMA((requests,)),
                pltpu.SemaphoreType.DMA((requests,)),
            ],
        ),
        compiler_params=pltpu.CompilerParams(vmem_limit_bytes=60 << 20),
        name="layer",
    )(position, live, arrived, tokens, grad_out, w_query, w_pair, w_out)


def body(
    query_tokens, past_tokens, source_dev, source_slot, kept, w_query, w_key, w_value, w_out,
    grad_out,
):
    _, patches, block, width = query_tokens.shape
    tokens, grads, past = query_tokens[0], grad_out[0], past_tokens[0]
    peers = lax.axis_size("patch")
    y, x, z, _ = place()
    per_device = patches * source_dev.shape[1] * source_dev.shape[2]
    blocks = past.shape[0]

    grid = lambda a: a.reshape(4, 2, 4, per_device)
    near = lambda a: jnp.concatenate([grid(a)[y, x], grid(a)[:, x, z]], axis=0)
    owner, slot, kept = (a.reshape(peers, per_device) for a in (source_dev, source_slot, kept))
    from_y, half, from_z = owner // 8, (owner // 4) % 2, owner % 4
    key = half * 4 + jnp.where(half == 0, from_z, from_y)
    number = jnp.where(half == 0, from_y, from_z) * blocks + slot
    key = jnp.where(kept > 0, key, 8)
    most = jnp.max(jnp.sum((key[:, None, :] == jnp.arange(8)[None, :, None]).astype(jnp.int32), axis=2))
    key, number = near(key), near(number)
    order = jnp.arange(per_device)
    matches = (key[:, :, None] == key[:, None, :]) & (order[:, None] > order[None, :])
    rank = jnp.sum(matches.astype(jnp.int32), axis=2)
    chosen_here = jnp.where(jnp.arange(8) < 4, z, 4 + y)
    live = grid(kept)[y, x, z]
    w_pair = jnp.concatenate([w_key, w_value], axis=1)
    flat = lambda a: a.reshape(-1, a.shape[-1])

    def exchange(cap, ident):
        hit = (rank[:, :, None] == jnp.arange(cap)) & (key == chosen_here[:, None])[:, :, None]
        table = jnp.sum(jnp.where(hit, number[:, :, None], 0), axis=1)
        used = jnp.sum(hit.astype(jnp.int32), axis=1).reshape(-1)
        target = (table + jnp.where(jnp.arange(8) < 4, 0, 4 * blocks)[:, None]).reshape(-1)
        mine = jnp.where(live > 0, key[z] * cap + rank[z], 0)
        arrived = spread(past, table.reshape(-1), ident)
        attn, token_grad, far_grad, seen, dkv, dq, mixed = layer(
            mine, live, arrived, tokens, grads, w_query, w_pair, w_out, 8 * cap
        )
        returned, *weight_grads = send_back(
            far_grad, flat(tokens), flat(grads), flat(seen), flat(dkv), flat(dq), flat(mixed), ident + 1
        )
        partial = scatter_sum(returned, target, used, 8 * blocks)
        return attn, token_grad, partial, tuple(weight_grads)

    attn, token_grad, partial, weight_grads = lax.cond(
        most <= 6, lambda: exchange(6, 0), lambda: exchange(8, 3)
    )
    scale = 1.0 / math.sqrt(lax.axis_size("dp") * peers * patches * block)
    past_grad, weights = collect(partial.reshape((8,) + past.shape), weight_grads, scale)
    weights = weights.astype(F32)
    return (
        attn[None],
        token_grad[None],
        past_grad[None],
        weights[0],
        weights[1],
        weights[2],
        weights[3],
    )


def solution(mesh):
    split = P("dp", "patch", None, None)
    return jax.shard_map(
        body,
        mesh=mesh,
        in_specs=(split, split, P(), P(), P(), P(), P(), P(), P(), split),
        out_specs=(split, split, split, P(), P(), P(), P()),
        check_vma=False,
    )
```

```python
import math

import jax
import jax.numpy as jnp
from jax import lax
from jax.experimental import pallas as pl
from jax.experimental.pallas import tpu as pltpu
from jax.sharding import PartitionSpec as P

H = 12
HD = 64
F32 = jnp.float32
MESH = pl.DeviceIdType.MESH
BF16 = jnp.bfloat16
NN = (((1,), (0,)), ((), ()))
NT = (((1,), (1,)), ((), ()))
TN = (((0,), (0,)), ((), ()))


def mm(a, b, dims=NN):
    return lax.dot_general(a, b, dims, preferred_element_type=F32)


def place():
    device = lax.axis_index("patch")
    return device // 8, (device // 4) % 2, device % 4, lax.axis_index("dp")


def step_id(y, x, z, dim, hop):
    return ((y + hop * (1 - dim)) % 4) * 8 + x * 4 + (z + hop * dim) % 4


def meet(y, x, z, dp, across):
    barrier = pltpu.get_barrier_semaphore()
    ids = [step_id(y, x, z, dim, hop) for dim in (0, 1) for hop in (1, 2, 3)]
    if across:
        ids.append(y * 8 + (1 - x) * 4 + z)
    for other in ids:
        pl.semaphore_signal(barrier, 1, device_id=(dp, other), device_id_type=MESH)
    pl.semaphore_wait(barrier, len(ids))


def spread(past, table, cap, ident):
    blocks, rows, width = past.shape
    parts = 4
    chunk = blocks // parts

    def kernel(
        table_ref, past_ref, out_ref, have_a, have_b, sel_a, sel_b,
        in_sem, x_send, x_recv, g_send, g_recv, e_send, e_recv, own_sem,
    ):
        y, x, z, dp = place()
        pos = lambda dim, hop=0: (y * (1 - dim) + z * dim + hop) % 4
        have, sel = (have_a, have_b), (sel_a, sel_b)
        half = (x, 1 - x)

        def region(t, hop, c):
            return have[t].at[pl.ds(pos(half[t], hop) * blocks + c * chunk, chunk)]

        local = pltpu.make_async_copy(
            past_ref, have_a.at[pl.ds(pos(half[0]) * blocks, blocks)], in_sem
        )
        local.start()
        meet(y, x, z, dp, True)

        def cross(c):
            at = pl.ds(pos(half[0]) * blocks + c * chunk, chunk)
            return pltpu.make_async_remote_copy(
                past_ref.at[pl.ds(c * chunk, chunk)], have_b.at[at], x_send.at[c], x_recv.at[c],
                device_id=(dp, y * 8 + (1 - x) * 4 + z), device_id_type=MESH,
            )

        def crossed(c):
            at = pl.ds(pos(half[1]) * blocks + c * chunk, chunk)
            return pltpu.make_async_remote_copy(
                past_ref.at[pl.ds(c * chunk, chunk)], have_b.at[at], x_send.at[c], x_recv.at[c],
                device_id=(dp, y * 8 + (1 - x) * 4 + z), device_id_type=MESH,
            )

        turn = (0, 2, 1, 3)
        ways = [(way, 0, c) for c in turn for way in ((1, 3) if c < 2 else (3, 1))]
        ways += [(1, 3, c) if c < 2 else (3, 1, c) for c in turn]

        def go(t, n):
            way, owner, c = ways[n]
            return pltpu.make_async_remote_copy(
                region(t, owner, c), region(t, owner, c), g_send.at[t, n], g_recv.at[t, n],
                device_id=(dp, step_id(y, x, z, half[t], way)), device_id_type=MESH,
            )

        def came(t, n):
            way, owner, c = ways[n]
            owner = (owner - way) % 4
            return pltpu.make_async_remote_copy(
                region(t, owner, c), region(t, owner, c), g_send.at[t, n], g_recv.at[t, n],
                device_id=(dp, step_id(y, x, z, half[t], way)), device_id_type=MESH,
            )

        def swap(t, hop, arriving=False):
            h = half[t]
            at = h * 4 + pos(1 - h, -hop if arriving else 0)
            return pltpu.make_async_remote_copy(
                sel[t].at[hop], out_ref.at[pl.ds(at * cap, cap)],
                e_send.at[t, hop - 1], e_recv.at[t, hop - 1],
                device_id=(dp, step_id(y, x, z, 1 - h, hop)), device_id_type=MESH,
            )

        def keep(t):
            h = half[t]
            at = h * 4 + pos(1 - h)
            return pltpu.make_async_copy(
                sel[t].at[0], out_ref.at[pl.ds(at * cap, cap)], own_sem.at[t]
            )

        def choose(t):
            h = half[t]
            for hop in (2, 1, 3, 0):
                row = h * 4 + pos(1 - h, hop)

                @pl.loop(0, cap)
                def _(s):
                    sel[t][hop, s] = have[t][table_ref[row * cap + s]]

                if hop:
                    swap(t, hop).start()
                else:
                    keep(t).start()

        for c in turn:
            cross(c).start()
        local.wait()
        for n in range(2 * parts):
            go(0, n).start()

        def relay(t, i):
            came(t, 2 * i).wait_recv()
            go(t, 2 * parts + i).start()

        for i in range(parts):
            crossed(turn[i]).wait_recv()
            go(1, 2 * i).start()
            go(1, 2 * i + 1).start()
            relay(0, i)
        for i in range(parts):
            relay(1, i)
        for t in (0, 1):
            for n in range(2 * parts):
                if n % 2:
                    came(t, n).wait_recv()
            for n in range(2 * parts, 3 * parts):
                came(t, n).wait_recv()
        choose(0)
        choose(1)
        for t in (0, 1):
            for hop in (1, 2, 3):
                swap(t, hop, True).wait_recv()
            keep(t).wait()
        for c in turn:
            cross(c).wait_send()
        for t in (0, 1):
            for n in range(3 * parts):
                go(t, n).wait_send()
            for hop in (1, 2, 3):
                swap(t, hop).wait_send()

    return pl.pallas_call(
        kernel,
        out_shape=jax.ShapeDtypeStruct((table.shape[0], rows, width), past.dtype),
        in_specs=[pl.BlockSpec(memory_space=pltpu.SMEM), pl.BlockSpec(memory_space=pl.ANY)],
        out_specs=pl.BlockSpec(memory_space=pl.ANY),
        scratch_shapes=[
            pltpu.VMEM((4 * blocks, rows, width), past.dtype),
            pltpu.VMEM((4 * blocks, rows, width), past.dtype),
            pltpu.VMEM((4, cap, rows, width), past.dtype),
            pltpu.VMEM((4, cap, rows, width), past.dtype),
            pltpu.SemaphoreType.DMA,
            pltpu.SemaphoreType.DMA((parts,)),
            pltpu.SemaphoreType.DMA((parts,)),
            pltpu.SemaphoreType.DMA((2, 3 * parts)),
            pltpu.SemaphoreType.DMA((2, 3 * parts)),
            pltpu.SemaphoreType.DMA((2, 3)),
            pltpu.SemaphoreType.DMA((2, 3)),
            pltpu.SemaphoreType.DMA((2,)),
        ],
        compiler_params=pltpu.CompilerParams(
            collective_id=ident, has_side_effects=True, vmem_limit_bytes=48 << 20
        ),
        name="spread",
    )(table, past)


def send_back(grads, tokens, grad_out, seen, dkv, dq, mixed, cap, ident):
    _, rows, width = grads.shape
    total = seen.shape[0]
    chunk = total // 8

    def kernel(
        grad_ref, tok_in, gout_in, seen_in, dkv_in, dq_in, mixed_in,
        out_ref, wq_ref, wk_ref, wv_ref, wo_ref, own, send, recv, own_sem,
        tok_ref, gout_ref, seen_ref, dkv_ref, dq_ref, mixed_ref, op_sem,
    ):
        pairs = (
            (tok_in, tok_ref), (dq_in, dq_ref), (mixed_in, mixed_ref), (gout_in, gout_ref),
            (seen_in, seen_ref), (dkv_in, dkv_ref),
        )
        operands = [pltpu.make_async_copy(a, b, op_sem.at[i]) for i, (a, b) in enumerate(pairs)]
        y, x, z, dp = place()
        pos = lambda dim, hop=0: (y * (1 - dim) + z * dim + hop) % 4
        part = lambda ref, at: ref.at[pl.ds(at * cap, cap)]

        def swap(h, hop, arriving=False):
            return pltpu.make_async_remote_copy(
                part(grad_ref, h * 4 + pos(1 - h, hop)),
                part(out_ref, h * 4 + pos(1 - h, -hop if arriving else 0)),
                send.at[h, hop - 1], recv.at[h, hop - 1],
                device_id=(dp, step_id(y, x, z, 1 - h, hop)), device_id_type=MESH,
            )

        def load(h):
            return pltpu.make_async_copy(
                part(grad_ref, h * 4 + pos(1 - h)), own.at[h], own_sem.at[h]
            )

        def store(h):
            return pltpu.make_async_copy(
                own.at[h], part(out_ref, h * 4 + pos(1 - h)), own_sem.at[h]
            )

        for h in (0, 1):
            load(h).start()
        meet(y, x, z, dp, False)
        for hop in (2, 1, 3):
            for h in (0, 1):
                swap(h, hop).start()
        for h in (0, 1):
            load(h).wait()
            store(h).start()
        for operand in operands:
            operand.start()
        for operand in operands:
            operand.wait()
        wq_ref[...] = mm(tok_ref[...], dq_ref[...], TN)
        wo_ref[...] = mm(mixed_ref[...], gout_ref[...], TN)
        wk_ref[...] = jnp.zeros_like(wk_ref)
        wv_ref[...] = jnp.zeros_like(wv_ref)

        @pl.loop(0, total // chunk)
        def _(n):
            at = pl.ds(pl.multiple_of(n * chunk, 16), chunk)
            left = seen_ref[at]
            wk_ref[...] += mm(left, dkv_ref[at, :width], TN)
            wv_ref[...] += mm(left, dkv_ref[at, width:], TN)

        for h in (0, 1):
            store(h).wait()
            for hop in (1, 2, 3):
                swap(h, hop, True).wait_recv()
        for h in (0, 1):
            for hop in (1, 2, 3):
                swap(h, hop).wait_send()

    return pl.pallas_call(
        kernel,
        out_shape=(jax.ShapeDtypeStruct(grads.shape, grads.dtype),)
        + (jax.ShapeDtypeStruct((width, width), F32),) * 4,
        in_specs=[pl.BlockSpec(memory_space=pl.ANY)] * 7,
        out_specs=(pl.BlockSpec(memory_space=pl.ANY),) + (pl.BlockSpec(memory_space=pltpu.VMEM),) * 4,
        scratch_shapes=[
            pltpu.VMEM((2, cap, rows, width), grads.dtype),
            pltpu.SemaphoreType.DMA((2, 3)),
            pltpu.SemaphoreType.DMA((2, 3)),
            pltpu.SemaphoreType.DMA((2,)),
        ]
        + [pltpu.VMEM(a.shape, a.dtype) for a in (tokens, grad_out, seen, dkv, dq, mixed)]
        + [pltpu.SemaphoreType.DMA((6,))],
        compiler_params=pltpu.CompilerParams(
            collective_id=ident, has_side_effects=True, vmem_limit_bytes=56 << 20
        ),
        name="send_back",
    )(grads, tokens, grad_out, seen, dkv, dq, mixed)


def collect(partial, grads, scale):
    groups, blocks, rows, width = partial.shape
    chunk = blocks // 4
    w_rows = grads[0].shape[0]
    block = w_rows // 24
    half_w = 48

    def collect_steps(
        part_in, part_ref, part_sem, out_ref, relay, staged, inward, mine, across,
        r_send, r_recv, d_send, d_recv, x_send, x_recv,
    ):
        y, x, z, dp = place()
        pos = lambda dim, hop=0: (y * (1 - dim) + z * dim + hop) % 4
        half = (1 - x, x)
        held = pltpu.make_async_copy(part_in, part_ref, part_sem)
        held.start()
        ways = (3, 1)
        side_of = (0, 0, 1, 1)

        def row(t, hop):
            return half[t] * 4 + pos(half[t], hop)

        def span(c):
            return pl.ds(c * chunk, chunk)

        def send_to(source, target, sends, recvs, t, side):
            return pltpu.make_async_remote_copy(
                source, target, sends, recvs,
                device_id=(dp, step_id(y, x, z, half[t], ways[side])), device_id_type=MESH,
            )

        def pass_on(t, c):
            return send_to(
                part_in.at[row(t, 2), span(c)], relay.at[t, span(c)],
                r_send.at[t, c], r_recv.at[t, c], t, side_of[c],
            )

        def plain(t, c):
            side = 1 - side_of[c]
            return send_to(
                part_in.at[row(t, ways[side]), span(c)], inward.at[t, side, span(c)],
                d_send.at[t, c, 0], d_recv.at[t, c, 0], t, side,
            )

        def summed(t, c):
            side = side_of[c]
            return send_to(
                staged.at[t, span(c)], inward.at[t, side, span(c)],
                d_send.at[t, c, 1], d_recv.at[t, c, 1], t, side,
            )

        def cross(c):
            return pltpu.make_async_remote_copy(
                mine.at[span(c)], across.at[span(c)], x_send.at[c], x_recv.at[c],
                device_id=(dp, y * 8 + (1 - x) * 4 + z), device_id_type=MESH,
            )

        def final(t, b):
            return (
                part_ref[row(t, 0), b].astype(F32)
                + inward[t, 0, b].astype(F32)
                + inward[t, 1, b].astype(F32)
            )

        def join(t, c):
            pass_on(t, c).wait_recv()

            @pl.loop(c * chunk, c * chunk + chunk)
            def _(b):
                own = part_ref[row(t, ways[side_of[c]]), b]
                staged[t, b] = (own.astype(F32) + relay[t, b].astype(F32)).astype(staged.dtype)

            summed(t, c).start()

        def arrive(t, c):
            plain(t, c).wait_recv()
            summed(t, c).wait_recv()

        def finish_other(c):
            arrive(0, c)

            @pl.loop(c * chunk, c * chunk + chunk)
            def _(b):
                mine[b] = final(0, b).astype(mine.dtype)

            cross(c).start()

        for c in (0, 2, 1, 3):
            for t in (0, 1):
                pass_on(t, c).start()
        for c in (2, 0):
            for t in (0, 1):
                plain(t, c).start()
        yield
        held.wait()
        for c in (0, 2):
            for t in (0, 1):
                join(t, c)
                plain(t, 3 - c).start()
        yield
        for c in (1, 3):
            for t in (0, 1):
                join(t, c)
        yield
        for c in (0, 2):
            finish_other(c)
        yield
        for c in (1, 3):
            finish_other(c)
        yield
        for c in (0, 2, 1, 3):
            arrive(1, c)
            cross(c).wait_recv()

            @pl.loop(c * chunk, c * chunk + chunk)
            def _(b):
                out_ref[b] = (final(1, b) + across[b].astype(F32)).astype(out_ref.dtype)

        yield
        for c in range(4):
            cross(c).wait_send()
            for t in (0, 1):
                pass_on(t, c).wait_send()
                plain(t, c).wait_send()
                summed(t, c).wait_send()

    def reduce_steps(
        given, refs, grad_sem, out_ref, acc, stage, peer, mid, in_a, mid_b, in_b, in_c, got_b, full,
        core_send, core_recv, send, recv, back_send, back_recv, out_sem,
    ):
        y, x_low, z, dp = place()
        core = dp % 2
        spot = {"x": (dp // 2) * 2 + x_low, "y": y, "z": z}
        orders = ("xyz", "yzx", "zxy")
        a_ref, b_ref, c_ref, d_ref = refs
        loads = [pltpu.make_async_copy(given[i], refs[i], grad_sem.at[i]) for i in range(4)]
        for load in loads:
            load.start()

        def there(axis, hop):
            at = dict(spot)
            at[axis] = (at[axis] + hop) % 4
            return (
                (at["x"] // 2) * 2 + core,
                at["y"] * 8 + (at["x"] % 2) * 4 + at["z"],
            )

        other = (dp + 1 - 2 * core, y * 8 + x_low * 4 + z)
        barrier = pltpu.get_barrier_semaphore()
        for axis in "xyz":
            for hop in (1, 2, 3):
                pl.semaphore_signal(barrier, 1, device_id=there(axis, hop), device_id_type=MESH)
        pl.semaphore_signal(barrier, 1, device_id=other, device_id_type=MESH)
        pl.semaphore_wait(barrier, 10)
        yield
        for load in loads:
            load.wait()

        def take(keep, give):
            for i in (0, 1):
                @pl.loop(0, half_w // 2)
                def _(n):
                    at = pl.ds(pl.multiple_of(n * block, block), block)
                    stage[i * (half_w // 2) + n] = (give[i][at] * scale).astype(BF16)
                    acc[i * (half_w // 2) + n] = keep[i][at] * scale

        @pl.when(core == 0)
        def _():
            take((a_ref, b_ref), (c_ref, d_ref))

        @pl.when(core == 1)
        def _():
            take((c_ref, d_ref), (a_ref, b_ref))

        def pair(p):
            at = pl.ds(p * 16, 16)
            return pltpu.make_async_remote_copy(
                stage.at[at], peer.at[at], core_send.at[p], core_recv.at[p],
                device_id=other, device_id_type=MESH,
            )

        def copy(source, target, phase, p, hop, sems=None):
            s, r = sems or (send, recv)
            return pltpu.make_async_remote_copy(
                source, target, s.at[phase, p, hop - 1], r.at[phase, p, hop - 1],
                device_id=there(orders[p][(0, 1, 2, 1, 0)[phase]], hop), device_id_type=MESH,
            )

        def at_axis(p, phase, hop=0):
            return (spot[orders[p][phase]] + hop) % 4

        def scatter_a(p, hop):
            at = pl.ds(p * 16 + at_axis(p, 0, hop) * 4, 4)
            return copy(mid.at[at], in_a.at[p, hop - 1], 0, p, hop)

        def scatter_b(p, hop):
            return copy(mid_b.at[p, at_axis(p, 1, hop)], in_b.at[p, hop - 1], 1, p, hop)

        def swap_c(p, hop, arriving=False):
            to = at_axis(p, 2, -hop if arriving else 0)
            return copy(in_c.at[p, at_axis(p, 2)], in_c.at[p, to], 2, p, hop)

        def spread_b(p, hop, arriving=False):
            to = at_axis(p, 1, -hop if arriving else 0)
            return copy(got_b.at[p, at_axis(p, 1)], got_b.at[p, to], 3, p, hop)

        def spread_a(p, hop, arriving=False):
            row = lambda back: pl.ds(core * half_w + p * 16 + at_axis(p, 0, back) * 4, 4)
            return copy(
                full.at[row(0)], full.at[row(-hop if arriving else 0)], 4, p, hop
            )

        def final(p, arriving=False):
            side = 1 - core if arriving else core
            at = pl.ds(side * half_w + p * 16, 16)
            return pltpu.make_async_remote_copy(
                full.at[at], full.at[at], back_send.at[p], back_recv.at[p],
                device_id=other, device_id_type=MESH,
            )

        hops = (2, 1, 3)
        for p in range(3):
            pair(p).start()
        yield
        for p in range(3):
            pair(p).wait_recv()

            @pl.loop(0, 16)
            def _(n):
                total = acc[p * 16 + n] + peer[p * 16 + n].astype(F32)
                acc[p * 16 + n] = total
                mid[p * 16 + n] = total.astype(BF16)

            for hop in hops:
                scatter_a(p, hop).start()
        yield
        for p in range(3):
            for hop in hops:
                scatter_a(p, hop).wait_recv()

            @pl.loop(0, 4)
            def _(n):
                at = p * 16 + at_axis(p, 0) * 4 + n
                total = acc[at]
                for i in range(3):
                    total = total + in_a[p, i, n].astype(F32)
                acc[at] = total
                mid_b[p, n] = total.astype(BF16)

            for hop in hops:
                scatter_b(p, hop).start()
        yield
        for p in range(3):
            for hop in hops:
                scatter_b(p, hop).wait_recv()
            total = acc[p * 16 + at_axis(p, 0) * 4 + at_axis(p, 1)]
            for i in range(3):
                total = total + in_b[p, i].astype(F32)
            in_c[p, at_axis(p, 2)] = total.astype(BF16)
            for hop in hops:
                swap_c(p, hop).start()
        yield
        for p in range(3):
            for hop in hops:
                swap_c(p, hop, True).wait_recv()
            total = in_c[p, 0].astype(F32)
            for i in range(1, 4):
                total = total + in_c[p, i].astype(F32)
            got_b[p, at_axis(p, 1)] = total.astype(BF16)
            for hop in hops:
                spread_b(p, hop).start()
        yield
        for p in range(3):
            for hop in hops:
                spread_b(p, hop, True).wait_recv()

            @pl.loop(0, 4)
            def _(n):
                full[core * half_w + p * 16 + at_axis(p, 0) * 4 + n] = got_b[p, n]

            for hop in hops:
                spread_a(p, hop).start()
        yield
        for p in range(3):
            for hop in hops:
                spread_a(p, hop, True).wait_recv()
            final(p).start()
        yield
        for p in range(3):
            final(p, True).wait_recv()
        done = pltpu.make_async_copy(full, out_ref, out_sem)
        done.start()
        yield
        for p in range(3):
            pair(p).wait_send()
            final(p).wait_send()
            for hop in hops:
                scatter_a(p, hop).wait_send()
                scatter_b(p, hop).wait_send()
                swap_c(p, hop).wait_send()
                spread_b(p, hop).wait_send()
                spread_a(p, hop).wait_send()
        done.wait()

    def kernel(part_in, a, b, c, d, out_ref, weights_ref, part_ref, part_sem, *scratch):
        weights = reduce_steps(
            (a, b, c, d), scratch[:4], scratch[4], weights_ref, *scratch[16:]
        )
        blocks_back = collect_steps(part_in, part_ref, part_sem, out_ref, *scratch[5:16])
        for step in "wbwwbwbbwbwwwbwbw":
            next(weights if step == "w" else blocks_back, None)

    shape = lambda *s: pltpu.VMEM(s + (rows, width), partial.dtype)
    bf = lambda *s: pltpu.VMEM(s + (block, width), BF16)
    dma = lambda *s: pltpu.SemaphoreType.DMA(s)
    vmem = pl.BlockSpec(memory_space=pltpu.VMEM)
    past_grad, weights = pl.pallas_call(
        kernel,
        out_shape=(
            jax.ShapeDtypeStruct((blocks, rows, width), partial.dtype),
            jax.ShapeDtypeStruct((2 * half_w, block, width), BF16),
        ),
        in_specs=[pl.BlockSpec(memory_space=pl.ANY)] * 5,
        out_specs=(vmem, pl.BlockSpec(memory_space=pl.ANY)),
        scratch_shapes=[
            shape(groups, blocks), pltpu.SemaphoreType.DMA,
            *[pltpu.VMEM(a.shape, a.dtype) for a in grads], dma(4),
            shape(2, blocks), shape(2, blocks), shape(2, 2, blocks), shape(blocks), shape(blocks),
            dma(2, 4), dma(2, 4), dma(2, 4, 2), dma(2, 4, 2), dma(4), dma(4),
            pltpu.VMEM((half_w, block, width), F32),
            bf(half_w), bf(half_w), bf(half_w), bf(3, 3, 4), bf(3, 4), bf(3, 3), bf(3, 4), bf(3, 4),
            bf(2 * half_w),
            dma(3), dma(3), dma(5, 3, 3), dma(5, 3, 3), dma(3), dma(3), pltpu.SemaphoreType.DMA,
        ],
        compiler_params=pltpu.CompilerParams(
            collective_id=2, has_side_effects=True, vmem_limit_bytes=62 << 20
        ),
        name="collect",
    )(partial, *grads)
    return past_grad, weights.reshape(4, w_rows, width)


def scatter_sum(source, target, used, outputs):
    count, rows, width = source.shape
    step = 8

    def kernel(target_ref, used_ref, source_ref, out_ref, acc):
        t = pl.program_id(0)

        @pl.when(t == 0)
        def _():
            acc[...] = jnp.zeros_like(acc)

        for j in range(step):
            @pl.when(used_ref[t * step + j] > 0)
            def _():
                m = target_ref[t * step + j]
                acc[m] = acc[m] + source_ref[j].astype(F32)

        @pl.when(t == pl.num_programs(0) - 1)
        def _():
            out_ref[...] = acc[...].astype(out_ref.dtype)

    return pl.pallas_call(
        kernel,
        out_shape=jax.ShapeDtypeStruct((outputs, rows, width), source.dtype),
        grid_spec=pltpu.PrefetchScalarGridSpec(
            num_scalar_prefetch=2,
            grid=(count // step,),
            in_specs=[pl.BlockSpec((step, rows, width), lambda t, *_: (t, 0, 0))],
            out_specs=pl.BlockSpec((outputs, rows, width), lambda t, *_: (0, 0, 0)),
            scratch_shapes=[pltpu.VMEM((outputs, rows, width), F32)],
        ),
        compiler_params=pltpu.CompilerParams(vmem_limit_bytes=48 << 20),
        name="scatter_sum",
    )(target, used, source)


def layer(position, live, arrived, tokens, grad_out, w_query, w_pair, w_out, slots):
    patches, block, width = tokens.shape
    requests = position.shape[0] // patches
    far = requests * block
    rows = block + far
    chunks = 1
    chunk = far // chunks
    pairs = width // 128
    parts = requests + 1

    def kernel(
        position_ref, live_ref, arrived_ref, tokens_ref, grad_ref, wq_ref, wkv_ref, wo_ref,
        attn_ref, tokgrad_ref, fargrad_ref, x_ref, dkv_ref, dq_ref, mixed_ref,
        key_s, val_s, q_s, up_s, s_s, dp_s, pb_s, ds_s, fg_s, in_sem, out_sem,
    ):
        p = pl.program_id(0)

        def fetch(r):
            return pltpu.make_async_copy(
                arrived_ref.at[position_ref[p * requests + r]],
                x_ref.at[0, pl.ds(block + r * block, block)],
                in_sem.at[r],
            )

        for r in range(requests):
            fetch(r).start()
        tok = tokens_ref[0]
        x_ref[0, 0:block] = tok
        q_s[...] = mm(tok, wq_ref[...]).astype(BF16)
        own = mm(tok, wkv_ref[...]).astype(BF16)
        key_s[0:block] = own[:, :width]
        val_s[0:block] = own[:, width:]
        up_s[...] = mm(grad_ref[0], wo_ref[...], NT).astype(BF16)
        for r in range(requests):
            fetch(r).wait()

        @pl.loop(0, chunks)
        def _(c):
            at = pl.multiple_of(block + c * chunk, 128)
            x = x_ref[0, pl.ds(at, chunk)]
            key_s[pl.ds(at, chunk)] = mm(x, wkv_ref[:, :width]).astype(BF16)
            val_s[pl.ds(at, chunk)] = mm(x, wkv_ref[:, width:]).astype(BF16)

        low = lax.broadcasted_iota(jnp.int32, (block, 128), 1) < HD
        zero = jnp.zeros((block, 128), BF16)

        @pl.loop(0, pairs)
        def _(j):
            lanes = pl.ds(pl.multiple_of(j * 128, 128), 128)
            k = key_s[:, lanes]
            v = val_s[:, lanes]
            q = q_s[:, lanes] * jnp.asarray(1.0 / math.sqrt(HD), BF16)
            u = up_s[:, lanes]
            q2 = jnp.concatenate([jnp.where(low, q, zero), jnp.where(low, zero, q)], axis=0)
            u2 = jnp.concatenate([jnp.where(low, u, zero), jnp.where(low, zero, u)], axis=0)
            s_s[...] = mm(k, q2, NT)
            dp_s[...] = mm(v, u2, NT)

            def bias(r):
                dead = live_ref[p * requests + jnp.maximum(r - 1, 0)] == 0
                return jnp.where((r > 0) & dead, -jnp.inf, 0.0).astype(F32)

            def part(r):
                return pl.ds(pl.multiple_of(r * block, block), block)

            def largest(r, m):
                s = s_s[part(r)] + bias(r)
                return jnp.maximum(m, jnp.max(s.reshape(block // 8, 8, 2 * block), axis=0))

            m = lax.fori_loop(0, parts, largest, jnp.full((8, 2 * block), -jnp.inf, F32), unroll=True)
            m = jnp.max(m, axis=0, keepdims=True)

            def exps(r, carry):
                total, delta = carry
                e = jnp.exp(s_s[part(r)] + bias(r) - m)
                s_s[part(r)] = e
                g = e * dp_s[part(r)]
                fold = lambda t: jnp.sum(t.reshape(block // 8, 8, 2 * block), axis=0)
                return total + fold(e), delta + fold(g)

            nil = jnp.zeros((8, 2 * block), F32)
            total, delta = lax.fori_loop(0, parts, exps, (nil, nil), unroll=True)
            inverse = 1.0 / jnp.sum(total, axis=0, keepdims=True)
            delta = jnp.sum(delta, axis=0, keepdims=True) * inverse

            @pl.loop(0, parts, unroll=True)
            def _(r):
                prob = s_s[part(r)] * inverse
                pb_s[part(r)] = prob.astype(BF16)
                ds_s[part(r)] = (prob * (dp_s[part(r)] - delta)).astype(BF16)

            pb = pb_s[...]
            ds = ds_s[...]
            dkv_ref[0, :, lanes] = mm(ds, q2).astype(BF16)
            dkv_ref[0, :, pl.ds(pl.multiple_of(width + j * 128, 128), 128)] = mm(pb, u2).astype(BF16)
            o = mm(pb, v, TN)
            mixed_ref[0, :, lanes] = jnp.where(low, o[:block], o[block:]).astype(BF16)
            dq = mm(ds, k, TN)
            dq = jnp.where(low, dq[:block], dq[block:]) * (1.0 / math.sqrt(HD))
            dq_ref[0, :, lanes] = dq.astype(BF16)

        attn_ref[0] = mm(mixed_ref[0], wo_ref[...]).astype(BF16)
        tokgrad_ref[0] = (
            mm(dq_ref[0], wq_ref[...], NT) + mm(dkv_ref[0, 0:block], wkv_ref[...], NT)
        ).astype(BF16)

        @pl.loop(0, chunks)
        def _(c):
            at = pl.multiple_of(block + c * chunk, 128)
            g = mm(dkv_ref[0, pl.ds(at, chunk)], wkv_ref[...], NT).astype(BF16)
            fg_s[pl.ds(pl.multiple_of(c * chunk, 128), chunk)] = g

        def put(r):
            return pltpu.make_async_copy(
                fg_s.at[pl.ds(r * block, block)],
                fargrad_ref.at[position_ref[p * requests + r]],
                out_sem.at[r],
            )

        for r in range(requests):
            @pl.when(live_ref[p * requests + r] > 0)
            def _():
                put(r).start()

        for r in range(requests):
            @pl.when(live_ref[p * requests + r] > 0)
            def _():
                put(r).wait()

    per_patch = lambda n, w: pl.BlockSpec((1, n, w), lambda p, *_: (p, 0, 0))
    whole = lambda a: pl.BlockSpec(a.shape, lambda p, *_: (0, 0), pipeline_mode=pl.Buffered(1))
    hbm = pl.BlockSpec(memory_space=pl.ANY)
    shape = lambda *s: jax.ShapeDtypeStruct(s, BF16)
    return pl.pallas_call(
        kernel,
        out_shape=(
            shape(patches, block, width),
            shape(patches, block, width),
            shape(slots, block, width),
            shape(patches, rows, width),
            shape(patches, rows, 2 * width),
            shape(patches, block, width),
            shape(patches, block, width),
        ),
        grid_spec=pltpu.PrefetchScalarGridSpec(
            num_scalar_prefetch=2,
            grid=(patches,),
            in_specs=[
                hbm, per_patch(block, width), per_patch(block, width),
                whole(w_query), whole(w_pair), whole(w_out),
            ],
            out_specs=(
                per_patch(block, width), per_patch(block, width), hbm, per_patch(rows, width),
                per_patch(rows, 2 * width), per_patch(block, width), per_patch(block, width),
            ),
            scratch_shapes=[
                pltpu.VMEM((rows, width), BF16),
                pltpu.VMEM((rows, width), BF16),
                pltpu.VMEM((block, width), BF16),
                pltpu.VMEM((block, width), BF16),
                pltpu.VMEM((rows, 2 * block), F32),
                pltpu.VMEM((rows, 2 * block), F32),
                pltpu.VMEM((rows, 2 * block), BF16),
                pltpu.VMEM((rows, 2 * block), BF16),
                pltpu.VMEM((far, width), BF16),
                pltpu.SemaphoreType.DMA((requests,)),
                pltpu.SemaphoreType.DMA((requests,)),
            ],
        ),
        compiler_params=pltpu.CompilerParams(vmem_limit_bytes=60 << 20),
        name="layer",
    )(position, live, arrived, tokens, grad_out, w_query, w_pair, w_out)


def body(
    query_tokens, past_tokens, source_dev, source_slot, kept, w_query, w_key, w_value, w_out,
    grad_out,
):
    _, patches, block, width = query_tokens.shape
    tokens, grads, past = query_tokens[0], grad_out[0], past_tokens[0]
    peers = lax.axis_size("patch")
    y, x, z, _ = place()
    per_device = patches * source_dev.shape[1] * source_dev.shape[2]
    blocks = past.shape[0]

    grid = lambda a: a.reshape(4, 2, 4, per_device)
    near = lambda a: jnp.concatenate([grid(a)[y, x], grid(a)[:, x, z]], axis=0)
    owner, slot, kept = (a.reshape(peers, per_device) for a in (source_dev, source_slot, kept))
    from_y, half, from_z = owner // 8, (owner // 4) % 2, owner % 4
    key = half * 4 + jnp.where(half == 0, from_z, from_y)
    number = jnp.where(half == 0, from_y, from_z) * blocks + slot
    key = jnp.where(kept > 0, key, 8)
    most = jnp.max(jnp.sum((key[:, None, :] == jnp.arange(8)[None, :, None]).astype(jnp.int32), axis=2))
    key, number = near(key), near(number)
    order = jnp.arange(per_device)
    matches = (key[:, :, None] == key[:, None, :]) & (order[:, None] > order[None, :])
    rank = jnp.sum(matches.astype(jnp.int32), axis=2)
    chosen_here = jnp.where(jnp.arange(8) < 4, z, 4 + y)
    live = grid(kept)[y, x, z]
    w_pair = jnp.concatenate([w_key, w_value], axis=1)
    flat = lambda a: a.reshape(-1, a.shape[-1])

    few, many = 6, 8
    small = most <= few
    cap = jnp.where(small, few, many)

    def pick(a):
        tight = jnp.pad(a[:, :few].reshape(-1), (0, 8 * (many - few)))
        return jnp.where(small, tight, a.reshape(-1))

    hit = (rank[:, :, None] == jnp.arange(many)) & (key == chosen_here[:, None])[:, :, None]
    table = jnp.sum(jnp.where(hit, number[:, :, None], 0), axis=1)
    used = pick(jnp.sum(hit.astype(jnp.int32), axis=1))
    target = pick(table + jnp.where(jnp.arange(8) < 4, 0, 4 * blocks)[:, None])
    table = pick(table)
    mine = jnp.where(live > 0, key[z] * cap + rank[z], 0)
    arrived = lax.cond(
        small, lambda: spread(past, table, few, 0), lambda: spread(past, table, many, 3)
    )
    attn, token_grad, far_grad, seen, dkv, dq, mixed = layer(
        mine, live, arrived, tokens, grads, w_query, w_pair, w_out, 8 * many
    )
    back = (far_grad, flat(tokens), flat(grads), flat(seen), flat(dkv), flat(dq), flat(mixed))
    returned, *weight_grads = lax.cond(
        small, lambda: send_back(*back, few, 1), lambda: send_back(*back, many, 4)
    )
    partial = scatter_sum(returned, target, used, 8 * blocks)
    scale = 1.0 / math.sqrt(lax.axis_size("dp") * peers * patches * block)
    past_grad, weights = collect(partial.reshape((8,) + past.shape), weight_grads, scale)
    weights = weights.astype(F32)
    return (
        attn[None],
        token_grad[None],
        past_grad[None],
        weights[0],
        weights[1],
        weights[2],
        weights[3],
    )


def solution(mesh):
    split = P("dp", "patch", None, None)
    return jax.shard_map(
        body,
        mesh=mesh,
        in_specs=(split, split, P(), P(), P(), P(), P(), P(), P(), split),
        out_specs=(split, split, split, P(), P(), P(), P()),
        check_vma=False,
    )
```

```python
import math

import jax
import jax.numpy as jnp
from jax import lax
from jax.experimental import pallas as pl
from jax.experimental.pallas import tpu as pltpu
from jax.sharding import PartitionSpec as P

H = 12
HD = 64
F32 = jnp.float32
MESH = pl.DeviceIdType.MESH
BF16 = jnp.bfloat16
NN = (((1,), (0,)), ((), ()))
NT = (((1,), (1,)), ((), ()))
TN = (((0,), (0,)), ((), ()))


def mm(a, b, dims=NN):
    return lax.dot_general(a, b, dims, preferred_element_type=F32)


def place():
    device = lax.axis_index("patch")
    return device // 8, (device // 4) % 2, device % 4, lax.axis_index("dp")


def step_id(y, x, z, dim, hop):
    return ((y + hop * (1 - dim)) % 4) * 8 + x * 4 + (z + hop * dim) % 4


def meet(y, x, z, dp, across):
    barrier = pltpu.get_barrier_semaphore()
    ids = [step_id(y, x, z, dim, hop) for dim in (0, 1) for hop in (1, 2, 3)]
    if across:
        ids.append(y * 8 + (1 - x) * 4 + z)
    for other in ids:
        pl.semaphore_signal(barrier, 1, device_id=(dp, other), device_id_type=MESH)
    pl.semaphore_wait(barrier, len(ids))


def spread(past, table, cap, ident):
    blocks, rows, width = past.shape
    parts = 4
    chunk = blocks // parts

    def kernel(
        table_ref, past_ref, out_ref, have_a, have_b, sel_a, sel_b,
        in_sem, x_send, x_recv, g_send, g_recv, e_send, e_recv, own_sem,
    ):
        y, x, z, dp = place()
        pos = lambda dim, hop=0: (y * (1 - dim) + z * dim + hop) % 4
        have, sel = (have_a, have_b), (sel_a, sel_b)
        half = (x, 1 - x)

        def region(t, hop, c):
            return have[t].at[pl.ds(pos(half[t], hop) * blocks + c * chunk, chunk)]

        local = pltpu.make_async_copy(
            past_ref, have_a.at[pl.ds(pos(half[0]) * blocks, blocks)], in_sem
        )
        local.start()
        meet(y, x, z, dp, True)

        def cross(c):
            at = pl.ds(pos(half[0]) * blocks + c * chunk, chunk)
            return pltpu.make_async_remote_copy(
                past_ref.at[pl.ds(c * chunk, chunk)], have_b.at[at], x_send.at[c], x_recv.at[c],
                device_id=(dp, y * 8 + (1 - x) * 4 + z), device_id_type=MESH,
            )

        def crossed(c):
            at = pl.ds(pos(half[1]) * blocks + c * chunk, chunk)
            return pltpu.make_async_remote_copy(
                past_ref.at[pl.ds(c * chunk, chunk)], have_b.at[at], x_send.at[c], x_recv.at[c],
                device_id=(dp, y * 8 + (1 - x) * 4 + z), device_id_type=MESH,
            )

        turn = (0, 2, 1, 3)
        ways = [(way, 0, c) for c in turn for way in ((1, 3) if c < 2 else (3, 1))]
        ways += [(1, 3, c) if c < 2 else (3, 1, c) for c in turn]

        def go(t, n):
            way, owner, c = ways[n]
            return pltpu.make_async_remote_copy(
                region(t, owner, c), region(t, owner, c), g_send.at[t, n], g_recv.at[t, n],
                device_id=(dp, step_id(y, x, z, half[t], way)), device_id_type=MESH,
            )

        def came(t, n):
            way, owner, c = ways[n]
            owner = (owner - way) % 4
            return pltpu.make_async_remote_copy(
                region(t, owner, c), region(t, owner, c), g_send.at[t, n], g_recv.at[t, n],
                device_id=(dp, step_id(y, x, z, half[t], way)), device_id_type=MESH,
            )

        def swap(t, hop, arriving=False):
            h = half[t]
            at = h * 4 + pos(1 - h, -hop if arriving else 0)
            return pltpu.make_async_remote_copy(
                sel[t].at[hop], out_ref.at[pl.ds(at * cap, cap)],
                e_send.at[t, hop - 1], e_recv.at[t, hop - 1],
                device_id=(dp, step_id(y, x, z, 1 - h, hop)), device_id_type=MESH,
            )

        def keep(t):
            h = half[t]
            at = h * 4 + pos(1 - h)
            return pltpu.make_async_copy(
                sel[t].at[0], out_ref.at[pl.ds(at * cap, cap)], own_sem.at[t]
            )

        def choose(t):
            h = half[t]
            for hop in (2, 1, 3, 0):
                row = h * 4 + pos(1 - h, hop)

                @pl.loop(0, cap)
                def _(s):
                    sel[t][hop, s] = have[t][table_ref[row * cap + s]]

                if hop:
                    swap(t, hop).start()
                else:
                    keep(t).start()

        for c in turn:
            cross(c).start()
        local.wait()
        for n in range(2 * parts):
            go(0, n).start()

        def relay(t, i):
            came(t, 2 * i).wait_recv()
            go(t, 2 * parts + i).start()

        for i in range(parts):
            crossed(turn[i]).wait_recv()
            go(1, 2 * i).start()
            go(1, 2 * i + 1).start()
            relay(0, i)
        for i in range(parts):
            relay(1, i)
        for t in (0, 1):
            for n in range(2 * parts):
                if n % 2:
                    came(t, n).wait_recv()
            for n in range(2 * parts, 3 * parts):
                came(t, n).wait_recv()
        choose(0)
        choose(1)
        for t in (0, 1):
            for hop in (1, 2, 3):
                swap(t, hop, True).wait_recv()
            keep(t).wait()
        for c in turn:
            cross(c).wait_send()
        for t in (0, 1):
            for n in range(3 * parts):
                go(t, n).wait_send()
            for hop in (1, 2, 3):
                swap(t, hop).wait_send()

    return pl.pallas_call(
        kernel,
        out_shape=jax.ShapeDtypeStruct((table.shape[0], rows, width), past.dtype),
        in_specs=[pl.BlockSpec(memory_space=pltpu.SMEM), pl.BlockSpec(memory_space=pl.ANY)],
        out_specs=pl.BlockSpec(memory_space=pl.ANY),
        scratch_shapes=[
            pltpu.VMEM((4 * blocks, rows, width), past.dtype),
            pltpu.VMEM((4 * blocks, rows, width), past.dtype),
            pltpu.VMEM((4, cap, rows, width), past.dtype),
            pltpu.VMEM((4, cap, rows, width), past.dtype),
            pltpu.SemaphoreType.DMA,
            pltpu.SemaphoreType.DMA((parts,)),
            pltpu.SemaphoreType.DMA((parts,)),
            pltpu.SemaphoreType.DMA((2, 3 * parts)),
            pltpu.SemaphoreType.DMA((2, 3 * parts)),
            pltpu.SemaphoreType.DMA((2, 3)),
            pltpu.SemaphoreType.DMA((2, 3)),
            pltpu.SemaphoreType.DMA((2,)),
        ],
        compiler_params=pltpu.CompilerParams(
            collective_id=ident, has_side_effects=True, vmem_limit_bytes=48 << 20
        ),
        name="spread",
    )(table, past)


def send_back(grads, tokens, grad_out, seen, dkv, dq, mixed, cap, ident):
    _, rows, width = grads.shape
    total = seen.shape[0]
    chunk = total // 8

    def kernel(
        grad_ref, tok_in, gout_in, seen_in, dkv_in, dq_in, mixed_in,
        out_ref, wq_ref, wk_ref, wv_ref, wo_ref, own, send, recv, own_sem,
        tok_ref, gout_ref, seen_ref, dkv_ref, dq_ref, mixed_ref, op_sem,
    ):
        pairs = (
            (tok_in, tok_ref), (dq_in, dq_ref), (mixed_in, mixed_ref), (gout_in, gout_ref),
            (seen_in, seen_ref), (dkv_in, dkv_ref),
        )
        operands = [pltpu.make_async_copy(a, b, op_sem.at[i]) for i, (a, b) in enumerate(pairs)]
        y, x, z, dp = place()
        pos = lambda dim, hop=0: (y * (1 - dim) + z * dim + hop) % 4
        part = lambda ref, at: ref.at[pl.ds(at * cap, cap)]

        def swap(h, hop, arriving=False):
            return pltpu.make_async_remote_copy(
                part(grad_ref, h * 4 + pos(1 - h, hop)),
                part(out_ref, h * 4 + pos(1 - h, -hop if arriving else 0)),
                send.at[h, hop - 1], recv.at[h, hop - 1],
                device_id=(dp, step_id(y, x, z, 1 - h, hop)), device_id_type=MESH,
            )

        def load(h):
            return pltpu.make_async_copy(
                part(grad_ref, h * 4 + pos(1 - h)), own.at[h], own_sem.at[h]
            )

        def store(h):
            return pltpu.make_async_copy(
                own.at[h], part(out_ref, h * 4 + pos(1 - h)), own_sem.at[h]
            )

        for h in (0, 1):
            load(h).start()
        meet(y, x, z, dp, False)
        for hop in (2, 1, 3):
            for h in (0, 1):
                swap(h, hop).start()
        for h in (0, 1):
            load(h).wait()
            store(h).start()
        for operand in operands:
            operand.start()
        for operand in operands:
            operand.wait()
        wq_ref[...] = mm(tok_ref[...], dq_ref[...], TN)
        wo_ref[...] = mm(mixed_ref[...], gout_ref[...], TN)
        wk_ref[...] = jnp.zeros_like(wk_ref)
        wv_ref[...] = jnp.zeros_like(wv_ref)

        @pl.loop(0, total // chunk)
        def _(n):
            at = pl.ds(pl.multiple_of(n * chunk, 16), chunk)
            left = seen_ref[at]
            wk_ref[...] += mm(left, dkv_ref[at, :width], TN)
            wv_ref[...] += mm(left, dkv_ref[at, width:], TN)

        for h in (0, 1):
            store(h).wait()
            for hop in (1, 2, 3):
                swap(h, hop, True).wait_recv()
        for h in (0, 1):
            for hop in (1, 2, 3):
                swap(h, hop).wait_send()

    return pl.pallas_call(
        kernel,
        out_shape=(jax.ShapeDtypeStruct(grads.shape, grads.dtype),)
        + (jax.ShapeDtypeStruct((width, width), F32),) * 4,
        in_specs=[pl.BlockSpec(memory_space=pl.ANY)] * 7,
        out_specs=(pl.BlockSpec(memory_space=pl.ANY),) + (pl.BlockSpec(memory_space=pltpu.VMEM),) * 4,
        scratch_shapes=[
            pltpu.VMEM((2, cap, rows, width), grads.dtype),
            pltpu.SemaphoreType.DMA((2, 3)),
            pltpu.SemaphoreType.DMA((2, 3)),
            pltpu.SemaphoreType.DMA((2,)),
        ]
        + [pltpu.VMEM(a.shape, a.dtype) for a in (tokens, grad_out, seen, dkv, dq, mixed)]
        + [pltpu.SemaphoreType.DMA((6,))],
        compiler_params=pltpu.CompilerParams(
            collective_id=ident, has_side_effects=True, vmem_limit_bytes=56 << 20
        ),
        name="send_back",
    )(grads, tokens, grad_out, seen, dkv, dq, mixed)


def collect(partial, grads, scale):
    groups, blocks, rows, width = partial.shape
    chunk = blocks // 4
    w_rows = grads[0].shape[0]
    block = w_rows // 24
    half_w = 48

    def collect_steps(
        part_in, part_ref, part_sem, out_ref, relay, staged, inward, mine, across,
        r_send, r_recv, d_send, d_recv, x_send, x_recv,
    ):
        y, x, z, dp = place()
        pos = lambda dim, hop=0: (y * (1 - dim) + z * dim + hop) % 4
        half = (1 - x, x)
        held = pltpu.make_async_copy(part_in, part_ref, part_sem)
        held.start()
        ways = (3, 1)
        side_of = (0, 0, 1, 1)

        def row(t, hop):
            return half[t] * 4 + pos(half[t], hop)

        def span(c):
            return pl.ds(c * chunk, chunk)

        def send_to(source, target, sends, recvs, t, side):
            return pltpu.make_async_remote_copy(
                source, target, sends, recvs,
                device_id=(dp, step_id(y, x, z, half[t], ways[side])), device_id_type=MESH,
            )

        def pass_on(t, c):
            return send_to(
                part_in.at[row(t, 2), span(c)], relay.at[t, span(c)],
                r_send.at[t, c], r_recv.at[t, c], t, side_of[c],
            )

        def plain(t, c):
            side = 1 - side_of[c]
            return send_to(
                part_in.at[row(t, ways[side]), span(c)], inward.at[t, side, span(c)],
                d_send.at[t, c, 0], d_recv.at[t, c, 0], t, side,
            )

        def summed(t, c):
            side = side_of[c]
            return send_to(
                staged.at[t, span(c)], inward.at[t, side, span(c)],
                d_send.at[t, c, 1], d_recv.at[t, c, 1], t, side,
            )

        def cross(c):
            return pltpu.make_async_remote_copy(
                mine.at[span(c)], across.at[span(c)], x_send.at[c], x_recv.at[c],
                device_id=(dp, y * 8 + (1 - x) * 4 + z), device_id_type=MESH,
            )

        def final(t, b):
            return (
                part_ref[row(t, 0), b].astype(F32)
                + inward[t, 0, b].astype(F32)
                + inward[t, 1, b].astype(F32)
            )

        def join(t, c):
            pass_on(t, c).wait_recv()

            @pl.loop(c * chunk, c * chunk + chunk)
            def _(b):
                own = part_ref[row(t, ways[side_of[c]]), b]
                staged[t, b] = (own.astype(F32) + relay[t, b].astype(F32)).astype(staged.dtype)

            summed(t, c).start()

        def arrive(t, c):
            plain(t, c).wait_recv()
            summed(t, c).wait_recv()

        def finish_other(c):
            arrive(0, c)

            @pl.loop(c * chunk, c * chunk + chunk)
            def _(b):
                mine[b] = final(0, b).astype(mine.dtype)

            cross(c).start()

        for c in (0, 2, 1, 3):
            for t in (0, 1):
                pass_on(t, c).start()
        for c in (2, 0):
            for t in (0, 1):
                plain(t, c).start()
        yield
        held.wait()
        for c in (0, 2):
            for t in (0, 1):
                join(t, c)
                plain(t, 3 - c).start()
        yield
        for c in (1, 3):
            for t in (0, 1):
                join(t, c)
        yield
        for c in (0, 2):
            finish_other(c)
        yield
        for c in (1, 3):
            finish_other(c)
        yield
        for c in (0, 2, 1, 3):
            arrive(1, c)
            cross(c).wait_recv()

            @pl.loop(c * chunk, c * chunk + chunk)
            def _(b):
                out_ref[b] = (final(1, b) + across[b].astype(F32)).astype(out_ref.dtype)

        yield
        for c in range(4):
            cross(c).wait_send()
            for t in (0, 1):
                pass_on(t, c).wait_send()
                plain(t, c).wait_send()
                summed(t, c).wait_send()

    def reduce_steps(
        given, refs, grad_sem, out_ref, acc, stage, peer, mid, in_a, mid_b, in_b, in_c, got_b, full,
        core_send, core_recv, send, recv, back_send, back_recv, out_sem,
    ):
        y, x_low, z, dp = place()
        core = dp % 2
        spot = {"x": (dp // 2) * 2 + x_low, "y": y, "z": z}
        orders = ("xyz", "yzx", "zxy")
        a_ref, b_ref, c_ref, d_ref = refs
        loads = [pltpu.make_async_copy(given[i], refs[i], grad_sem.at[i]) for i in range(4)]
        for load in loads:
            load.start()

        def there(axis, hop):
            at = dict(spot)
            at[axis] = (at[axis] + hop) % 4
            return (
                (at["x"] // 2) * 2 + core,
                at["y"] * 8 + (at["x"] % 2) * 4 + at["z"],
            )

        other = (dp + 1 - 2 * core, y * 8 + x_low * 4 + z)
        barrier = pltpu.get_barrier_semaphore()
        for axis in "xyz":
            for hop in (1, 2, 3):
                pl.semaphore_signal(barrier, 1, device_id=there(axis, hop), device_id_type=MESH)
        pl.semaphore_signal(barrier, 1, device_id=other, device_id_type=MESH)
        pl.semaphore_wait(barrier, 10)
        yield
        for load in loads:
            load.wait()

        def take(keep, give):
            for i in (0, 1):
                @pl.loop(0, half_w // 2)
                def _(n):
                    at = pl.ds(pl.multiple_of(n * block, block), block)
                    stage[i * (half_w // 2) + n] = (give[i][at] * scale).astype(BF16)
                    acc[i * (half_w // 2) + n] = keep[i][at] * scale

        @pl.when(core == 0)
        def _():
            take((a_ref, b_ref), (c_ref, d_ref))

        @pl.when(core == 1)
        def _():
            take((c_ref, d_ref), (a_ref, b_ref))

        def pair(p):
            at = pl.ds(p * 16, 16)
            return pltpu.make_async_remote_copy(
                stage.at[at], peer.at[at], core_send.at[p], core_recv.at[p],
                device_id=other, device_id_type=MESH,
            )

        def copy(source, target, phase, p, hop, sems=None):
            s, r = sems or (send, recv)
            return pltpu.make_async_remote_copy(
                source, target, s.at[phase, p, hop - 1], r.at[phase, p, hop - 1],
                device_id=there(orders[p][(0, 1, 2, 1, 0)[phase]], hop), device_id_type=MESH,
            )

        def at_axis(p, phase, hop=0):
            return (spot[orders[p][phase]] + hop) % 4

        def scatter_a(p, hop):
            at = pl.ds(p * 16 + at_axis(p, 0, hop) * 4, 4)
            return copy(mid.at[at], in_a.at[p, hop - 1], 0, p, hop)

        def scatter_b(p, hop):
            return copy(mid_b.at[p, at_axis(p, 1, hop)], in_b.at[p, hop - 1], 1, p, hop)

        def swap_c(p, hop, arriving=False):
            to = at_axis(p, 2, -hop if arriving else 0)
            return copy(in_c.at[p, at_axis(p, 2)], in_c.at[p, to], 2, p, hop)

        def spread_b(p, hop, arriving=False):
            to = at_axis(p, 1, -hop if arriving else 0)
            return copy(got_b.at[p, at_axis(p, 1)], got_b.at[p, to], 3, p, hop)

        def spread_a(p, hop, arriving=False):
            row = lambda back: pl.ds(core * half_w + p * 16 + at_axis(p, 0, back) * 4, 4)
            return copy(
                full.at[row(0)], full.at[row(-hop if arriving else 0)], 4, p, hop
            )

        def final(p, arriving=False):
            side = 1 - core if arriving else core
            at = pl.ds(side * half_w + p * 16, 16)
            return pltpu.make_async_remote_copy(
                full.at[at], full.at[at], back_send.at[p], back_recv.at[p],
                device_id=other, device_id_type=MESH,
            )

        hops = (2, 1, 3)
        for p in range(3):
            pair(p).start()
        yield
        for p in range(3):
            pair(p).wait_recv()

            @pl.loop(0, 16)
            def _(n):
                total = acc[p * 16 + n] + peer[p * 16 + n].astype(F32)
                acc[p * 16 + n] = total
                mid[p * 16 + n] = total.astype(BF16)

            for hop in hops:
                scatter_a(p, hop).start()
        yield
        for p in range(3):
            for hop in hops:
                scatter_a(p, hop).wait_recv()

            @pl.loop(0, 4)
            def _(n):
                at = p * 16 + at_axis(p, 0) * 4 + n
                total = acc[at]
                for i in range(3):
                    total = total + in_a[p, i, n].astype(F32)
                acc[at] = total
                mid_b[p, n] = total.astype(BF16)

            for hop in hops:
                scatter_b(p, hop).start()
        yield
        for p in range(3):
            for hop in hops:
                scatter_b(p, hop).wait_recv()
            total = acc[p * 16 + at_axis(p, 0) * 4 + at_axis(p, 1)]
            for i in range(3):
                total = total + in_b[p, i].astype(F32)
            in_c[p, at_axis(p, 2)] = total.astype(BF16)
            for hop in hops:
                swap_c(p, hop).start()
        yield
        for p in range(3):
            for hop in hops:
                swap_c(p, hop, True).wait_recv()
            total = in_c[p, 0].astype(F32)
            for i in range(1, 4):
                total = total + in_c[p, i].astype(F32)
            got_b[p, at_axis(p, 1)] = total.astype(BF16)
            for hop in hops:
                spread_b(p, hop).start()
        yield
        for p in range(3):
            for hop in hops:
                spread_b(p, hop, True).wait_recv()

            @pl.loop(0, 4)
            def _(n):
                full[core * half_w + p * 16 + at_axis(p, 0) * 4 + n] = got_b[p, n]

            for hop in hops:
                spread_a(p, hop).start()
        yield
        for p in range(3):
            for hop in hops:
                spread_a(p, hop, True).wait_recv()
            final(p).start()
        yield
        for p in range(3):
            final(p, True).wait_recv()
        done = pltpu.make_async_copy(full, out_ref, out_sem)
        done.start()
        yield
        for p in range(3):
            pair(p).wait_send()
            final(p).wait_send()
            for hop in hops:
                scatter_a(p, hop).wait_send()
                scatter_b(p, hop).wait_send()
                swap_c(p, hop).wait_send()
                spread_b(p, hop).wait_send()
                spread_a(p, hop).wait_send()
        done.wait()

    def kernel(part_in, a, b, c, d, out_ref, weights_ref, part_ref, part_sem, *scratch):
        weights = reduce_steps(
            (a, b, c, d), scratch[:4], scratch[4], weights_ref, *scratch[16:]
        )
        blocks_back = collect_steps(part_in, part_ref, part_sem, out_ref, *scratch[5:16])
        for step in "wbwwbwbbwbwwwbwbw":
            next(weights if step == "w" else blocks_back, None)

    shape = lambda *s: pltpu.VMEM(s + (rows, width), partial.dtype)
    bf = lambda *s: pltpu.VMEM(s + (block, width), BF16)
    dma = lambda *s: pltpu.SemaphoreType.DMA(s)
    vmem = pl.BlockSpec(memory_space=pltpu.VMEM)
    past_grad, weights = pl.pallas_call(
        kernel,
        out_shape=(
            jax.ShapeDtypeStruct((blocks, rows, width), partial.dtype),
            jax.ShapeDtypeStruct((2 * half_w, block, width), BF16),
        ),
        in_specs=[pl.BlockSpec(memory_space=pl.ANY)] * 5,
        out_specs=(vmem, pl.BlockSpec(memory_space=pl.ANY)),
        scratch_shapes=[
            shape(groups, blocks), pltpu.SemaphoreType.DMA,
            *[pltpu.VMEM(a.shape, a.dtype) for a in grads], dma(4),
            shape(2, blocks), shape(2, blocks), shape(2, 2, blocks), shape(blocks), shape(blocks),
            dma(2, 4), dma(2, 4), dma(2, 4, 2), dma(2, 4, 2), dma(4), dma(4),
            pltpu.VMEM((half_w, block, width), F32),
            bf(half_w), bf(half_w), bf(half_w), bf(3, 3, 4), bf(3, 4), bf(3, 3), bf(3, 4), bf(3, 4),
            bf(2 * half_w),
            dma(3), dma(3), dma(5, 3, 3), dma(5, 3, 3), dma(3), dma(3), pltpu.SemaphoreType.DMA,
        ],
        compiler_params=pltpu.CompilerParams(
            collective_id=6, has_side_effects=True, vmem_limit_bytes=62 << 20
        ),
        name="collect",
    )(partial, *grads)
    return past_grad, weights.reshape(4, w_rows, width)


def scatter_sum(source, target, used, outputs):
    count, rows, width = source.shape
    step = 8

    def kernel(target_ref, used_ref, source_ref, out_ref, acc):
        t = pl.program_id(0)

        @pl.when(t == 0)
        def _():
            acc[...] = jnp.zeros_like(acc)

        for j in range(step):
            @pl.when(used_ref[t * step + j] > 0)
            def _():
                m = target_ref[t * step + j]
                acc[m] = acc[m] + source_ref[j].astype(F32)

        @pl.when(t == pl.num_programs(0) - 1)
        def _():
            out_ref[...] = acc[...].astype(out_ref.dtype)

    return pl.pallas_call(
        kernel,
        out_shape=jax.ShapeDtypeStruct((outputs, rows, width), source.dtype),
        grid_spec=pltpu.PrefetchScalarGridSpec(
            num_scalar_prefetch=2,
            grid=(count // step,),
            in_specs=[pl.BlockSpec((step, rows, width), lambda t, *_: (t, 0, 0))],
            out_specs=pl.BlockSpec((outputs, rows, width), lambda t, *_: (0, 0, 0)),
            scratch_shapes=[pltpu.VMEM((outputs, rows, width), F32)],
        ),
        compiler_params=pltpu.CompilerParams(vmem_limit_bytes=48 << 20),
        name="scatter_sum",
    )(target, used, source)


def layer(position, live, arrived, tokens, grad_out, w_query, w_pair, w_out, slots):
    patches, block, width = tokens.shape
    requests = position.shape[0] // patches
    far = requests * block
    rows = block + far
    chunks = 1
    chunk = far // chunks
    pairs = width // 128
    parts = requests + 1

    def kernel(
        position_ref, live_ref, arrived_ref, tokens_ref, grad_ref, wq_ref, wkv_ref, wo_ref,
        attn_ref, tokgrad_ref, fargrad_ref, x_ref, dkv_ref, dq_ref, mixed_ref,
        key_s, val_s, q_s, up_s, s_s, dp_s, pb_s, ds_s, fg_s, in_sem, out_sem,
    ):
        p = pl.program_id(0)

        def fetch(r):
            return pltpu.make_async_copy(
                arrived_ref.at[position_ref[p * requests + r]],
                x_ref.at[0, pl.ds(block + r * block, block)],
                in_sem.at[r],
            )

        for r in range(requests):
            fetch(r).start()
        tok = tokens_ref[0]
        x_ref[0, 0:block] = tok
        q_s[...] = mm(tok, wq_ref[...]).astype(BF16)
        own = mm(tok, wkv_ref[...]).astype(BF16)
        key_s[0:block] = own[:, :width]
        val_s[0:block] = own[:, width:]
        up_s[...] = mm(grad_ref[0], wo_ref[...], NT).astype(BF16)
        for r in range(requests):
            fetch(r).wait()

        @pl.loop(0, chunks)
        def _(c):
            at = pl.multiple_of(block + c * chunk, 128)
            x = x_ref[0, pl.ds(at, chunk)]
            key_s[pl.ds(at, chunk)] = mm(x, wkv_ref[:, :width]).astype(BF16)
            val_s[pl.ds(at, chunk)] = mm(x, wkv_ref[:, width:]).astype(BF16)

        low = lax.broadcasted_iota(jnp.int32, (block, 128), 1) < HD
        zero = jnp.zeros((block, 128), BF16)

        @pl.loop(0, pairs)
        def _(j):
            lanes = pl.ds(pl.multiple_of(j * 128, 128), 128)
            k = key_s[:, lanes]
            v = val_s[:, lanes]
            q = q_s[:, lanes] * jnp.asarray(1.0 / math.sqrt(HD), BF16)
            u = up_s[:, lanes]
            q2 = jnp.concatenate([jnp.where(low, q, zero), jnp.where(low, zero, q)], axis=0)
            u2 = jnp.concatenate([jnp.where(low, u, zero), jnp.where(low, zero, u)], axis=0)
            s_s[...] = mm(k, q2, NT)
            dp_s[...] = mm(v, u2, NT)

            def bias(r):
                dead = live_ref[p * requests + jnp.maximum(r - 1, 0)] == 0
                return jnp.where((r > 0) & dead, -jnp.inf, 0.0).astype(F32)

            def part(r):
                return pl.ds(pl.multiple_of(r * block, block), block)

            def largest(r, m):
                s = s_s[part(r)] + bias(r)
                return jnp.maximum(m, jnp.max(s.reshape(block // 8, 8, 2 * block), axis=0))

            m = lax.fori_loop(0, parts, largest, jnp.full((8, 2 * block), -jnp.inf, F32), unroll=True)
            m = jnp.max(m, axis=0, keepdims=True)

            def exps(r, carry):
                total, delta = carry
                e = jnp.exp(s_s[part(r)] + bias(r) - m)
                s_s[part(r)] = e
                g = e * dp_s[part(r)]
                fold = lambda t: jnp.sum(t.reshape(block // 8, 8, 2 * block), axis=0)
                return total + fold(e), delta + fold(g)

            nil = jnp.zeros((8, 2 * block), F32)
            total, delta = lax.fori_loop(0, parts, exps, (nil, nil), unroll=True)
            inverse = 1.0 / jnp.sum(total, axis=0, keepdims=True)
            delta = jnp.sum(delta, axis=0, keepdims=True) * inverse

            @pl.loop(0, parts, unroll=True)
            def _(r):
                prob = s_s[part(r)] * inverse
                pb_s[part(r)] = prob.astype(BF16)
                ds_s[part(r)] = (prob * (dp_s[part(r)] - delta)).astype(BF16)

            pb = pb_s[...]
            ds = ds_s[...]
            dkv_ref[0, :, lanes] = mm(ds, q2).astype(BF16)
            dkv_ref[0, :, pl.ds(pl.multiple_of(width + j * 128, 128), 128)] = mm(pb, u2).astype(BF16)
            o = mm(pb, v, TN)
            mixed_ref[0, :, lanes] = jnp.where(low, o[:block], o[block:]).astype(BF16)
            dq = mm(ds, k, TN)
            dq = jnp.where(low, dq[:block], dq[block:]) * (1.0 / math.sqrt(HD))
            dq_ref[0, :, lanes] = dq.astype(BF16)

        attn_ref[0] = mm(mixed_ref[0], wo_ref[...]).astype(BF16)
        tokgrad_ref[0] = (
            mm(dq_ref[0], wq_ref[...], NT) + mm(dkv_ref[0, 0:block], wkv_ref[...], NT)
        ).astype(BF16)

        @pl.loop(0, chunks)
        def _(c):
            at = pl.multiple_of(block + c * chunk, 128)
            g = mm(dkv_ref[0, pl.ds(at, chunk)], wkv_ref[...], NT).astype(BF16)
            fg_s[pl.ds(pl.multiple_of(c * chunk, 128), chunk)] = g

        def put(r):
            return pltpu.make_async_copy(
                fg_s.at[pl.ds(r * block, block)],
                fargrad_ref.at[position_ref[p * requests + r]],
                out_sem.at[r],
            )

        for r in range(requests):
            @pl.when(live_ref[p * requests + r] > 0)
            def _():
                put(r).start()

        for r in range(requests):
            @pl.when(live_ref[p * requests + r] > 0)
            def _():
                put(r).wait()

    per_patch = lambda n, w: pl.BlockSpec((1, n, w), lambda p, *_: (p, 0, 0))
    whole = lambda a: pl.BlockSpec(a.shape, lambda p, *_: (0, 0), pipeline_mode=pl.Buffered(1))
    hbm = pl.BlockSpec(memory_space=pl.ANY)
    shape = lambda *s: jax.ShapeDtypeStruct(s, BF16)
    return pl.pallas_call(
        kernel,
        out_shape=(
            shape(patches, block, width),
            shape(patches, block, width),
            shape(slots, block, width),
            shape(patches, rows, width),
            shape(patches, rows, 2 * width),
            shape(patches, block, width),
            shape(patches, block, width),
        ),
        grid_spec=pltpu.PrefetchScalarGridSpec(
            num_scalar_prefetch=2,
            grid=(patches,),
            in_specs=[
                hbm, per_patch(block, width), per_patch(block, width),
                whole(w_query), whole(w_pair), whole(w_out),
            ],
            out_specs=(
                per_patch(block, width), per_patch(block, width), hbm, per_patch(rows, width),
                per_patch(rows, 2 * width), per_patch(block, width), per_patch(block, width),
            ),
            scratch_shapes=[
                pltpu.VMEM((rows, width), BF16),
                pltpu.VMEM((rows, width), BF16),
                pltpu.VMEM((block, width), BF16),
                pltpu.VMEM((block, width), BF16),
                pltpu.VMEM((rows, 2 * block), F32),
                pltpu.VMEM((rows, 2 * block), F32),
                pltpu.VMEM((rows, 2 * block), BF16),
                pltpu.VMEM((rows, 2 * block), BF16),
                pltpu.VMEM((far, width), BF16),
                pltpu.SemaphoreType.DMA((requests,)),
                pltpu.SemaphoreType.DMA((requests,)),
            ],
        ),
        compiler_params=pltpu.CompilerParams(vmem_limit_bytes=60 << 20),
        name="layer",
    )(position, live, arrived, tokens, grad_out, w_query, w_pair, w_out)


def body(
    query_tokens, past_tokens, source_dev, source_slot, kept, w_query, w_key, w_value, w_out,
    grad_out,
):
    _, patches, block, width = query_tokens.shape
    tokens, grads, past = query_tokens[0], grad_out[0], past_tokens[0]
    peers = lax.axis_size("patch")
    y, x, z, _ = place()
    per_device = patches * source_dev.shape[1] * source_dev.shape[2]
    blocks = past.shape[0]

    grid = lambda a: a.reshape(4, 2, 4, per_device)
    near = lambda a: jnp.concatenate([grid(a)[y, x], grid(a)[:, x, z]], axis=0)
    owner, slot, kept = (a.reshape(peers, per_device) for a in (source_dev, source_slot, kept))
    from_y, half, from_z = owner // 8, (owner // 4) % 2, owner % 4
    key = half * 4 + jnp.where(half == 0, from_z, from_y)
    number = jnp.where(half == 0, from_y, from_z) * blocks + slot
    key = jnp.where(kept > 0, key, 8)
    most = jnp.max(jnp.sum((key[:, None, :] == jnp.arange(8)[None, :, None]).astype(jnp.int32), axis=2))
    key, number = near(key), near(number)
    order = jnp.arange(per_device)
    matches = (key[:, :, None] == key[:, None, :]) & (order[:, None] > order[None, :])
    rank = jnp.sum(matches.astype(jnp.int32), axis=2)
    chosen_here = jnp.where(jnp.arange(8) < 4, z, 4 + y)
    live = grid(kept)[y, x, z]
    w_pair = jnp.concatenate([w_key, w_value], axis=1)
    flat = lambda a: a.reshape(-1, a.shape[-1])

    caps = (5, 6, 8)
    many = caps[-1]
    size = (most > caps[0]).astype(jnp.int32) + (most > caps[1]).astype(jnp.int32)
    by_size = lambda options: jnp.where(
        size == 0, options[0], jnp.where(size == 1, options[1], options[2])
    )
    cap = by_size(caps)

    def pick(a):
        return by_size([jnp.pad(a[:, :n].reshape(-1), (0, 8 * (many - n))) for n in caps])

    hit = (rank[:, :, None] == jnp.arange(many)) & (key == chosen_here[:, None])[:, :, None]
    table = jnp.sum(jnp.where(hit, number[:, :, None], 0), axis=1)
    used = pick(jnp.sum(hit.astype(jnp.int32), axis=1))
    target = pick(table + jnp.where(jnp.arange(8) < 4, 0, 4 * blocks)[:, None])
    table = pick(table)
    mine = jnp.where(live > 0, key[z] * cap + rank[z], 0)
    arrived = lax.switch(
        size, [lambda n=n, i=i: spread(past, table, n, 2 * i) for i, n in enumerate(caps)]
    )
    attn, token_grad, far_grad, seen, dkv, dq, mixed = layer(
        mine, live, arrived, tokens, grads, w_query, w_pair, w_out, 8 * many
    )
    back = (far_grad, flat(tokens), flat(grads), flat(seen), flat(dkv), flat(dq), flat(mixed))
    returned, *weight_grads = lax.switch(
        size, [lambda n=n, i=i: send_back(*back, n, 2 * i + 1) for i, n in enumerate(caps)]
    )
    partial = scatter_sum(returned, target, used, 8 * blocks)
    scale = 1.0 / math.sqrt(lax.axis_size("dp") * peers * patches * block)
    past_grad, weights = collect(partial.reshape((8,) + past.shape), weight_grads, scale)
    weights = weights.astype(F32)
    return (
        attn[None],
        token_grad[None],
        past_grad[None],
        weights[0],
        weights[1],
        weights[2],
        weights[3],
    )


def solution(mesh):
    split = P("dp", "patch", None, None)
    return jax.shard_map(
        body,
        mesh=mesh,
        in_specs=(split, split, P(), P(), P(), P(), P(), P(), P(), split),
        out_specs=(split, split, split, P(), P(), P(), P()),
        check_vma=False,
    )
```
